32 devices in a mesh: lon: 8 (over y, x, core), lat: 4 (over z).
Axes of the slice: x: 2, y: 2, z: 4, core: 2. Of those that a mesh axis runs over, the one named last changes fastest.
Arguments:
- state: float32 [3, 4, 256, 1024], P(None, None, 'lat', 'lon'), may hold values from -0.010253906 to 0.010253906
- depth: float32 [256, 1024], P('lat', 'lon'), may hold values from 0.1 to 1
- source_mask: int32 [8, 32], P('lat', 'lon'), may hold values 0 or 1
- gauge_lat: int32 [4], replicated, may hold values from 0 to 255
- gauge_lon: int32 [4], replicated, may hold values from 0 to 1023
- misfit: float32 [6, 4], replicated, may hold values from -4 to 4
Outputs:
- adjoint_state: float32 [3, 4, 256, 1024], P(None, None, 'lat', 'lon')
- coefficients: float32 [4, 512, 512], P(None, 'lon', 'lat')
The draws below stay inside these ranges and needn't reach their ends.
All inputs are finite; a program needn't handle non-finite values. No bound on the sum of `source_mask` on one device may be relied on, other than what follows from the above.
Results may differ from the reference program's by a relative error of at most 0.0003.
Values sent between devices are 32-bit elements; how exact they have to be, the bound alone decides.
A program may use at most 64 MiB of HBM per device.

```python
import math
import jax
import jax.numpy as jnp
from jax import lax

ADJ = 4
STEPS = 6
BLOCK = 32
KX = 512
KY = 512
NY = 256
NX = 1024


noise_level = 3.0


noise_bound = 3.5


def draw_state(key, part):
    scale = noise_level / NX
    shape = (3, ADJ, NY, NX)
    values = jnp.clip(jax.random.normal(key, shape, jnp.float32), -noise_bound, noise_bound)
    return (values * scale).astype(jnp.float32)


def set_ends(entries, stream_key, low, largest):
    extent = entries.shape
    place = [jax.random.randint(jax.random.fold_in(stream_key, axis), (), 0, extent[axis]) for axis in range(len(extent))]
    entries = entries.at[tuple(place)].set(low)
    longest = extent.index(max(extent))
    place[longest] = (place[longest] + 1) % extent[longest]
    return entries.at[tuple(place)].set(largest)


def level_of(key, dims, shards, least, high):
    def one(position, blocks):
        steps = jax.random.uniform(jax.random.fold_in(jax.random.fold_in(key, 6), position), (blocks,), jnp.float32, least / len(shards), high / len(shards))
        return jnp.repeat(jnp.exp(steps), dims[position] // blocks).reshape((-1,) + (1,) * (len(dims) - position - 1))

    level = one(*shards[0])
    for cut in shards[1:]:
        level = level * one(*cut)
    return level


def centred(rng, extent, deviation, most, held_as=jnp.bfloat16):
    result = jax.random.normal(rng, extent, jnp.float32) * deviation
    return jnp.minimum(jnp.maximum(result, -most), most).astype(held_as)


def setup_inputs(seed: int = 0) -> dict:
    seeds = jax.random.split(jax.random.key(seed), 7)
    return {
        "state": draw_state(jax.random.fold_in(seeds[6], 71), 0),
        "depth": jnp.clip(jnp.exp(math.log(1.0) - 2.3025851 * jax.random.uniform(seeds[1], (NY, NX), jnp.float32) ** level_of(seeds[1], (NY, NX), ((0, 4), (1, 8)), -0.2, 0.2)), 0.1, 1.0),
        "source_mask": set_ends((jax.random.randint(seeds[2], (NY // BLOCK, NX // BLOCK), 0, 2) < 1).astype(jnp.int32), jax.random.fold_in(seeds[2], 1), 0, 1),
        "gauge_lat": set_ends(jax.random.randint(seeds[3], (ADJ,), 0, NY), jax.random.fold_in(seeds[3], 1), 0, NY - 1).astype(jnp.int32),
        "gauge_lon": set_ends(jax.random.randint(seeds[4], (ADJ,), 0, NX), jax.random.fold_in(seeds[4], 1), 0, NX - 1).astype(jnp.int32),
        "misfit": centred(seeds[5], (STEPS, ADJ), 1.0, 4.0, jnp.float32),
    }


time_step = 0.5

def centred_x(f):
    return 0.5 * (f[..., 1:-1, 2:] - f[..., 1:-1, :-2])

def centred_y(f):
    return 0.5 * (f[..., 2:, 1:-1] - f[..., :-2, 1:-1])

def basis(total, modes, start, count):
    cells = start + jnp.arange(count, dtype=jnp.int32)
    order = jnp.arange(modes, dtype=jnp.int32)
    half = modes // 2
    wave = jnp.where(order < half, order, order - half + 1)
    phase = (cells[:, None] * wave[None, :] % total).astype(jnp.float32) * (2.0 * math.pi / total)
    return jnp.where(order[None, :] < half, jnp.cos(phase), jnp.sin(phase))

def reference(state, depth, source_mask, gauge_lat, gauge_lon, misfit):
    full_mask = jnp.repeat(jnp.repeat(source_mask, BLOCK, 0), BLOCK, 1).astype(jnp.float32)
    lat_basis = basis(NY, KY, 0, NY)
    lon_basis = basis(NX, KX, 0, NX)
    scale = 2.0 / math.sqrt(NX * NY)

    def one_adjoint(items):
        heights, east, north, row, col, pushes = items
        for step in range(STEPS):
            padded_east = jnp.pad(east, 1)
            padded_north = jnp.pad(north, 1)
            heights = heights + time_step * (centred_x(padded_east) + centred_y(padded_north))
            heights = heights.at[row, col].add(pushes[step])
            padded = jnp.pad(heights, 1)
            east = east + time_step * depth * centred_x(padded)
            north = north + time_step * depth * centred_y(padded)
        masked = heights * full_mask
        partial_sums = jnp.dot(lat_basis.T, masked, precision=lax.Precision.HIGHEST)
        modes = jnp.dot(partial_sums, lon_basis, precision=lax.Precision.HIGHEST).T * scale
        return (jnp.stack([heights, east, north]), modes)
    fields, modes = lax.map(one_adjoint, (state[0], state[1], state[2], gauge_lat, gauge_lon, misfit.T))
    return (jnp.transpose(fields, (1, 0, 2, 3)), modes)
```

```python
import functools
import math

import jax
import jax.numpy as jnp
import ml_dtypes
import numpy as np
from jax import lax
from jax.experimental import pallas as pl
from jax.experimental.pallas import tpu as pltpu
from jax.sharding import PartitionSpec as P

STEPS = 6
KX = 512
KY = 512
ADJ = 4
ROUNDS = ADJ // 2
HALO = 16
SLOTS = 128 // HALO

MESH = pl.DeviceIdType.MESH
FLOAT = jnp.float32
HALF = jnp.bfloat16


def basis(total, modes):
    cells = np.arange(total, dtype=np.int64)
    order = np.arange(modes, dtype=np.int64)
    half = modes // 2
    wave = np.where(order < half, order, order - half + 1)
    phase = (cells[:, None] * wave[None, :] % total).astype(np.float64) * (2.0 * math.pi / total)
    return np.where(order[None, :] < half, np.cos(phase), np.sin(phase))


def halves(table):
    high = table.astype(ml_dtypes.bfloat16)
    low = (table - high.astype(np.float64)).astype(ml_dtypes.bfloat16)
    return high, low


def lon_table(total, count):
    chips, part = count // 2, KX // count // 2
    table = basis(total, KX).T.reshape(count, 2, part, chips, total // chips).transpose(3, 0, 2, 1, 4)
    return np.stack(halves(table.reshape(chips, KX // 2, 2 * total // chips)), axis=1)


def lat_table(total, count, scale):
    own, rows = KY // count, total // count
    table = (scale * basis(total, KY)).reshape(count, rows, count, own).transpose(2, 0, 1, 3)
    both = np.zeros((count, count, 2, rows, 2, own))
    both[:, :, 0, :, 0, :] = table
    both[:, :, 1, :, 1, :] = table
    return np.stack(halves(both.reshape(count, 2 * total, 2 * own)), axis=1)


def split(x):
    high = x.astype(HALF)
    return high, (x - high.astype(FLOAT)).astype(HALF)


def sent_lines(rows, own, lon_count, lat_count):
    return 14 * rows + ROUNDS * (own // 2 * (lon_count - 1) + own * (lat_count - 1))


def kernel(
    lon_count, lat_count,
    state_hbm, depth_hbm, source_hbm, gauge_lat_hbm, gauge_lon_hbm, misfit_hbm, lon_hbm, lat_hbm,
    fields, modes,
    source, gauge_lat, gauge_lon, misfit,
    ext, dep, stage, masks, pack, corner, got, met,
    height, flow, total, coef_e, coef_w, coef_n, inside, gauges,
    lon_tab, lat_tab, part, pieces, gathered,
    zero, zero_strip, blank, sems,
):
    rows, cols = depth_hbm.shape
    high = rows + 2 * HALO
    depth_of = high // 8
    own = modes.shape[1]
    part_own = own // 2
    bits = pieces.shape[1]
    bit = part_own // bits
    fold = rows // 2
    own_y = modes.shape[2]
    lon = lax.axis_index("lon")
    lat = lax.axis_index("lat")
    chips = lon_count // 2
    chip, core = lon // 2, lax.rem(lon, 2)
    mate = lon + 1 - 2 * core
    has_e, has_w = chip < chips - 1, chip > 0
    has_n, has_s = lat < lat_count - 1, lat > 0
    side = 2 * core - 1
    has_side = jnp.logical_or(jnp.logical_and(core == 0, has_w), jnp.logical_and(core == 1, has_e))
    lower, upper = slice(0, HALO), slice(rows - HALO, rows)
    north, south = slice(rows, rows + HALO), slice(rows + HALO, high)

    arrived_a, arrived_b, returned, sent, sent_n, sent_s, sent_side, sent_side_n, sent_side_s, staged_a, staged_b, waves = range(12)
    reduced = waves + 6
    spread = reduced + ROUNDS * bits

    def settle(index, lines):
        pltpu.make_async_copy(blank.at[0:lines], blank.at[0:lines], sems.at[index]).wait()

    barrier = pltpu.get_barrier_semaphore()

    def greet(there, device):
        if there is True:
            pl.semaphore_signal(barrier, 1, device_id=device, device_id_type=MESH)
        else:
            @pl.when(there)
            def _():
                pl.semaphore_signal(barrier, 1, device_id=device, device_id_type=MESH)

    both = jnp.logical_and
    greet(has_n, (lon, lat + 1))
    greet(has_s, (lon, lat - 1))
    greet(has_n, (mate, lat + 1))
    greet(has_s, (mate, lat - 1))
    for d in range(1, lon_count):
        greet(True, (lax.rem(lon + d, lon_count), lat))
    greet(both(has_e, has_n), (2 * chip + 2, lat + 1))
    greet(both(has_e, has_s), (2 * chip + 2, lat - 1))
    greet(both(has_w, has_n), (2 * chip - 1, lat + 1))
    greet(both(has_w, has_s), (2 * chip - 1, lat - 1))
    for d in range(1, lat_count):
        target = lax.rem(lat + d, lat_count)
        near = jnp.logical_or(target == lat + 1, target == lat - 1)
        greet(jnp.logical_not(near), (lon, target))

    pairs = [
        (source_hbm, source), (gauge_lat_hbm, gauge_lat), (gauge_lon_hbm, gauge_lon), (misfit_hbm, misfit),
        (depth_hbm, dep.at[core, 0:rows]),
        (state_hbm.at[:, 2 * core], ext.at[0, :, core, 0:rows]), (state_hbm.at[:, 2 * core + 1], ext.at[1, :, core, 0:rows]),
        (lon_hbm.at[chip], lon_tab), (lat_hbm.at[lat], lat_tab),
        *[(state_hbm.at[:, i], stage.at[i]) for i in range(ADJ)],
    ]
    places = [waves + 2, waves + 3, waves + 4, waves + 5, staged_a, arrived_a, arrived_b, waves, waves + 1]
    places += [staged_a, staged_b] * (ADJ // 2)
    loads = [pltpu.make_async_copy(a, b, sems.at[i]) for i, (a, b) in zip(places, pairs)]
    for i in (4, 9, 11, 10, 12, 0, 1, 2, 3, 5, 6):
        loads[i].start()

    def remote(source_ref, target, send, recv, device):
        return pltpu.make_async_remote_copy(
            src_ref=source_ref, dst_ref=target, send_sem=sems.at[send], recv_sem=sems.at[recv],
            device_id=device, device_id_type=MESH,
        )

    def ns_copy(way, k, item):
        taken, put, step = ((upper, south, 1), (lower, north, -1))[way]
        if item == 0:
            source_ref, target = depth_hbm.at[taken], dep.at[core, put]
        else:
            source_ref, target = state_hbm.at[:, 2 * k + item - 1, taken], ext.at[item - 1, :, core, put]
        return remote(source_ref, target, (sent_n, sent_s)[way], arrived_b if item == 2 else arrived_a, (2 * chip + k, lat + step))

    def ns_blank(way, k, item):
        put = (south, north)[way]
        if item == 0:
            return pltpu.make_async_copy(zero.at[0], dep.at[k, put], sems.at[arrived_a])
        return pltpu.make_async_copy(zero, ext.at[item - 1, :, k, put], sems.at[(arrived_a, arrived_b)[item - 1]])

    ns_goes, ns_comes = (has_n, has_s), (has_s, has_n)

    def side_copy(k, piece):
        step = (0, 0, 1, -1)[piece]
        source_ref = pack.at[piece, k] if piece < 2 else corner.at[piece - 2, k]
        target = got.at[piece, core] if piece < 2 else met.at[piece - 2, core]
        return remote(
            source_ref, target, (sent_side, sent_side, sent_side_n, sent_side_s)[piece],
            arrived_b if piece == 1 else arrived_a, (2 * (chip + side) + k, lat + step),
        )

    def side_blank(way, piece):
        source_ref = zero_strip if piece < 2 else zero.at[0]
        target = got.at[piece, way] if piece < 2 else met.at[piece - 2, way]
        return pltpu.make_async_copy(source_ref, target, sems.at[arrived_b if piece == 1 else arrived_a])

    side_goes = (has_side, has_side, both(has_side, has_n), both(has_side, has_s))
    side_comes = [(x, x, both(x, has_s), both(x, has_n)) for x in (has_e, has_w)]

    def mate_copy(item):
        if item == 0:
            source_ref, target = depth_hbm, dep.at[core, 0:rows]
        elif item == 3:
            source_ref, target = masks.at[core], masks.at[core]
        elif item < 3:
            source_ref, target = state_hbm.at[:, 2 * (1 - core) + item - 1], ext.at[item - 1, :, core, 0:rows]
        else:
            source_ref, target = ext.at[item - 4, :, 1 - core, 0:rows], fields.at[:, 2 * core + item - 4]
        arrived = (arrived_a, arrived_a, arrived_b, arrived_a, returned, returned)[item]
        return remote(source_ref, target, sent, arrived, (mate, lat))

    def when(there, action):
        @pl.when(there)
        def _():
            action()

    zero[...] = jnp.zeros(zero.shape, FLOAT)
    zero_strip[...] = jnp.zeros(zero_strip.shape, FLOAT)
    for way in range(2):
        for k in range(2):
            for item in range(3):
                when(jnp.logical_not(ns_comes[way]), lambda: ns_blank(way, k, item).start())
        for piece in range(4):
            when(jnp.logical_not(side_comes[way][piece]), lambda: side_blank(way, piece).start())

    count = lon_count - 1 + lat_count - 1 + has_n.astype(jnp.int32) + has_s.astype(jnp.int32)
    count = count + 2 * side_goes[2].astype(jnp.int32) + 2 * side_goes[3].astype(jnp.int32)
    pl.semaphore_wait(barrier, count)

    for item in (0, 1):
        for k in range(2):
            for way in range(2):
                when(ns_goes[way], lambda: ns_copy(way, k, item).start())
    mate_copy(0).start()
    mate_copy(1).start()

    lane = lax.broadcasted_iota(jnp.int32, (fold, 128), 1)

    def slot_of(item, i, upper_half):
        return (i + SLOTS // 2 * (item + upper_half)) % SLOTS

    strips = {}
    for item in range(2):
        settle((staged_a, staged_b)[item], (7 - item) * rows)
        for k in range(2):
            arrays = [stage[2 * k + item, f] for f in range(3)]
            if item == 0:
                arrays.append(dep[core, 0:rows])
            strip = jnp.zeros((fold, 128), FLOAT)
            for i, array in enumerate(arrays):
                for upper_half in range(2):
                    at = slot_of(item, i, upper_half) * HALO
                    moved = pltpu.roll(array[upper_half * fold:(upper_half + 1) * fold], at + HALO * core, 1)
                    strip = jnp.where(jnp.logical_and(lane >= at, lane < at + HALO), moved, strip)
            pack[item, k] = strip
            strips[item, k] = strip
            when(has_side, lambda: side_copy(k, item).start())
            if item == 1:
                begin = lane[:HALO] < 64
                first, second = strips[0, k], strips[1, k]
                corner[0, k] = jnp.where(begin, second[fold - HALO:], first[fold - HALO:])
                corner[1, k] = jnp.where(begin, first[:HALO], second[:HALO])
                for piece in (2, 3):
                    when(side_goes[piece], lambda: side_copy(k, piece).start())
    for k in range(2):
        for way in range(2):
            when(ns_goes[way], lambda: ns_copy(way, k, 2).start())
    mate_copy(2).start()

    loads[7].start()
    loads[8].start()

    for copy in loads[:4]:
        copy.wait()
    line = lax.broadcasted_iota(jnp.int32, (rows, cols), 0)
    place = lax.broadcasted_iota(jnp.int32, (rows, cols), 1)
    mask = jnp.zeros((rows, cols), FLOAT)
    width = rows // source.shape[0]
    for i in range(source.shape[0]):
        for j in range(source.shape[1]):
            tile = (line >= i * width) & (line < (i + 1) * width) & (place >= j * width) & (place < (j + 1) * width)
            mask = jnp.where(tile, source[i, j].astype(FLOAT), mask)
    masks[core] = mask
    mate_copy(3).start()

    shape = (depth_of, 8, 128)
    near = lax.broadcasted_iota(jnp.int32, shape, 1) * depth_of + lax.broadcasted_iota(jnp.int32, shape, 0)
    row = lat * rows + jnp.where(near < rows + HALO, near, near - high)
    across = lax.broadcasted_iota(jnp.int32, shape, 2)
    for j in range(3):
        if j < 2:
            col, real = across + j * 128, row == row
        else:
            col = jnp.where(across < HALO, across + 256, across - 128)
            real = jnp.logical_or(across < HALO, across >= 128 - HALO)
        col = chip * 256 + col
        valid = (row >= 0) & (row < lat_count * rows) & (col >= 0) & (col < chips * 256) & real
        inside[j] = jnp.where(valid, 1.0, 0.0).astype(FLOAT)
        for a in range(2):
            hit = (row == gauge_lat[2 * core + a]) & (col == gauge_lon[2 * core + a]) & real
            gauges[a, j] = jnp.where(hit, 1.0, 0.0).astype(FLOAT)

    half_wide = lax.broadcasted_iota(jnp.int32, (fold + HALO, 128), 1)

    def unpacked(item, i):
        parts = []
        for upper_half in range(2):
            at = slot_of(item, i, upper_half) * HALO
            sides = [jnp.concatenate([got[item, way], met[1 - upper_half, way]], axis=0) for way in range(2)]
            right = pltpu.roll(sides[0], (128 - at) % 128, 1)
            left = pltpu.roll(sides[1], (128 - at - HALO) % 128, 1)
            parts.append(jnp.where(half_wide < HALO, right, jnp.where(half_wide >= 128 - HALO, left, 0.0)))
        lower_half, upper_half = parts
        return jnp.concatenate([lower_half[:fold], upper_half[:fold], lower_half[fold:], upper_half[fold:]], axis=0)

    def dealt(ref):
        return jnp.stack([ref[pl.ds(v, 8, stride=depth_of), :] for v in range(depth_of)])

    def north_of(x, n):
        return jnp.concatenate([x[n:], pltpu.roll(x[:n], 7, 1)], axis=0)

    def south_of(x, n):
        return jnp.concatenate([pltpu.roll(x[-n:], 1, 1), x[:-n]], axis=0)

    def east_of(xs, n):
        turned = [pltpu.roll(x, 128 - n, 2) for x in xs]
        return [jnp.where(across < 128 - n, turned[j], turned[(j + 1) % 3]) for j in range(3)]

    def west_of(xs, n):
        turned = [pltpu.roll(x, n, 2) for x in xs]
        return [jnp.where(across >= n, turned[j], turned[j - 1]) for j in range(3)]

    tiles = range(3)

    edges = 2 * 2 * 3 * HALO + 2 * fold

    def prepare(a):
        settle((arrived_a, arrived_b)[a], edges + 6 * rows + (0 if a else 2 * 2 * HALO + 2 * 2 * HALO + 2 * rows))
        if a == 0:
            dep[2] = unpacked(0, 3)
            deep = [dealt(dep.at[j]) * 0.0625 for j in tiles]
            ahead, behind = east_of(deep, 1), west_of(deep, 1)
            for j in tiles:
                coef_e[j] = ahead[j]
                coef_w[j] = behind[j]
                coef_n[j] = north_of(deep[j], 1)
        for f in range(3):
            ext[a, f, 2] = unpacked(a, f)
        east = [dealt(ext.at[a, 1, j]) for j in tiles]
        ahead, behind = east_of(east, 1), west_of(east, 1)
        for j in tiles:
            up = dealt(ext.at[a, 2, j])
            height[j] = dealt(ext.at[a, 0, j])
            change = (ahead[j] - behind[j]) + (north_of(up, 1) - south_of(up, 1))
            flow[j] = inside[j] * (0.25 * change)

    def rise(a, t, first):
        push = misfit[2 * core + a, t]
        now = []
        for j in tiles:
            h = height[j] + flow[j] + gauges[a, j] * push
            height[j] = h
            total[a, j] = h if first else total[a, j] + h
            now.append(h)
        return now

    def drive(now):
        ahead, behind = east_of(now, 2), west_of(now, 2)
        for j in tiles:
            lift = coef_n[j] * (north_of(now[j], 2) - now[j])
            along = coef_e[j] * (ahead[j] - now[j]) - coef_w[j] * (now[j] - behind[j])
            flow[j] = flow[j] + inside[j] * (along + (lift - south_of(lift, 2)))

    def advance(a):
        drive(rise(a, 0, True))

        def step(t, carry):
            drive(rise(a, t, False))
            return carry

        lax.fori_loop(1, STEPS - 1, step, 0)
        rise(a, STEPS - 1, False)

    def rs_copy(a, n, target):
        start = pl.multiple_of(target * part_own + n * bit, bit)
        return remote(
            part.at[a, pl.ds(start, bit)], pieces.at[a, n, lon],
            sent, reduced + a * bits + n, (target, lat),
        )

    dims = (((1,), (1,)), ((), ()))

    def project(a):
        for j in range(2):
            for v in range(depth_of):
                ext[a, 0, j, pl.ds(v, 8, stride=depth_of), :] = height[j, v]
        masked = jnp.concatenate([ext[a, 0, j, 0:rows] * masks[j] for j in range(2)], axis=1)
        high_m, low_m = split(masked)
        blank = jnp.zeros_like(high_m)

        def doubled(x):
            return jnp.concatenate(
                [jnp.concatenate([x, blank], axis=1), jnp.concatenate([blank, x], axis=1)], axis=0
            )

        high_m, low_m = doubled(high_m), doubled(low_m)
        part[a] = (
            lax.dot_general(lon_tab[0], high_m, dims, preferred_element_type=FLOAT)
            + lax.dot_general(lon_tab[0], low_m, dims, preferred_element_type=FLOAT)
            + lax.dot_general(lon_tab[1], high_m, dims, preferred_element_type=FLOAT)
        )
        for n in range(bits):
            for d in range(1, lon_count):
                rs_copy(a, n, lax.rem(lon + d, lon_count)).start()
        for n in range(bits):
            pieces[a, n, lon] = part[a, pl.ds(pl.multiple_of(lon * part_own + n * bit, bit), bit)]

    def finish(a):
        sums = [total[a, j] for j in tiles]
        ahead, behind = east_of(sums, 1), west_of(sums, 1)
        for j in range(2):
            deep = 0.25 * dealt(dep.at[j])
            east = dealt(ext.at[a, 1, j]) + deep * (ahead[j] - behind[j])
            up = dealt(ext.at[a, 2, j]) + deep * (north_of(sums[j], 1) - south_of(sums[j], 1))
            for v in range(depth_of):
                ext[a, 1, j, pl.ds(v, 8, stride=depth_of), :] = east[v]
                ext[a, 2, j, pl.ds(v, 8, stride=depth_of), :] = up[v]
        mate_copy(4 + a).start()
        for f in range(3):
            fields[f, 2 * core + a] = ext[a, f, core, 0:rows]

    def ga_copy(a, n, z):
        return remote(gathered.at[a, n, lat], gathered.at[a, n, lat], sent, spread + a * bits + n, (lon, z))

    def collect(a, n):
        settle(reduced + a * bits + n, (lon_count - 1) * bit)
        sums = []
        for k in range(2):
            value = pieces[a, n, k]
            for c in range(1, chips):
                value = value + pieces[a, n, 2 * c + k]
            sums.append(value)
        gathered[a, n, lat] = jnp.concatenate(sums, axis=0)
        for z in range(lat_count):
            when(z != lat, lambda: ga_copy(a, n, z).start())

    def conclude(a, n):
        settle(spread + a * bits + n, (lat_count - 1) * 2 * bit)
        high_g, low_g = split(jnp.concatenate([gathered[a, n, z] for z in range(lat_count)], axis=1))
        result = (
            jnp.dot(high_g, lat_tab[0], preferred_element_type=FLOAT)
            + jnp.dot(low_g, lat_tab[0], preferred_element_type=FLOAT)
            + jnp.dot(high_g, lat_tab[1], preferred_element_type=FLOAT)
        )
        for k in range(2):
            for h in range(2):
                modes[2 * k + a, h * part_own + n * bit:h * part_own + (n + 1) * bit] = result[
                    k * bit:(k + 1) * bit, h * own_y:(h + 1) * own_y
                ]

    prepare(0)
    advance(0)
    loads[7].wait()
    project(0)
    prepare(1)
    advance(1)
    project(1)
    finish(0)
    finish(1)
    loads[8].wait()
    for a in range(ROUNDS):
        for n in range(bits):
            collect(a, n)
    settle(returned, 2 * 3 * rows)
    for a in range(ROUNDS):
        for n in range(bits):
            conclude(a, n)

    for way in range(2):
        when(ns_goes[way], lambda: settle((sent_n, sent_s)[way], 2 * 7 * HALO))
        when(side_goes[2 + way], lambda: settle((sent_side_n, sent_side_s)[way], 2 * HALO))
    when(has_side, lambda: settle(sent_side, 4 * fold))
    settle(sent, sent_lines(rows, own, lon_count, lat_count))


def place(fields, modes, fields_out, modes_out, sem):
    copies = [
        pltpu.make_async_copy(fields, fields_out, sem.at[0]),
        pltpu.make_async_copy(modes, modes_out, sem.at[1]),
    ]
    for copy in copies:
        copy.start()
    for copy in copies:
        copy.wait()


def on_device(lon_count, lat_count, tables, state, depth, source_mask, gauge_lat, gauge_lon, misfit):
    rows, cols = depth.shape
    own_x, own_y = KX // lon_count, KY // lat_count
    high = rows + 2 * HALO
    bits = 2 if own_x % 32 == 0 else 1
    vmem = pl.BlockSpec(memory_space=pltpu.VMEM)
    hbm = pl.BlockSpec(memory_space=pltpu.HBM)
    dma = pltpu.SemaphoreType.DMA
    dealt = (3, high // 8, 8, 128)
    shapes = (
        jax.ShapeDtypeStruct((3, ADJ, rows, cols), FLOAT),
        jax.ShapeDtypeStruct((ADJ, own_x, own_y), FLOAT),
    )
    results = pl.pallas_call(
        functools.partial(kernel, lon_count, lat_count),
        out_shape=shapes,
        in_specs=[hbm] * 8,
        out_specs=(vmem, vmem),
        scratch_shapes=[
            pltpu.SMEM(source_mask.shape, jnp.int32),
            pltpu.SMEM((ADJ,), jnp.int32),
            pltpu.SMEM((ADJ,), jnp.int32),
            pltpu.SMEM((ADJ, STEPS), FLOAT),
            pltpu.VMEM((2, 3, 3, high, 128), FLOAT),
            pltpu.VMEM((3, high, 128), FLOAT),
            pltpu.VMEM((ADJ, 3, rows, cols), FLOAT),
            pltpu.VMEM((2, rows, cols), FLOAT),
            pltpu.VMEM((2, 2, rows // 2, 128), FLOAT),
            pltpu.VMEM((2, 2, HALO, 128), FLOAT),
            pltpu.VMEM((2, 2, rows // 2, 128), FLOAT),
            pltpu.VMEM((2, 2, HALO, 128), FLOAT),
            pltpu.VMEM(dealt, FLOAT),
            pltpu.VMEM(dealt, FLOAT),
            pltpu.VMEM((2, *dealt), FLOAT),
            pltpu.VMEM(dealt, FLOAT),
            pltpu.VMEM(dealt, FLOAT),
            pltpu.VMEM(dealt, FLOAT),
            pltpu.VMEM(dealt, FLOAT),
            pltpu.VMEM((2, *dealt), FLOAT),
            pltpu.VMEM((2, KX // 2, 4 * cols), HALF),
            pltpu.VMEM((2, 2 * lat_count * rows, 2 * own_y), HALF),
            pltpu.VMEM((ROUNDS, KX // 2, 2 * rows), FLOAT),
            pltpu.VMEM((ROUNDS, bits, lon_count, own_x // 2 // bits, 2 * rows), FLOAT),
            pltpu.VMEM((ROUNDS, bits, lat_count, own_x // bits, 2 * rows), FLOAT),
            pltpu.VMEM((3, HALO, 128), FLOAT),
            pltpu.VMEM((rows // 2, 128), FLOAT),
            pltpu.VMEM((sent_lines(rows, own_x, lon_count, lat_count), 128), FLOAT),
            dma((17 + 2 * ROUNDS * bits,)),
        ],
        compiler_params=pltpu.CompilerParams(
            collective_id=0, has_side_effects=True, vmem_limit_bytes=32 * 1024 * 1024
        ),
    )(*[pltpu.with_memory_space_constraint(x, pltpu.HBM) for x in (state, depth, source_mask, gauge_lat, gauge_lon, misfit.T, *tables)])
    return pl.pallas_call(
        place,
        out_shape=shapes,
        in_specs=[vmem] * 2,
        out_specs=(hbm, hbm),
        scratch_shapes=[dma((2,))],
    )(*[pltpu.with_memory_space_constraint(x, pltpu.VMEM) for x in results])


def solution(mesh):
    lon_count, lat_count = mesh.shape["lon"], mesh.shape["lat"]
    placed = (P(None, None, "lat", "lon"), P("lat", "lon"), P("lat", "lon"), P(), P(), P())

    def whole(state, depth, source_mask, gauge_lat, gauge_lon, misfit):
        total_rows, total_cols = depth.shape
        scale = 2.0 / math.sqrt(total_rows * total_cols)
        tables = (lon_table(total_cols, lon_count), lat_table(total_rows, lat_count, scale))

        def local(*args):
            constants = tuple(jnp.asarray(table) for table in tables)
            return on_device(lon_count, lat_count, constants, *args)

        return jax.shard_map(
            local,
            mesh=mesh,
            in_specs=placed,
            out_specs=(P(None, None, "lat", "lon"), P(None, "lon", "lat")),
            check_vma=False,
        )(state, depth, source_mask, gauge_lat, gauge_lon, misfit)

    return whole
```

```python
import functools
import math

import jax
import jax.numpy as jnp
import ml_dtypes
import numpy as np
from jax import lax
from jax.experimental import pallas as pl
from jax.experimental.pallas import tpu as pltpu
from jax.sharding import PartitionSpec as P

STEPS = 6
KX = 512
KY = 512
ADJ = 4
ROUNDS = ADJ // 2
HALO = 16
REACH = 2 * STEPS
SLOTS = 128 // HALO

MESH = pl.DeviceIdType.MESH
FLOAT = jnp.float32
HALF = jnp.bfloat16


def basis(total, modes):
    cells = np.arange(total, dtype=np.int64)
    order = np.arange(modes, dtype=np.int64)
    half = modes // 2
    wave = np.where(order < half, order, order - half + 1)
    phase = (cells[:, None] * wave[None, :] % total).astype(np.float64) * (2.0 * math.pi / total)
    return np.where(order[None, :] < half, np.cos(phase), np.sin(phase))


def halves(table):
    high = table.astype(ml_dtypes.bfloat16)
    low = (table - high.astype(np.float64)).astype(ml_dtypes.bfloat16)
    return high, low


def lon_table(total, count):
    chips, part = count // 2, KX // count // 2
    table = basis(total, KX).T.reshape(count, 2, part, chips, total // chips).transpose(3, 0, 2, 1, 4)
    return np.stack(halves(table.reshape(chips, KX // 2, 2 * total // chips)), axis=1)


def lat_table(total, count, scale):
    own, rows = KY // count, total // count
    table = (scale * basis(total, KY)).reshape(count, rows, count, own).transpose(2, 0, 1, 3)
    both = np.zeros((count, count, 2, rows, 2, own))
    both[:, :, 0, :, 0, :] = table
    both[:, :, 1, :, 1, :] = table
    return np.stack(halves(both.reshape(count, 2 * total, 2 * own)), axis=1)


def split(x):
    high = x.astype(HALF)
    return high, (x - high.astype(FLOAT)).astype(HALF)


def sent_lines(rows, own, lon_count, lat_count):
    return 14 * rows + ROUNDS * (own // 2 * (lon_count - 1) + own * (lat_count - 1))


def kernel(
    lon_count, lat_count,
    state_hbm, depth_hbm, source_hbm, gauge_lat_hbm, gauge_lon_hbm, misfit_hbm, lon_hbm, lat_hbm,
    fields, modes,
    source, gauge_lat, gauge_lon, misfit,
    ext, dep, stage, masks, pack, corner, got, met,
    height, flow, total, coef_e, coef_w, coef_n, inside, gauges,
    lon_tab, lat_tab, part, pieces, gathered,
    zero, zero_strip, blank, sems,
):
    rows, cols = depth_hbm.shape
    high = rows + 2 * HALO
    depth_of = high // 8
    own = modes.shape[1]
    part_own = own // 2
    bits = pieces.shape[1]
    bit = part_own // bits
    fold = rows // 2
    own_y = modes.shape[2]
    lon = lax.axis_index("lon")
    lat = lax.axis_index("lat")
    chips = lon_count // 2
    chip, core = lon // 2, lax.rem(lon, 2)
    mate = lon + 1 - 2 * core
    has_e, has_w = chip < chips - 1, chip > 0
    has_n, has_s = lat < lat_count - 1, lat > 0
    side = 2 * core - 1
    has_side = jnp.logical_or(jnp.logical_and(core == 0, has_w), jnp.logical_and(core == 1, has_e))
    lower, upper = slice(0, REACH), slice(rows - REACH, rows)
    north, south = slice(rows, rows + REACH), slice(high - REACH, high)

    arrived_a, arrived_b, returned, sent, sent_n, sent_s, sent_side, sent_side_n, sent_side_s, staged_a, staged_b, waves = range(12)
    reduced = waves + 6
    spread = reduced + ROUNDS * bits

    def settle(index, lines):
        pltpu.make_async_copy(blank.at[0:lines], blank.at[0:lines], sems.at[index]).wait()

    barrier = pltpu.get_barrier_semaphore()

    def greet(there, device):
        if there is True:
            pl.semaphore_signal(barrier, 1, device_id=device, device_id_type=MESH)
        else:
            @pl.when(there)
            def _():
                pl.semaphore_signal(barrier, 1, device_id=device, device_id_type=MESH)

    both = jnp.logical_and
    greet(has_n, (lon, lat + 1))
    greet(has_s, (lon, lat - 1))
    greet(has_n, (mate, lat + 1))
    greet(has_s, (mate, lat - 1))
    for d in range(1, lon_count):
        greet(True, (lax.rem(lon + d, lon_count), lat))
    greet(both(has_e, has_n), (2 * chip + 2, lat + 1))
    greet(both(has_e, has_s), (2 * chip + 2, lat - 1))
    greet(both(has_w, has_n), (2 * chip - 1, lat + 1))
    greet(both(has_w, has_s), (2 * chip - 1, lat - 1))
    for d in range(1, lat_count):
        target = lax.rem(lat + d, lat_count)
        near = jnp.logical_or(target == lat + 1, target == lat - 1)
        greet(jnp.logical_not(near), (lon, target))

    pairs = [
        (source_hbm, source), (gauge_lat_hbm, gauge_lat), (gauge_lon_hbm, gauge_lon), (misfit_hbm, misfit),
        (depth_hbm, dep.at[core, 0:rows]),
        (state_hbm.at[:, 2 * core], ext.at[0, :, core, 0:rows]), (state_hbm.at[:, 2 * core + 1], ext.at[1, :, core, 0:rows]),
        (lon_hbm.at[chip], lon_tab), (lat_hbm.at[lat], lat_tab),
        *[(state_hbm.at[:, i], stage.at[i]) for i in range(ADJ)],
    ]
    places = [waves + 2, waves + 3, waves + 4, waves + 5, staged_a, arrived_a, arrived_b, waves, waves + 1]
    places += [staged_a, staged_b] * (ADJ // 2)
    loads = [pltpu.make_async_copy(a, b, sems.at[i]) for i, (a, b) in zip(places, pairs)]
    for i in (4, 9, 11, 10, 12, 0, 1, 2, 3, 5, 6):
        loads[i].start()

    def remote(source_ref, target, send, recv, device):
        return pltpu.make_async_remote_copy(
            src_ref=source_ref, dst_ref=target, send_sem=sems.at[send], recv_sem=sems.at[recv],
            device_id=device, device_id_type=MESH,
        )

    def ns_copy(way, k, item):
        taken, put, step = ((upper, south, 1), (lower, north, -1))[way]
        if item == 0:
            source_ref, target = depth_hbm.at[taken], dep.at[core, put]
        else:
            source_ref, target = state_hbm.at[:, 2 * k + item - 1, taken], ext.at[item - 1, :, core, put]
        return remote(source_ref, target, (sent_n, sent_s)[way], arrived_b if item == 2 else arrived_a, (2 * chip + k, lat + step))

    def ns_blank(way, k, item):
        put = (south, north)[way]
        if item == 0:
            return pltpu.make_async_copy(zero.at[0, 0:REACH], dep.at[k, put], sems.at[arrived_a])
        return pltpu.make_async_copy(zero.at[:, 0:REACH], ext.at[item - 1, :, k, put], sems.at[(arrived_a, arrived_b)[item - 1]])

    ns_goes, ns_comes = (has_n, has_s), (has_s, has_n)

    def side_copy(k, piece):
        step = (0, 0, 1, -1)[piece]
        source_ref = pack.at[piece, k] if piece < 2 else corner.at[piece - 2, k]
        target = got.at[piece, core] if piece < 2 else met.at[piece - 2, core]
        return remote(
            source_ref, target, (sent_side, sent_side, sent_side_n, sent_side_s)[piece],
            arrived_b if piece == 1 else arrived_a, (2 * (chip + side) + k, lat + step),
        )

    def side_blank(way, piece):
        source_ref = zero_strip if piece < 2 else zero.at[0]
        target = got.at[piece, way] if piece < 2 else met.at[piece - 2, way]
        return pltpu.make_async_copy(source_ref, target, sems.at[arrived_b if piece == 1 else arrived_a])

    side_goes = (has_side, has_side, both(has_side, has_n), both(has_side, has_s))
    side_comes = [(x, x, both(x, has_s), both(x, has_n)) for x in (has_e, has_w)]

    def mate_copy(item):
        if item == 0:
            source_ref, target = depth_hbm, dep.at[core, 0:rows]
        elif item == 3:
            source_ref, target = masks.at[core], masks.at[core]
        elif item < 3:
            source_ref, target = state_hbm.at[:, 2 * (1 - core) + item - 1], ext.at[item - 1, :, core, 0:rows]
        else:
            source_ref, target = ext.at[item - 4, :, 1 - core, 0:rows], fields.at[:, 2 * core + item - 4]
        arrived = (arrived_a, arrived_a, arrived_b, arrived_a, returned, returned)[item]
        return remote(source_ref, target, sent, arrived, (mate, lat))

    def when(there, action):
        @pl.when(there)
        def _():
            action()

    zero[...] = jnp.zeros(zero.shape, FLOAT)
    zero_strip[...] = jnp.zeros(zero_strip.shape, FLOAT)
    between = slice(rows + REACH, high - REACH)
    for k in range(2):
        dep[k, between] = jnp.zeros((2 * (HALO - REACH), 128), FLOAT)
        for a in range(2):
            for f in range(3):
                ext[a, f, k, between] = jnp.zeros((2 * (HALO - REACH), 128), FLOAT)
    for way in range(2):
        for k in range(2):
            for item in range(3):
                when(jnp.logical_not(ns_comes[way]), lambda: ns_blank(way, k, item).start())
        for piece in range(4):
            when(jnp.logical_not(side_comes[way][piece]), lambda: side_blank(way, piece).start())

    count = lon_count - 1 + lat_count - 1 + has_n.astype(jnp.int32) + has_s.astype(jnp.int32)
    count = count + 2 * side_goes[2].astype(jnp.int32) + 2 * side_goes[3].astype(jnp.int32)
    pl.semaphore_wait(barrier, count)

    for item in (0, 1):
        for k in range(2):
            for way in range(2):
                when(ns_goes[way], lambda: ns_copy(way, k, item).start())
    mate_copy(0).start()
    mate_copy(1).start()

    lane = lax.broadcasted_iota(jnp.int32, (fold, 128), 1)

    def slot_of(item, i, upper_half):
        return (i + SLOTS // 2 * (item + upper_half)) % SLOTS

    strips = {}
    for item in range(2):
        settle((staged_a, staged_b)[item], (7 - item) * rows)
        for k in range(2):
            arrays = [stage[2 * k + item, f] for f in range(3)]
            if item == 0:
                arrays.append(dep[core, 0:rows])
            strip = jnp.zeros((fold, 128), FLOAT)
            for i, array in enumerate(arrays):
                for upper_half in range(2):
                    at = slot_of(item, i, upper_half) * HALO
                    moved = pltpu.roll(array[upper_half * fold:(upper_half + 1) * fold], at + HALO * core, 1)
                    strip = jnp.where(jnp.logical_and(lane >= at, lane < at + HALO), moved, strip)
            pack[item, k] = strip
            strips[item, k] = strip
            when(has_side, lambda: side_copy(k, item).start())
            if item == 1:
                begin = lane[:HALO] < 64
                first, second = strips[0, k], strips[1, k]
                corner[0, k] = jnp.where(begin, second[fold - HALO:], first[fold - HALO:])
                corner[1, k] = jnp.where(begin, first[:HALO], second[:HALO])
                for piece in (2, 3):
                    when(side_goes[piece], lambda: side_copy(k, piece).start())
    for k in range(2):
        for way in range(2):
            when(ns_goes[way], lambda: ns_copy(way, k, 2).start())
    mate_copy(2).start()

    loads[7].start()
    loads[8].start()

    for copy in loads[:4]:
        copy.wait()
    line = lax.broadcasted_iota(jnp.int32, (rows, cols), 0)
    place = lax.broadcasted_iota(jnp.int32, (rows, cols), 1)
    mask = jnp.zeros((rows, cols), FLOAT)
    width = rows // source.shape[0]
    for i in range(source.shape[0]):
        for j in range(source.shape[1]):
            tile = (line >= i * width) & (line < (i + 1) * width) & (place >= j * width) & (place < (j + 1) * width)
            mask = jnp.where(tile, source[i, j].astype(FLOAT), mask)
    masks[core] = mask
    mate_copy(3).start()

    shape = (depth_of, 8, 128)
    near = lax.broadcasted_iota(jnp.int32, shape, 1) * depth_of + lax.broadcasted_iota(jnp.int32, shape, 0)
    row = lat * rows + jnp.where(near < rows + HALO, near, near - high)
    across = lax.broadcasted_iota(jnp.int32, shape, 2)
    for j in range(3):
        if j < 2:
            col, real = across + j * 128, row == row
        else:
            col = jnp.where(across < HALO, across + 256, across - 128)
            real = jnp.logical_or(across < HALO, across >= 128 - HALO)
        col = chip * 256 + col
        valid = (row >= 0) & (row < lat_count * rows) & (col >= 0) & (col < chips * 256) & real
        inside[j] = jnp.where(valid, 1.0, 0.0).astype(FLOAT)
        for a in range(2):
            hit = (row == gauge_lat[2 * core + a]) & (col == gauge_lon[2 * core + a]) & real
            gauges[a, j] = jnp.where(hit, 1.0, 0.0).astype(FLOAT)

    half_wide = lax.broadcasted_iota(jnp.int32, (fold + HALO, 128), 1)

    def unpacked(item, i):
        parts = []
        for upper_half in range(2):
            at = slot_of(item, i, upper_half) * HALO
            sides = [jnp.concatenate([got[item, way], met[1 - upper_half, way]], axis=0) for way in range(2)]
            right = pltpu.roll(sides[0], (128 - at) % 128, 1)
            left = pltpu.roll(sides[1], (128 - at - HALO) % 128, 1)
            parts.append(jnp.where(half_wide < HALO, right, jnp.where(half_wide >= 128 - HALO, left, 0.0)))
        lower_half, upper_half = parts
        return jnp.concatenate([lower_half[:fold], upper_half[:fold], lower_half[fold:], upper_half[fold:]], axis=0)

    def dealt(ref):
        return jnp.stack([ref[pl.ds(v, 8, stride=depth_of), :] for v in range(depth_of)])

    def north_of(x, n):
        return jnp.concatenate([x[n:], pltpu.roll(x[:n], 7, 1)], axis=0)

    def south_of(x, n):
        return jnp.concatenate([pltpu.roll(x[-n:], 1, 1), x[:-n]], axis=0)

    def east_of(xs, n):
        turned = [pltpu.roll(x, 128 - n, 2) for x in xs]
        return [jnp.where(across < 128 - n, turned[j], turned[(j + 1) % 3]) for j in range(3)]

    def west_of(xs, n):
        turned = [pltpu.roll(x, n, 2) for x in xs]
        return [jnp.where(across >= n, turned[j], turned[j - 1]) for j in range(3)]

    tiles = range(3)

    edges = 2 * 2 * 3 * REACH + 2 * fold

    def prepare(a):
        settle((arrived_a, arrived_b)[a], edges + 6 * rows + (0 if a else 2 * 2 * REACH + 2 * 2 * HALO + 2 * rows))
        if a == 0:
            dep[2] = unpacked(0, 3)
            deep = [dealt(dep.at[j]) * 0.0625 for j in tiles]
            ahead, behind = east_of(deep, 1), west_of(deep, 1)
            for j in tiles:
                coef_e[j] = ahead[j]
                coef_w[j] = behind[j]
                coef_n[j] = north_of(deep[j], 1)
        for f in range(3):
            ext[a, f, 2] = unpacked(a, f)
        east = [dealt(ext.at[a, 1, j]) for j in tiles]
        ahead, behind = east_of(east, 1), west_of(east, 1)
        for j in tiles:
            up = dealt(ext.at[a, 2, j])
            height[j] = dealt(ext.at[a, 0, j])
            change = (ahead[j] - behind[j]) + (north_of(up, 1) - south_of(up, 1))
            flow[j] = inside[j] * (0.25 * change)

    def rise(a, t, first):
        push = misfit[2 * core + a, t]
        now = []
        for j in tiles:
            h = height[j] + flow[j] + gauges[a, j] * push
            height[j] = h
            total[a, j] = h if first else total[a, j] + h
            now.append(h)
        return now

    def drive(now):
        ahead, behind = east_of(now, 2), west_of(now, 2)
        for j in tiles:
            lift = coef_n[j] * (north_of(now[j], 2) - now[j])
            along = coef_e[j] * (ahead[j] - now[j]) - coef_w[j] * (now[j] - behind[j])
            flow[j] = flow[j] + inside[j] * (along + (lift - south_of(lift, 2)))

    def advance(a):
        drive(rise(a, 0, True))

        def step(t, carry):
            drive(rise(a, t, False))
            return carry

        lax.fori_loop(1, STEPS - 1, step, 0)
        rise(a, STEPS - 1, False)

    def rs_copy(a, n, target):
        start = pl.multiple_of(target * part_own + n * bit, bit)
        return remote(
            part.at[a, pl.ds(start, bit)], pieces.at[a, n, lon],
            sent, reduced + a * bits + n, (target, lat),
        )

    dims = (((1,), (1,)), ((), ()))

    def project(a):
        for j in range(2):
            for v in range(depth_of):
                ext[a, 0, j, pl.ds(v, 8, stride=depth_of), :] = height[j, v]
        masked = jnp.concatenate([ext[a, 0, j, 0:rows] * masks[j] for j in range(2)], axis=1)
        high_m, low_m = split(masked)
        blank = jnp.zeros_like(high_m)

        def doubled(x):
            return jnp.concatenate(
                [jnp.concatenate([x, blank], axis=1), jnp.concatenate([blank, x], axis=1)], axis=0
            )

        high_m, low_m = doubled(high_m), doubled(low_m)
        part[a] = (
            lax.dot_general(lon_tab[0], high_m, dims, preferred_element_type=FLOAT)
            + lax.dot_general(lon_tab[0], low_m, dims, preferred_element_type=FLOAT)
            + lax.dot_general(lon_tab[1], high_m, dims, preferred_element_type=FLOAT)
        )
        for n in range(bits):
            for d in range(1, lon_count):
                rs_copy(a, n, lax.rem(lon + d, lon_count)).start()
        for n in range(bits):
            pieces[a, n, lon] = part[a, pl.ds(pl.multiple_of(lon * part_own + n * bit, bit), bit)]

    def finish(a):
        sums = [total[a, j] for j in tiles]
        ahead, behind = east_of(sums, 1), west_of(sums, 1)
        for j in range(2):
            deep = 0.25 * dealt(dep.at[j])
            east = dealt(ext.at[a, 1, j]) + deep * (ahead[j] - behind[j])
            up = dealt(ext.at[a, 2, j]) + deep * (north_of(sums[j], 1) - south_of(sums[j], 1))
            for v in range(depth_of):
                ext[a, 1, j, pl.ds(v, 8, stride=depth_of), :] = east[v]
                ext[a, 2, j, pl.ds(v, 8, stride=depth_of), :] = up[v]
        mate_copy(4 + a).start()
        for f in range(3):
            fields[f, 2 * core + a] = ext[a, f, core, 0:rows]

    def ga_copy(a, n, z):
        return remote(gathered.at[a, n, lat], gathered.at[a, n, lat], sent, spread + a * bits + n, (lon, z))

    def collect(a, n):
        settle(reduced + a * bits + n, (lon_count - 1) * bit)
        sums = []
        for k in range(2):
            value = pieces[a, n, k]
            for c in range(1, chips):
                value = value + pieces[a, n, 2 * c + k]
            sums.append(value)
        gathered[a, n, lat] = jnp.concatenate(sums, axis=0)
        for z in range(lat_count):
            when(jnp.logical_or(z > lat, jnp.logical_and(z == 0, lat > 0)), lambda: ga_copy(a, n, z).start())

    def conclude(a, n):
        settle(spread + a * bits + n, (lat_count - 1) * 2 * bit)
        high_g, low_g = split(jnp.concatenate([gathered[a, n, z] for z in range(lat_count)], axis=1))
        result = (
            jnp.dot(high_g, lat_tab[0], preferred_element_type=FLOAT)
            + jnp.dot(low_g, lat_tab[0], preferred_element_type=FLOAT)
            + jnp.dot(high_g, lat_tab[1], preferred_element_type=FLOAT)
        )
        for k in range(2):
            for h in range(2):
                modes[2 * k + a, h * part_own + n * bit:h * part_own + (n + 1) * bit] = result[
                    k * bit:(k + 1) * bit, h * own_y:(h + 1) * own_y
                ]

    prepare(0)
    advance(0)
    loads[7].wait()
    project(0)
    prepare(1)
    advance(1)
    project(1)
    finish(0)
    finish(1)
    loads[8].wait()
    for a in range(ROUNDS):
        for n in range(bits):
            collect(a, n)
    for a in range(ROUNDS):
        for n in range(bits):
            for z in range(1, lat_count - 1):
                when(z < lat, lambda: ga_copy(a, n, z).start())
    settle(returned, 2 * 3 * rows)
    for a in range(ROUNDS):
        for n in range(bits):
            conclude(a, n)

    for way in range(2):
        when(ns_goes[way], lambda: settle((sent_n, sent_s)[way], 2 * 7 * REACH))
        when(side_goes[2 + way], lambda: settle((sent_side_n, sent_side_s)[way], 2 * HALO))
    when(has_side, lambda: settle(sent_side, 4 * fold))
    settle(sent, sent_lines(rows, own, lon_count, lat_count))


def place(fields, modes, fields_out, modes_out, sem):
    copies = [
        pltpu.make_async_copy(fields, fields_out, sem.at[0]),
        pltpu.make_async_copy(modes, modes_out, sem.at[1]),
    ]
    for copy in copies:
        copy.start()
    for copy in copies:
        copy.wait()


def on_device(lon_count, lat_count, tables, state, depth, source_mask, gauge_lat, gauge_lon, misfit):
    rows, cols = depth.shape
    own_x, own_y = KX // lon_count, KY // lat_count
    high = rows + 2 * HALO
    bits = 2 if own_x % 32 == 0 else 1
    vmem = pl.BlockSpec(memory_space=pltpu.VMEM)
    hbm = pl.BlockSpec(memory_space=pltpu.HBM)
    dma = pltpu.SemaphoreType.DMA
    dealt = (3, high // 8, 8, 128)
    shapes = (
        jax.ShapeDtypeStruct((3, ADJ, rows, cols), FLOAT),
        jax.ShapeDtypeStruct((ADJ, own_x, own_y), FLOAT),
    )
    results = pl.pallas_call(
        functools.partial(kernel, lon_count, lat_count),
        out_shape=shapes,
        in_specs=[hbm] * 8,
        out_specs=(vmem, vmem),
        scratch_shapes=[
            pltpu.SMEM(source_mask.shape, jnp.int32),
            pltpu.SMEM((ADJ,), jnp.int32),
            pltpu.SMEM((ADJ,), jnp.int32),
            pltpu.SMEM((ADJ, STEPS), FLOAT),
            pltpu.VMEM((2, 3, 3, high, 128), FLOAT),
            pltpu.VMEM((3, high, 128), FLOAT),
            pltpu.VMEM((ADJ, 3, rows, cols), FLOAT),
            pltpu.VMEM((2, rows, cols), FLOAT),
            pltpu.VMEM((2, 2, rows // 2, 128), FLOAT),
            pltpu.VMEM((2, 2, HALO, 128), FLOAT),
            pltpu.VMEM((2, 2, rows // 2, 128), FLOAT),
            pltpu.VMEM((2, 2, HALO, 128), FLOAT),
            pltpu.VMEM(dealt, FLOAT),
            pltpu.VMEM(dealt, FLOAT),
            pltpu.VMEM((2, *dealt), FLOAT),
            pltpu.VMEM(dealt, FLOAT),
            pltpu.VMEM(dealt, FLOAT),
            pltpu.VMEM(dealt, FLOAT),
            pltpu.VMEM(dealt, FLOAT),
            pltpu.VMEM((2, *dealt), FLOAT),
            pltpu.VMEM((2, KX // 2, 4 * cols), HALF),
            pltpu.VMEM((2, 2 * lat_count * rows, 2 * own_y), HALF),
            pltpu.VMEM((ROUNDS, KX // 2, 2 * rows), FLOAT),
            pltpu.VMEM((ROUNDS, bits, lon_count, own_x // 2 // bits, 2 * rows), FLOAT),
            pltpu.VMEM((ROUNDS, bits, lat_count, own_x // bits, 2 * rows), FLOAT),
            pltpu.VMEM((3, HALO, 128), FLOAT),
            pltpu.VMEM((rows // 2, 128), FLOAT),
            pltpu.VMEM((sent_lines(rows, own_x, lon_count, lat_count), 128), FLOAT),
            dma((17 + 2 * ROUNDS * bits,)),
        ],
        compiler_params=pltpu.CompilerParams(
            collective_id=0, has_side_effects=True, vmem_limit_bytes=32 * 1024 * 1024
        ),
    )(*[pltpu.with_memory_space_constraint(x, pltpu.HBM) for x in (state, depth, source_mask, gauge_lat, gauge_lon, misfit.T, *tables)])
    return pl.pallas_call(
        place,
        out_shape=shapes,
        in_specs=[vmem] * 2,
        out_specs=(hbm, hbm),
        scratch_shapes=[dma((2,))],
    )(*[pltpu.with_memory_space_constraint(x, pltpu.VMEM) for x in results])


def solution(mesh):
    lon_count, lat_count = mesh.shape["lon"], mesh.shape["lat"]
    placed = (P(None, None, "lat", "lon"), P("lat", "lon"), P("lat", "lon"), P(), P(), P())

    def whole(state, depth, source_mask, gauge_lat, gauge_lon, misfit):
        total_rows, total_cols = depth.shape
        scale = 2.0 / math.sqrt(total_rows * total_cols)
        tables = (lon_table(total_cols, lon_count), lat_table(total_rows, lat_count, scale))

        def local(*args):
            constants = tuple(jnp.asarray(table) for table in tables)
            return on_device(lon_count, lat_count, constants, *args)

        return jax.shard_map(
            local,
            mesh=mesh,
            in_specs=placed,
            out_specs=(P(None, None, "lat", "lon"), P(None, "lon", "lat")),
            check_vma=False,
        )(state, depth, source_mask, gauge_lat, gauge_lon, misfit)

    return whole
```

```python
import functools
import math

import jax
import jax.numpy as jnp
import ml_dtypes
import numpy as np
from jax import lax
from jax.experimental import pallas as pl
from jax.experimental.pallas import tpu as pltpu
from jax.sharding import PartitionSpec as P

STEPS = 6
KX = 512
KY = 512
ADJ = 4
ROUNDS = ADJ // 2
HALO = 16
REACH = 2 * STEPS
SLOTS = 128 // HALO

MESH = pl.DeviceIdType.MESH
FLOAT = jnp.float32
HALF = jnp.bfloat16


def basis(total, modes):
    cells = np.arange(total, dtype=np.int64)
    order = np.arange(modes, dtype=np.int64)
    half = modes // 2
    wave = np.where(order < half, order, order - half + 1)
    phase = (cells[:, None] * wave[None, :] % total).astype(np.float64) * (2.0 * math.pi / total)
    return np.where(order[None, :] < half, np.cos(phase), np.sin(phase))


def halves(table):
    high = table.astype(ml_dtypes.bfloat16)
    low = (table - high.astype(np.float64)).astype(ml_dtypes.bfloat16)
    return high, low


def bits_of(lon_count):
    return 2 if KX // lon_count % 32 == 0 else 1


def lon_table(total, count):
    chips, bits = count // 2, bits_of(count)
    part = KX // count // 2 // bits
    table = basis(total, KX).T.reshape(count, 2, bits, part, chips, total // chips).transpose(4, 2, 0, 3, 1, 5)
    return np.stack(halves(table.reshape(chips, KX // 2, 2 * total // chips)), axis=1)


def lat_table(total, count, scale):
    own, rows = KY // count, total // count
    table = (scale * basis(total, KY)).reshape(count, rows, count, own).transpose(2, 0, 1, 3)
    both = np.zeros((count, count, 2, rows, 2, own))
    both[:, :, 0, :, 0, :] = table
    both[:, :, 1, :, 1, :] = table
    return np.stack(halves(both.reshape(count, 2 * total, 2 * own)), axis=1)


def split(x):
    high = x.astype(HALF)
    return high, (x - high.astype(FLOAT)).astype(HALF)


def sent_lines(rows, own, lon_count, lat_count):
    return 14 * rows + ROUNDS * (own // 2 * (lon_count - 1) + own * (lat_count - 1))


def kernel(
    lon_count, lat_count,
    state_hbm, depth_hbm, source_hbm, gauge_lat_hbm, gauge_lon_hbm, misfit_hbm, lon_hbm, lat_hbm,
    fields, modes,
    source, gauge_lat, gauge_lon, misfit,
    ext, dep, stage, masks, pack, corner, got, met,
    height, flow, total, coef_e, coef_w, coef_n, inside, gauges,
    lon_tab, lat_tab, part, pieces, gathered,
    zero, zero_strip, blank, sems,
):
    rows, cols = depth_hbm.shape
    high = rows + 2 * HALO
    depth_of = (rows + 2 * REACH) // 8
    base = HALO - REACH
    mine = slice(HALO, HALO + rows)
    own = modes.shape[1]
    part_own = own // 2
    bits = pieces.shape[1]
    bit = part_own // bits
    fold = rows // 2
    own_y = modes.shape[2]
    lon = lax.axis_index("lon")
    lat = lax.axis_index("lat")
    chips = lon_count // 2
    chip, core = lon // 2, lax.rem(lon, 2)
    mate = lon + 1 - 2 * core
    has_e, has_w = chip < chips - 1, chip > 0
    has_n, has_s = lat < lat_count - 1, lat > 0
    side = 2 * core - 1
    has_side = jnp.logical_or(jnp.logical_and(core == 0, has_w), jnp.logical_and(core == 1, has_e))
    lower, upper = slice(0, REACH), slice(rows - REACH, rows)
    north, south = slice(HALO + rows, HALO + rows + REACH), slice(base, HALO)

    arrived_a, arrived_b, returned, sent, sent_n, sent_s, sent_side, sent_side_n, sent_side_s, staged_a, staged_b, waves = range(12)
    reduced = waves + 6
    spread = reduced + ROUNDS * bits

    def settle(index, lines):
        pltpu.make_async_copy(blank.at[0:lines], blank.at[0:lines], sems.at[index]).wait()

    barrier = pltpu.get_barrier_semaphore()

    def greet(there, device):
        if there is True:
            pl.semaphore_signal(barrier, 1, device_id=device, device_id_type=MESH)
        else:
            @pl.when(there)
            def _():
                pl.semaphore_signal(barrier, 1, device_id=device, device_id_type=MESH)

    both = jnp.logical_and
    greet(has_n, (lon, lat + 1))
    greet(has_s, (lon, lat - 1))
    greet(has_n, (mate, lat + 1))
    greet(has_s, (mate, lat - 1))
    for d in range(1, lon_count):
        greet(True, (lax.rem(lon + d, lon_count), lat))
    greet(both(has_e, has_n), (2 * chip + 2, lat + 1))
    greet(both(has_e, has_s), (2 * chip + 2, lat - 1))
    greet(both(has_w, has_n), (2 * chip - 1, lat + 1))
    greet(both(has_w, has_s), (2 * chip - 1, lat - 1))
    for d in range(1, lat_count):
        target = lax.rem(lat + d, lat_count)
        near = jnp.logical_or(target == lat + 1, target == lat - 1)
        greet(jnp.logical_not(near), (lon, target))

    pairs = [
        (source_hbm, source), (gauge_lat_hbm, gauge_lat), (gauge_lon_hbm, gauge_lon), (misfit_hbm, misfit),
        (depth_hbm, dep.at[core, mine]),
        (state_hbm.at[:, 2 * core], ext.at[0, :, core, mine]), (state_hbm.at[:, 2 * core + 1], ext.at[1, :, core, mine]),
        (lon_hbm.at[chip], lon_tab), (lat_hbm.at[lat], lat_tab),
        *[(state_hbm.at[:, i], stage.at[i]) for i in range(ADJ)],
    ]
    places = [waves + 2, waves + 3, waves + 4, waves + 5, staged_a, arrived_a, arrived_b, waves, waves + 1]
    places += [staged_a, staged_b] * (ADJ // 2)
    loads = [pltpu.make_async_copy(a, b, sems.at[i]) for i, (a, b) in zip(places, pairs)]
    for i in (4, 9, 11, 10, 12, 0, 1, 2, 3, 5, 6):
        loads[i].start()

    def remote(source_ref, target, send, recv, device):
        return pltpu.make_async_remote_copy(
            src_ref=source_ref, dst_ref=target, send_sem=sems.at[send], recv_sem=sems.at[recv],
            device_id=device, device_id_type=MESH,
        )

    def ns_copy(way, k, item):
        taken, put, step = ((upper, south, 1), (lower, north, -1))[way]
        if item == 0:
            source_ref, target = depth_hbm.at[taken], dep.at[core, put]
        else:
            source_ref, target = state_hbm.at[:, 2 * k + item - 1, taken], ext.at[item - 1, :, core, put]
        return remote(source_ref, target, (sent_n, sent_s)[way], arrived_b if item == 2 else arrived_a, (2 * chip + k, lat + step))

    def ns_blank(way, k, item):
        put = (south, north)[way]
        if item == 0:
            return pltpu.make_async_copy(zero.at[0, 0:REACH], dep.at[k, put], sems.at[arrived_a])
        return pltpu.make_async_copy(zero.at[:, 0:REACH], ext.at[item - 1, :, k, put], sems.at[(arrived_a, arrived_b)[item - 1]])

    ns_goes, ns_comes = (has_n, has_s), (has_s, has_n)

    def side_copy(k, piece):
        step = (0, 0, 1, -1)[piece]
        source_ref = pack.at[piece, k] if piece < 2 else corner.at[piece - 2, k]
        target = got.at[piece, core] if piece < 2 else met.at[piece - 2, core]
        return remote(
            source_ref, target, (sent_side, sent_side, sent_side_n, sent_side_s)[piece],
            arrived_b if piece == 1 else arrived_a, (2 * (chip + side) + k, lat + step),
        )

    def side_blank(way, piece):
        source_ref = zero_strip if piece < 2 else zero.at[0]
        target = got.at[piece, way] if piece < 2 else met.at[piece - 2, way]
        return pltpu.make_async_copy(source_ref, target, sems.at[arrived_b if piece == 1 else arrived_a])

    side_goes = (has_side, has_side, both(has_side, has_n), both(has_side, has_s))
    side_comes = [(x, x, both(x, has_s), both(x, has_n)) for x in (has_e, has_w)]

    def mate_copy(item):
        if item == 0:
            source_ref, target = depth_hbm, dep.at[core, mine]
        elif item == 3:
            source_ref, target = masks.at[core], masks.at[core]
        elif item < 3:
            source_ref, target = state_hbm.at[:, 2 * (1 - core) + item - 1], ext.at[item - 1, :, core, mine]
        else:
            source_ref, target = ext.at[item - 4, :, 1 - core, mine], fields.at[:, 2 * core + item - 4]
        arrived = (arrived_a, arrived_a, arrived_b, arrived_a, returned, returned)[item]
        return remote(source_ref, target, sent, arrived, (mate, lat))

    def when(there, action):
        @pl.when(there)
        def _():
            action()

    zero[...] = jnp.zeros(zero.shape, FLOAT)
    zero_strip[...] = jnp.zeros(zero_strip.shape, FLOAT)
    for way in range(2):
        for k in range(2):
            for item in range(3):
                when(jnp.logical_not(ns_comes[way]), lambda: ns_blank(way, k, item).start())
        for piece in range(4):
            when(jnp.logical_not(side_comes[way][piece]), lambda: side_blank(way, piece).start())

    count = lon_count - 1 + lat_count - 1 + has_n.astype(jnp.int32) + has_s.astype(jnp.int32)
    count = count + 2 * side_goes[2].astype(jnp.int32) + 2 * side_goes[3].astype(jnp.int32)
    pl.semaphore_wait(barrier, count)

    for item in (0, 1):
        for k in range(2):
            for way in range(2):
                when(ns_goes[way], lambda: ns_copy(way, k, item).start())
    mate_copy(0).start()
    mate_copy(1).start()

    lane = lax.broadcasted_iota(jnp.int32, (fold, 128), 1)

    def slot_of(item, i, upper_half):
        return (i + SLOTS // 2 * (item + upper_half)) % SLOTS

    strips = {}
    for item in range(2):
        settle((staged_a, staged_b)[item], (7 - item) * rows)
        for k in range(2):
            arrays = [stage[2 * k + item, f] for f in range(3)]
            if item == 0:
                arrays.append(dep[core, mine])
            strip = jnp.zeros((fold, 128), FLOAT)
            for i, array in enumerate(arrays):
                for upper_half in range(2):
                    at = slot_of(item, i, upper_half) * HALO
                    moved = pltpu.roll(array[upper_half * fold:(upper_half + 1) * fold], at + HALO * core, 1)
                    strip = jnp.where(jnp.logical_and(lane >= at, lane < at + HALO), moved, strip)
            pack[item, k] = strip
            strips[item, k] = strip
            when(has_side, lambda: side_copy(k, item).start())
            if item == 1:
                begin = lane[:HALO] < 64
                first, second = strips[0, k], strips[1, k]
                corner[0, k] = jnp.where(begin, second[fold - HALO:], first[fold - HALO:])
                corner[1, k] = jnp.where(begin, first[:HALO], second[:HALO])
                for piece in (2, 3):
                    when(side_goes[piece], lambda: side_copy(k, piece).start())
    for k in range(2):
        for way in range(2):
            when(ns_goes[way], lambda: ns_copy(way, k, 2).start())
    mate_copy(2).start()

    loads[7].start()
    loads[8].start()

    for copy in loads[:4]:
        copy.wait()
    line = lax.broadcasted_iota(jnp.int32, (rows, cols), 0)
    place = lax.broadcasted_iota(jnp.int32, (rows, cols), 1)
    mask = jnp.zeros((rows, cols), FLOAT)
    width = rows // source.shape[0]
    for i in range(source.shape[0]):
        for j in range(source.shape[1]):
            tile = (line >= i * width) & (line < (i + 1) * width) & (place >= j * width) & (place < (j + 1) * width)
            mask = jnp.where(tile, source[i, j].astype(FLOAT), mask)
    masks[core] = mask
    mate_copy(3).start()

    shape = (depth_of, 8, 128)
    near = lax.broadcasted_iota(jnp.int32, shape, 1) * depth_of + lax.broadcasted_iota(jnp.int32, shape, 0)
    row = lat * rows - REACH + near
    across = lax.broadcasted_iota(jnp.int32, shape, 2)
    for j in range(3):
        if j < 2:
            col, real = across + j * 128, row == row
        else:
            col = jnp.where(across < HALO, across + 256, across - 128)
            real = jnp.logical_or(across < HALO, across >= 128 - HALO)
        col = chip * 256 + col
        valid = (row >= 0) & (row < lat_count * rows) & (col >= 0) & (col < chips * 256) & real
        inside[j] = jnp.where(valid, 1.0, 0.0).astype(FLOAT)
        for a in range(2):
            hit = (row == gauge_lat[2 * core + a]) & (col == gauge_lon[2 * core + a]) & real
            gauges[a, j] = jnp.where(hit, 1.0, 0.0).astype(FLOAT)

    half_wide = lax.broadcasted_iota(jnp.int32, (fold + HALO, 128), 1)

    def unpacked(item, i):
        parts = []
        for upper_half in range(2):
            at = slot_of(item, i, upper_half) * HALO
            sides = [jnp.concatenate([got[item, way], met[1 - upper_half, way]], axis=0) for way in range(2)]
            right = pltpu.roll(sides[0], (128 - at) % 128, 1)
            left = pltpu.roll(sides[1], (128 - at - HALO) % 128, 1)
            parts.append(jnp.where(half_wide < HALO, right, jnp.where(half_wide >= 128 - HALO, left, 0.0)))
        lower_half, upper_half = parts
        return jnp.concatenate([upper_half[fold:], lower_half[:fold], upper_half[:fold], lower_half[fold:]], axis=0)

    def dealt(ref):
        return jnp.stack([ref[pl.ds(base + v, 8, stride=depth_of), :] for v in range(depth_of)])

    def north_of(x, n):
        return jnp.concatenate([x[n:], pltpu.roll(x[:n], 7, 1)], axis=0)

    def south_of(x, n):
        return jnp.concatenate([pltpu.roll(x[-n:], 1, 1), x[:-n]], axis=0)

    def east_of(xs, n):
        turned = [pltpu.roll(x, 128 - n, 2) for x in xs]
        return [jnp.where(across < 128 - n, turned[j], turned[(j + 1) % 3]) for j in range(3)]

    def west_of(xs, n):
        turned = [pltpu.roll(x, n, 2) for x in xs]
        return [jnp.where(across >= n, turned[j], turned[j - 1]) for j in range(3)]

    tiles = range(3)

    edges = 2 * 2 * 3 * REACH + 2 * fold

    def arrive(a):
        settle((arrived_a, arrived_b)[a], edges + 6 * rows + (0 if a else 2 * 2 * REACH + 2 * 2 * HALO + 2 * rows))

    def deepen():
        dep[2] = unpacked(0, 3)
        deep = [dealt(dep.at[j]) * 0.0625 for j in tiles]
        ahead, behind = east_of(deep, 1), west_of(deep, 1)
        for j in tiles:
            coef_e[j] = ahead[j]
            coef_w[j] = behind[j]
            coef_n[j] = north_of(deep[j], 1)

    def flank(a):
        for f in range(3):
            ext[a, f, 2] = unpacked(a, f)

    def begin(a):
        east = [dealt(ext.at[a, 1, j]) for j in tiles]
        ahead, behind = east_of(east, 1), west_of(east, 1)
        for j in tiles:
            up = dealt(ext.at[a, 2, j])
            height[j] = dealt(ext.at[a, 0, j])
            change = (ahead[j] - behind[j]) + (north_of(up, 1) - south_of(up, 1))
            flow[j] = inside[j] * (0.25 * change)

    def rise(a, t, first):
        push = misfit[2 * core + a, t]
        now = []
        for j in tiles:
            h = height[j] + flow[j] + gauges[a, j] * push
            height[j] = h
            total[a, j] = h if first else total[a, j] + h
            now.append(h)
        return now

    def drive(now):
        ahead, behind = east_of(now, 2), west_of(now, 2)
        for j in tiles:
            lift = coef_n[j] * (north_of(now[j], 2) - now[j])
            along = coef_e[j] * (ahead[j] - now[j]) - coef_w[j] * (now[j] - behind[j])
            flow[j] = flow[j] + inside[j] * (along + (lift - south_of(lift, 2)))

    def advance(a):
        drive(rise(a, 0, True))

        def step(t, carry):
            drive(rise(a, t, False))
            return carry

        lax.fori_loop(1, STEPS - 1, step, 0)
        rise(a, STEPS - 1, False)

    def rs_copy(a, n, target):
        start = pl.multiple_of((n * lon_count + target) * bit, bit)
        return remote(
            part.at[a, pl.ds(start, bit)], pieces.at[a, n, lon],
            sent, reduced + a * bits + n, (target, lat),
        )

    dims = (((1,), (1,)), ((), ()))

    def project(a, beside):
        for j in range(2):
            for v in range(depth_of):
                ext[a, 0, j, pl.ds(base + v, 8, stride=depth_of), :] = height[j, v]
        masked = jnp.concatenate([ext[a, 0, j, mine] * masks[j] for j in range(2)], axis=1)
        high_m, low_m = split(masked)
        blank_m = jnp.zeros_like(high_m)

        def doubled(x):
            return jnp.concatenate(
                [jnp.concatenate([x, blank_m], axis=1), jnp.concatenate([blank_m, x], axis=1)], axis=0
            )

        data = jnp.concatenate([doubled(high_m), doubled(low_m)], axis=0)
        lines = lon_count * bit
        width = 2 * rows
        for n in range(bits):
            table = jnp.concatenate([lon_tab[0, n * lines:(n + 1) * lines], lon_tab[1, n * lines:(n + 1) * lines]], axis=0)
            result = lax.dot_general(table, data, dims, preferred_element_type=FLOAT)
            part[a, n * lines:(n + 1) * lines] = result[:lines, :width] + result[:lines, width:] + result[lines:, :width]
            for action in beside[n::bits]:
                action()
            for target in range(lon_count):
                when(target != lon, lambda: rs_copy(a, n, target).start())
            pieces[a, n, lon] = part[a, pl.ds(pl.multiple_of((n * lon_count + lon) * bit, bit), bit)]

    def finish(a):
        sums = [total[a, j] for j in tiles]
        ahead, behind = east_of(sums, 1), west_of(sums, 1)
        for j in range(2):
            deep = 0.25 * dealt(dep.at[j])
            east = dealt(ext.at[a, 1, j]) + deep * (ahead[j] - behind[j])
            up = dealt(ext.at[a, 2, j]) + deep * (north_of(sums[j], 1) - south_of(sums[j], 1))
            for v in range(depth_of):
                ext[a, 1, j, pl.ds(base + v, 8, stride=depth_of), :] = east[v]
                ext[a, 2, j, pl.ds(base + v, 8, stride=depth_of), :] = up[v]
        mate_copy(4 + a).start()
        for f in range(3):
            fields[f, 2 * core + a] = ext[a, f, core, mine]

    def ga_copy(a, n, z):
        return remote(gathered.at[a, n, lat], gathered.at[a, n, lat], sent, spread + a * bits + n, (lon, z))

    def collect(a, n):
        settle(reduced + a * bits + n, (lon_count - 1) * bit)
        sums = []
        for k in range(2):
            value = pieces[a, n, k]
            for c in range(1, chips):
                value = value + pieces[a, n, 2 * c + k]
            sums.append(value)
        gathered[a, n, lat] = jnp.concatenate(sums, axis=0)
        for z in range(lat_count):
            when(jnp.logical_or(z > lat, jnp.logical_and(z == 0, lat > 0)), lambda: ga_copy(a, n, z).start())

    def conclude(a, n):
        settle(spread + a * bits + n, (lat_count - 1) * 2 * bit)
        high_g, low_g = split(jnp.concatenate([gathered[a, n, z] for z in range(lat_count)], axis=1))
        result = (
            jnp.dot(high_g, lat_tab[0], preferred_element_type=FLOAT)
            + jnp.dot(low_g, lat_tab[0], preferred_element_type=FLOAT)
            + jnp.dot(high_g, lat_tab[1], preferred_element_type=FLOAT)
        )
        for k in range(2):
            for h in range(2):
                modes[2 * k + a, h * part_own + n * bit:h * part_own + (n + 1) * bit] = result[
                    k * bit:(k + 1) * bit, h * own_y:(h + 1) * own_y
                ]

    arrive(0)
    deepen()
    flank(0)
    begin(0)
    advance(0)
    loads[7].wait()
    arrive(1)
    project(0, (lambda: flank(1), lambda: begin(1)))
    advance(1)
    project(1, ())
    finish(0)
    finish(1)
    loads[8].wait()
    for a in range(ROUNDS):
        for n in range(bits):
            collect(a, n)
    for a in range(ROUNDS):
        for n in range(bits):
            for z in range(1, lat_count - 1):
                when(z < lat, lambda: ga_copy(a, n, z).start())
    settle(returned, 2 * 3 * rows)
    for a in range(ROUNDS):
        for n in range(bits):
            conclude(a, n)

    for way in range(2):
        when(ns_goes[way], lambda: settle((sent_n, sent_s)[way], 2 * 7 * REACH))
        when(side_goes[2 + way], lambda: settle((sent_side_n, sent_side_s)[way], 2 * HALO))
    when(has_side, lambda: settle(sent_side, 4 * fold))
    settle(sent, sent_lines(rows, own, lon_count, lat_count))


def place(fields, modes, fields_out, modes_out, sem):
    copies = [
        pltpu.make_async_copy(fields, fields_out, sem.at[0]),
        pltpu.make_async_copy(modes, modes_out, sem.at[1]),
    ]
    for copy in copies:
        copy.start()
    for copy in copies:
        copy.wait()


def on_device(lon_count, lat_count, tables, state, depth, source_mask, gauge_lat, gauge_lon, misfit):
    rows, cols = depth.shape
    own_x, own_y = KX // lon_count, KY // lat_count
    high = rows + 2 * HALO
    bits = bits_of(lon_count)
    vmem = pl.BlockSpec(memory_space=pltpu.VMEM)
    hbm = pl.BlockSpec(memory_space=pltpu.HBM)
    dma = pltpu.SemaphoreType.DMA
    dealt = (3, (rows + 2 * REACH) // 8, 8, 128)
    shapes = (
        jax.ShapeDtypeStruct((3, ADJ, rows, cols), FLOAT),
        jax.ShapeDtypeStruct((ADJ, own_x, own_y), FLOAT),
    )
    results = pl.pallas_call(
        functools.partial(kernel, lon_count, lat_count),
        out_shape=shapes,
        in_specs=[hbm] * 8,
        out_specs=(vmem, vmem),
        scratch_shapes=[
            pltpu.SMEM(source_mask.shape, jnp.int32),
            pltpu.SMEM((ADJ,), jnp.int32),
            pltpu.SMEM((ADJ,), jnp.int32),
            pltpu.SMEM((ADJ, STEPS), FLOAT),
            pltpu.VMEM((2, 3, 3, high, 128), FLOAT),
            pltpu.VMEM((3, high, 128), FLOAT),
            pltpu.VMEM((ADJ, 3, rows, cols), FLOAT),
            pltpu.VMEM((2, rows, cols), FLOAT),
            pltpu.VMEM((2, 2, rows // 2, 128), FLOAT),
            pltpu.VMEM((2, 2, HALO, 128), FLOAT),
            pltpu.VMEM((2, 2, rows // 2, 128), FLOAT),
            pltpu.VMEM((2, 2, HALO, 128), FLOAT),
            pltpu.VMEM(dealt, FLOAT),
            pltpu.VMEM(dealt, FLOAT),
            pltpu.VMEM((2, *dealt), FLOAT),
            pltpu.VMEM(dealt, FLOAT),
            pltpu.VMEM(dealt, FLOAT),
            pltpu.VMEM(dealt, FLOAT),
            pltpu.VMEM(dealt, FLOAT),
            pltpu.VMEM((2, *dealt), FLOAT),
            pltpu.VMEM((2, KX // 2, 4 * cols), HALF),
            pltpu.VMEM((2, 2 * lat_count * rows, 2 * own_y), HALF),
            pltpu.VMEM((ROUNDS, KX // 2, 2 * rows), FLOAT),
            pltpu.VMEM((ROUNDS, bits, lon_count, own_x // 2 // bits, 2 * rows), FLOAT),
            pltpu.VMEM((ROUNDS, bits, lat_count, own_x // bits, 2 * rows), FLOAT),
            pltpu.VMEM((3, HALO, 128), FLOAT),
            pltpu.VMEM((rows // 2, 128), FLOAT),
            pltpu.VMEM((sent_lines(rows, own_x, lon_count, lat_count), 128), FLOAT),
            dma((17 + 2 * ROUNDS * bits,)),
        ],
        compiler_params=pltpu.CompilerParams(
            collective_id=0, has_side_effects=True, vmem_limit_bytes=32 * 1024 * 1024
        ),
    )(*[pltpu.with_memory_space_constraint(x, pltpu.HBM) for x in (state, depth, source_mask, gauge_lat, gauge_lon, misfit.T, *tables)])
    return pl.pallas_call(
        place,
        out_shape=shapes,
        in_specs=[vmem] * 2,
        out_specs=(hbm, hbm),
        scratch_shapes=[dma((2,))],
    )(*[pltpu.with_memory_space_constraint(x, pltpu.VMEM) for x in results])


def solution(mesh):
    lon_count, lat_count = mesh.shape["lon"], mesh.shape["lat"]
    placed = (P(None, None, "lat", "lon"), P("lat", "lon"), P("lat", "lon"), P(), P(), P())

    def whole(state, depth, source_mask, gauge_lat, gauge_lon, misfit):
        total_rows, total_cols = depth.shape
        scale = 2.0 / math.sqrt(total_rows * total_cols)
        tables = (lon_table(total_cols, lon_count), lat_table(total_rows, lat_count, scale))

        def local(*args):
            constants = tuple(jnp.asarray(table) for table in tables)
            return on_device(lon_count, lat_count, constants, *args)

        return jax.shard_map(
            local,
            mesh=mesh,
            in_specs=placed,
            out_specs=(P(None, None, "lat", "lon"), P(None, "lon", "lat")),
            check_vma=False,
        )(state, depth, source_mask, gauge_lat, gauge_lon, misfit)

    return whole
```

```python
import functools
import math

import jax
import jax.numpy as jnp
import ml_dtypes
import numpy as np
from jax import lax
from jax.experimental import pallas as pl
from jax.experimental.pallas import tpu as pltpu
from jax.sharding import PartitionSpec as P

STEPS = 6
KX = 512
KY = 512
ADJ = 4
ROUNDS = ADJ // 2
HALO = 16
REACH = 2 * STEPS
SLOTS = 128 // HALO

MESH = pl.DeviceIdType.MESH
FLOAT = jnp.float32
HALF = jnp.bfloat16


def basis(total, modes):
    cells = np.arange(total, dtype=np.int64)
    order = np.arange(modes, dtype=np.int64)
    half = modes // 2
    wave = np.where(order < half, order, order - half + 1)
    phase = (cells[:, None] * wave[None, :] % total).astype(np.float64) * (2.0 * math.pi / total)
    return np.where(order[None, :] < half, np.cos(phase), np.sin(phase))


def halves(table):
    high = table.astype(ml_dtypes.bfloat16)
    low = (table - high.astype(np.float64)).astype(ml_dtypes.bfloat16)
    return high, low


def bits_of(lon_count):
    return 2 if KX // lon_count % 32 == 0 else 1


def lon_table(total, count):
    chips, bits = count // 2, bits_of(count)
    part = KX // count // 2 // bits
    table = basis(total, KX).T.reshape(count, 2, bits, part, chips, total // chips).transpose(4, 2, 0, 3, 1, 5)
    return np.stack(halves(table.reshape(chips, KX // 2, 2 * total // chips)), axis=1)


def lat_table(total, count, scale):
    own, rows = KY // count, total // count
    table = (scale * basis(total, KY)).reshape(count, rows, count, own).transpose(2, 0, 1, 3)
    both = np.zeros((count, count, 2, rows, 2, own))
    both[:, :, 0, :, 0, :] = table
    both[:, :, 1, :, 1, :] = table
    return np.stack(halves(both.reshape(count, 2 * total, 2 * own)), axis=1)


def split(x):
    high = x.astype(HALF)
    return high, (x - high.astype(FLOAT)).astype(HALF)


def sent_lines(rows, own, lon_count, lat_count):
    return 14 * rows + ROUNDS * (own // 2 * (lon_count - 1) + own * (lat_count - 1))


def kernel(
    lon_count, lat_count,
    state_hbm, depth_hbm, source_hbm, gauge_lat_hbm, gauge_lon_hbm, misfit_hbm, lon_hbm, lat_hbm,
    fields, modes,
    source, gauge_lat, gauge_lon, misfit,
    ext, dep, stage, masks, pack, corner, got, met,
    height, flow, total, coef_e, coef_w, coef_n, inside, gauges,
    lon_tab, lat_tab, part, pieces, gathered,
    zero, zero_strip, blank, sems,
):
    rows, cols = depth_hbm.shape
    high = rows + 2 * HALO
    depth_of = (rows + 2 * REACH) // 8
    base = HALO - REACH
    mine = slice(HALO, HALO + rows)
    own = modes.shape[1]
    part_own = own // 2
    bits = pieces.shape[1]
    bit = part_own // bits
    fold = rows // 2
    own_y = modes.shape[2]
    lon = lax.axis_index("lon")
    lat = lax.axis_index("lat")
    chips = lon_count // 2
    chip, core = lon // 2, lax.rem(lon, 2)
    mate = lon + 1 - 2 * core
    has_e, has_w = chip < chips - 1, chip > 0
    has_n, has_s = lat < lat_count - 1, lat > 0
    side = 2 * core - 1
    has_side = jnp.logical_or(jnp.logical_and(core == 0, has_w), jnp.logical_and(core == 1, has_e))
    lower, upper = slice(0, REACH), slice(rows - REACH, rows)
    north, south = slice(HALO + rows, HALO + rows + REACH), slice(base, HALO)

    arrived_a, arrived_b, returned, sent, sent_n, sent_s, sent_side, sent_side_n, sent_side_s, staged_a, staged_b, waves = range(12)
    reduced = waves + 6
    spread = reduced + ROUNDS * bits

    def settle(index, lines):
        pltpu.make_async_copy(blank.at[0:lines], blank.at[0:lines], sems.at[index]).wait()

    barrier = pltpu.get_barrier_semaphore()

    def greet(there, device):
        if there is True:
            pl.semaphore_signal(barrier, 1, device_id=device, device_id_type=MESH)
        else:
            @pl.when(there)
            def _():
                pl.semaphore_signal(barrier, 1, device_id=device, device_id_type=MESH)

    both = jnp.logical_and
    greet(has_n, (lon, lat + 1))
    greet(has_s, (lon, lat - 1))
    greet(has_n, (mate, lat + 1))
    greet(has_s, (mate, lat - 1))
    for d in range(1, lon_count):
        greet(True, (lax.rem(lon + d, lon_count), lat))
    greet(both(has_e, has_n), (2 * chip + 2, lat + 1))
    greet(both(has_e, has_s), (2 * chip + 2, lat - 1))
    greet(both(has_w, has_n), (2 * chip - 1, lat + 1))
    greet(both(has_w, has_s), (2 * chip - 1, lat - 1))
    for d in range(1, lat_count):
        target = lax.rem(lat + d, lat_count)
        near = jnp.logical_or(target == lat + 1, target == lat - 1)
        greet(jnp.logical_not(near), (lon, target))

    pairs = [
        (source_hbm, source), (gauge_lat_hbm, gauge_lat), (gauge_lon_hbm, gauge_lon), (misfit_hbm, misfit),
        (depth_hbm, dep.at[core, mine]),
        (state_hbm.at[:, 2 * core], ext.at[0, :, core, mine]), (state_hbm.at[:, 2 * core + 1], ext.at[1, :, core, mine]),
        (lon_hbm.at[chip], lon_tab), (lat_hbm.at[lat], lat_tab),
        *[(state_hbm.at[:, i], stage.at[i]) for i in range(ADJ)],
    ]
    places = [waves + 2, waves + 3, waves + 4, waves + 5, staged_a, arrived_a, arrived_b, waves, waves + 1]
    places += [staged_a, staged_b] * (ADJ // 2)
    loads = [pltpu.make_async_copy(a, b, sems.at[i]) for i, (a, b) in zip(places, pairs)]
    for i in (4, 9, 11, 10, 12, 0, 1, 2, 3, 5, 6):
        loads[i].start()

    def remote(source_ref, target, send, recv, device):
        return pltpu.make_async_remote_copy(
            src_ref=source_ref, dst_ref=target, send_sem=sems.at[send], recv_sem=sems.at[recv],
            device_id=device, device_id_type=MESH,
        )

    def ns_copy(way, k, item):
        taken, put, step = ((upper, south, 1), (lower, north, -1))[way]
        if item == 0:
            source_ref, target = dep.at[core, slice(taken.start + HALO, taken.stop + HALO)], dep.at[core, put]
        else:
            source_ref, target = stage.at[2 * k + item - 1, :, taken], ext.at[item - 1, :, core, put]
        return remote(source_ref, target, (sent_n, sent_s)[way], arrived_b if item == 2 else arrived_a, (2 * chip + k, lat + step))

    def ns_blank(way, k, item):
        put = (south, north)[way]
        if item == 0:
            return pltpu.make_async_copy(zero.at[0, 0:REACH], dep.at[k, put], sems.at[arrived_a])
        return pltpu.make_async_copy(zero.at[:, 0:REACH], ext.at[item - 1, :, k, put], sems.at[(arrived_a, arrived_b)[item - 1]])

    ns_goes, ns_comes = (has_n, has_s), (has_s, has_n)

    def side_copy(k, piece):
        step = (0, 0, 1, -1)[piece]
        source_ref = pack.at[piece, k] if piece < 2 else corner.at[piece - 2, k]
        target = got.at[piece, core] if piece < 2 else met.at[piece - 2, core]
        return remote(
            source_ref, target, (sent_side, sent_side, sent_side_n, sent_side_s)[piece],
            arrived_b if piece == 1 else arrived_a, (2 * (chip + side) + k, lat + step),
        )

    def side_blank(way, piece):
        source_ref = zero_strip if piece < 2 else zero.at[0]
        target = got.at[piece, way] if piece < 2 else met.at[piece - 2, way]
        return pltpu.make_async_copy(source_ref, target, sems.at[arrived_b if piece == 1 else arrived_a])

    side_goes = (has_side, has_side, both(has_side, has_n), both(has_side, has_s))
    side_comes = [(x, x, both(x, has_s), both(x, has_n)) for x in (has_e, has_w)]

    def mate_copy(item):
        if item == 0:
            source_ref, target = dep.at[core, mine], dep.at[core, mine]
        elif item == 3:
            source_ref, target = masks.at[core], masks.at[core]
        elif item < 3:
            source_ref, target = stage.at[2 * (1 - core) + item - 1], ext.at[item - 1, :, core, mine]
        else:
            source_ref, target = ext.at[item - 4, :, 1 - core, mine], fields.at[:, 2 * core + item - 4]
        arrived = (arrived_a, arrived_a, arrived_b, arrived_a, returned, returned)[item]
        return remote(source_ref, target, sent, arrived, (mate, lat))

    def when(there, action):
        @pl.when(there)
        def _():
            action()

    zero[...] = jnp.zeros(zero.shape, FLOAT)
    zero_strip[...] = jnp.zeros(zero_strip.shape, FLOAT)
    for way in range(2):
        for k in range(2):
            for item in range(3):
                when(jnp.logical_not(ns_comes[way]), lambda: ns_blank(way, k, item).start())
        for piece in range(4):
            when(jnp.logical_not(side_comes[way][piece]), lambda: side_blank(way, piece).start())

    count = lon_count - 1 + lat_count - 1 + has_n.astype(jnp.int32) + has_s.astype(jnp.int32)
    count = count + 2 * side_goes[2].astype(jnp.int32) + 2 * side_goes[3].astype(jnp.int32)

    lane = lax.broadcasted_iota(jnp.int32, (fold, 128), 1)

    def slot_of(item, i, upper_half):
        return (i + SLOTS // 2 * (item + upper_half)) % SLOTS

    strips = {}
    for item in range(2):
        settle((staged_a, staged_b)[item], (7 - item) * rows)
        for k in range(2):
            arrays = [stage[2 * k + item, f] for f in range(3)]
            if item == 0:
                arrays.append(dep[core, mine])
            strip = jnp.zeros((fold, 128), FLOAT)
            for i, array in enumerate(arrays):
                for upper_half in range(2):
                    at = slot_of(item, i, upper_half) * HALO
                    moved = pltpu.roll(array[upper_half * fold:(upper_half + 1) * fold], at + HALO * core, 1)
                    strip = jnp.where(jnp.logical_and(lane >= at, lane < at + HALO), moved, strip)
            pack[item, k] = strip
            strips[item, k] = strip
    for k in range(2):
        begin_lane = lane[:HALO] < 64
        first, second = strips[0, k], strips[1, k]
        corner[0, k] = jnp.where(begin_lane, second[fold - HALO:], first[fold - HALO:])
        corner[1, k] = jnp.where(begin_lane, first[:HALO], second[:HALO])
    pl.semaphore_wait(barrier, count)
    for k in range(2):
        for piece in (2, 3):
            when(side_goes[piece], lambda: side_copy(k, piece).start())
    for item in range(2):
        for k in range(2):
            when(has_side, lambda: side_copy(k, item).start())

    for item in (0, 1):
        for k in range(2):
            for way in range(2):
                when(ns_goes[way], lambda: ns_copy(way, k, item).start())
    mate_copy(0).start()
    mate_copy(1).start()

    for k in range(2):
        for way in range(2):
            when(ns_goes[way], lambda: ns_copy(way, k, 2).start())
    mate_copy(2).start()

    loads[7].start()
    loads[8].start()

    for copy in loads[:4]:
        copy.wait()
    line = lax.broadcasted_iota(jnp.int32, (rows, cols), 0)
    place = lax.broadcasted_iota(jnp.int32, (rows, cols), 1)
    mask = jnp.zeros((rows, cols), FLOAT)
    width = rows // source.shape[0]
    for i in range(source.shape[0]):
        for j in range(source.shape[1]):
            tile = (line >= i * width) & (line < (i + 1) * width) & (place >= j * width) & (place < (j + 1) * width)
            mask = jnp.where(tile, source[i, j].astype(FLOAT), mask)
    masks[core] = mask
    mate_copy(3).start()

    shape = (depth_of, 8, 128)
    near = lax.broadcasted_iota(jnp.int32, shape, 1) * depth_of + lax.broadcasted_iota(jnp.int32, shape, 0)
    row = lat * rows - REACH + near
    across = lax.broadcasted_iota(jnp.int32, shape, 2)
    for j in range(3):
        if j < 2:
            col, real = across + j * 128, row == row
        else:
            col = jnp.where(across < HALO, across + 256, across - 128)
            real = jnp.logical_or(across < HALO, across >= 128 - HALO)
        col = chip * 256 + col
        valid = (row >= 0) & (row < lat_count * rows) & (col >= 0) & (col < chips * 256) & real
        inside[j] = jnp.where(valid, 1.0, 0.0).astype(FLOAT)
        for a in range(2):
            hit = (row == gauge_lat[2 * core + a]) & (col == gauge_lon[2 * core + a]) & real
            gauges[a, j] = jnp.where(hit, 1.0, 0.0).astype(FLOAT)

    half_wide = lax.broadcasted_iota(jnp.int32, (fold + HALO, 128), 1)

    def unpacked(item, i):
        parts = []
        for upper_half in range(2):
            at = slot_of(item, i, upper_half) * HALO
            sides = [jnp.concatenate([got[item, way], met[1 - upper_half, way]], axis=0) for way in range(2)]
            right = pltpu.roll(sides[0], (128 - at) % 128, 1)
            left = pltpu.roll(sides[1], (128 - at - HALO) % 128, 1)
            parts.append(jnp.where(half_wide < HALO, right, jnp.where(half_wide >= 128 - HALO, left, 0.0)))
        lower_half, upper_half = parts
        return jnp.concatenate([upper_half[fold:], lower_half[:fold], upper_half[:fold], lower_half[fold:]], axis=0)

    def dealt(ref):
        return jnp.stack([ref[pl.ds(base + v, 8, stride=depth_of), :] for v in range(depth_of)])

    def north_of(x, n):
        return jnp.concatenate([x[n:], pltpu.roll(x[:n], 7, 1)], axis=0)

    def south_of(x, n):
        return jnp.concatenate([pltpu.roll(x[-n:], 1, 1), x[:-n]], axis=0)

    def east_of(xs, n):
        turned = [pltpu.roll(x, 128 - n, 2) for x in xs]
        return [jnp.where(across < 128 - n, turned[j], turned[(j + 1) % 3]) for j in range(3)]

    def west_of(xs, n):
        turned = [pltpu.roll(x, n, 2) for x in xs]
        return [jnp.where(across >= n, turned[j], turned[j - 1]) for j in range(3)]

    tiles = range(3)

    edges = 2 * 2 * 3 * REACH + 2 * fold

    def arrive(a):
        settle((arrived_a, arrived_b)[a], edges + 6 * rows + (0 if a else 2 * 2 * REACH + 2 * 2 * HALO + 2 * rows))

    def deepen():
        dep[2] = unpacked(0, 3)
        deep = [dealt(dep.at[j]) * 0.0625 for j in tiles]
        ahead, behind = east_of(deep, 1), west_of(deep, 1)
        for j in tiles:
            coef_e[j] = ahead[j]
            coef_w[j] = behind[j]
            coef_n[j] = north_of(deep[j], 1)

    def flank(a):
        for f in range(3):
            ext[a, f, 2] = unpacked(a, f)

    def begin(a):
        east = [dealt(ext.at[a, 1, j]) for j in tiles]
        ahead, behind = east_of(east, 1), west_of(east, 1)
        for j in tiles:
            up = dealt(ext.at[a, 2, j])
            height[j] = dealt(ext.at[a, 0, j])
            change = (ahead[j] - behind[j]) + (north_of(up, 1) - south_of(up, 1))
            flow[j] = inside[j] * (0.25 * change)

    def rise(a, t, first):
        push = misfit[2 * core + a, t]
        now = []
        for j in tiles:
            h = height[j] + flow[j] + gauges[a, j] * push
            height[j] = h
            total[a, j] = h if first else total[a, j] + h
            now.append(h)
        return now

    def drive(now):
        ahead, behind = east_of(now, 2), west_of(now, 2)
        for j in tiles:
            lift = coef_n[j] * (north_of(now[j], 2) - now[j])
            along = coef_e[j] * (ahead[j] - now[j]) - coef_w[j] * (now[j] - behind[j])
            flow[j] = flow[j] + inside[j] * (along + (lift - south_of(lift, 2)))

    def advance(a):
        drive(rise(a, 0, True))

        def step(t, carry):
            drive(rise(a, t, False))
            return carry

        lax.fori_loop(1, STEPS - 1, step, 0)
        rise(a, STEPS - 1, False)

    def rs_copy(a, n, target):
        start = pl.multiple_of((n * lon_count + target) * bit, bit)
        return remote(
            part.at[a, pl.ds(start, bit)], pieces.at[a, n, lon],
            sent, reduced + a * bits + n, (target, lat),
        )

    dims = (((1,), (1,)), ((), ()))

    def project(a, beside):
        for j in range(2):
            for v in range(depth_of):
                ext[a, 0, j, pl.ds(base + v, 8, stride=depth_of), :] = height[j, v]
        masked = jnp.concatenate([ext[a, 0, j, mine] * masks[j] for j in range(2)], axis=1)
        high_m, low_m = split(masked)
        blank_m = jnp.zeros_like(high_m)

        def doubled(x):
            return jnp.concatenate(
                [jnp.concatenate([x, blank_m], axis=1), jnp.concatenate([blank_m, x], axis=1)], axis=0
            )

        data = jnp.concatenate([doubled(high_m), doubled(low_m)], axis=0)
        lines = lon_count * bit
        width = 2 * rows
        for n in range(bits):
            table = jnp.concatenate([lon_tab[0, n * lines:(n + 1) * lines], lon_tab[1, n * lines:(n + 1) * lines]], axis=0)
            result = lax.dot_general(table, data, dims, preferred_element_type=FLOAT)
            part[a, n * lines:(n + 1) * lines] = result[:lines, :width] + result[:lines, width:] + result[lines:, :width]
            for action in beside[n::bits]:
                action()
            for target in range(lon_count):
                when(target != lon, lambda: rs_copy(a, n, target).start())
            pieces[a, n, lon] = part[a, pl.ds(pl.multiple_of((n * lon_count + lon) * bit, bit), bit)]

    def finish(a):
        sums = [total[a, j] for j in tiles]
        ahead, behind = east_of(sums, 1), west_of(sums, 1)
        for j in range(2):
            deep = 0.25 * dealt(dep.at[j])
            east = dealt(ext.at[a, 1, j]) + deep * (ahead[j] - behind[j])
            up = dealt(ext.at[a, 2, j]) + deep * (north_of(sums[j], 1) - south_of(sums[j], 1))
            for v in range(depth_of):
                ext[a, 1, j, pl.ds(base + v, 8, stride=depth_of), :] = east[v]
                ext[a, 2, j, pl.ds(base + v, 8, stride=depth_of), :] = up[v]
        mate_copy(4 + a).start()
        for f in range(3):
            fields[f, 2 * core + a] = ext[a, f, core, mine]

    def ga_copy(a, n, z):
        return remote(gathered.at[a, n, lat], gathered.at[a, n, lat], sent, spread + a * bits + n, (lon, z))

    def collect(a, n):
        settle(reduced + a * bits + n, (lon_count - 1) * bit)
        sums = []
        for k in range(2):
            value = pieces[a, n, k]
            for c in range(1, chips):
                value = value + pieces[a, n, 2 * c + k]
            sums.append(value)
        gathered[a, n, lat] = jnp.concatenate(sums, axis=0)
        for z in range(lat_count):
            when(jnp.logical_or(z > lat, jnp.logical_and(z == 0, lat > 0)), lambda: ga_copy(a, n, z).start())

    def conclude(a, n):
        settle(spread + a * bits + n, (lat_count - 1) * 2 * bit)
        high_g, low_g = split(jnp.concatenate([gathered[a, n, z] for z in range(lat_count)], axis=1))
        result = jnp.dot(jnp.concatenate([high_g, low_g], axis=0), lat_tab[0], preferred_element_type=FLOAT)
        result = result[:2 * bit] + result[2 * bit:] + jnp.dot(high_g, lat_tab[1], preferred_element_type=FLOAT)
        for k in range(2):
            for h in range(2):
                modes[2 * k + a, h * part_own + n * bit:h * part_own + (n + 1) * bit] = result[
                    k * bit:(k + 1) * bit, h * own_y:(h + 1) * own_y
                ]

    arrive(0)
    deepen()
    flank(0)
    begin(0)
    advance(0)
    loads[7].wait()
    arrive(1)
    project(0, (lambda: flank(1), lambda: begin(1)))
    advance(1)
    project(1, ())
    finish(0)
    finish(1)
    loads[8].wait()
    for a in range(ROUNDS):
        for n in range(bits):
            collect(a, n)
    for a in range(ROUNDS):
        for n in range(bits):
            for z in range(1, lat_count - 1):
                when(z < lat, lambda: ga_copy(a, n, z).start())
    settle(returned, 2 * 3 * rows)
    for a in range(ROUNDS):
        for n in range(bits):
            conclude(a, n)

    for way in range(2):
        when(ns_goes[way], lambda: settle((sent_n, sent_s)[way], 2 * 7 * REACH))
        when(side_goes[2 + way], lambda: settle((sent_side_n, sent_side_s)[way], 2 * HALO))
    when(has_side, lambda: settle(sent_side, 4 * fold))
    settle(sent, sent_lines(rows, own, lon_count, lat_count))


def place(fields, modes, fields_out, modes_out, sem):
    copies = [
        pltpu.make_async_copy(fields, fields_out, sem.at[0]),
        pltpu.make_async_copy(modes, modes_out, sem.at[1]),
    ]
    for copy in copies:
        copy.start()
    for copy in copies:
        copy.wait()


def on_device(lon_count, lat_count, tables, state, depth, source_mask, gauge_lat, gauge_lon, misfit):
    rows, cols = depth.shape
    own_x, own_y = KX // lon_count, KY // lat_count
    high = rows + 2 * HALO
    bits = bits_of(lon_count)
    vmem = pl.BlockSpec(memory_space=pltpu.VMEM)
    hbm = pl.BlockSpec(memory_space=pltpu.HBM)
    dma = pltpu.SemaphoreType.DMA
    dealt = (3, (rows + 2 * REACH) // 8, 8, 128)
    shapes = (
        jax.ShapeDtypeStruct((3, ADJ, rows, cols), FLOAT),
        jax.ShapeDtypeStruct((ADJ, own_x, own_y), FLOAT),
    )
    results = pl.pallas_call(
        functools.partial(kernel, lon_count, lat_count),
        out_shape=shapes,
        in_specs=[hbm] * 8,
        out_specs=(vmem, vmem),
        scratch_shapes=[
            pltpu.SMEM(source_mask.shape, jnp.int32),
            pltpu.SMEM((ADJ,), jnp.int32),
            pltpu.SMEM((ADJ,), jnp.int32),
            pltpu.SMEM((ADJ, STEPS), FLOAT),
            pltpu.VMEM((2, 3, 3, high, 128), FLOAT),
            pltpu.VMEM((3, high, 128), FLOAT),
            pltpu.VMEM((ADJ, 3, rows, cols), FLOAT),
            pltpu.VMEM((2, rows, cols), FLOAT),
            pltpu.VMEM((2, 2, rows // 2, 128), FLOAT),
            pltpu.VMEM((2, 2, HALO, 128), FLOAT),
            pltpu.VMEM((2, 2, rows // 2, 128), FLOAT),
            pltpu.VMEM((2, 2, HALO, 128), FLOAT),
            pltpu.VMEM(dealt, FLOAT),
            pltpu.VMEM(dealt, FLOAT),
            pltpu.VMEM((2, *dealt), FLOAT),
            pltpu.VMEM(dealt, FLOAT),
            pltpu.VMEM(dealt, FLOAT),
            pltpu.VMEM(dealt, FLOAT),
            pltpu.VMEM(dealt, FLOAT),
            pltpu.VMEM((2, *dealt), FLOAT),
            pltpu.VMEM((2, KX // 2, 4 * cols), HALF),
            pltpu.VMEM((2, 2 * lat_count * rows, 2 * own_y), HALF),
            pltpu.VMEM((ROUNDS, KX // 2, 2 * rows), FLOAT),
            pltpu.VMEM((ROUNDS, bits, lon_count, own_x // 2 // bits, 2 * rows), FLOAT),
            pltpu.VMEM((ROUNDS, bits, lat_count, own_x // bits, 2 * rows), FLOAT),
            pltpu.VMEM((3, HALO, 128), FLOAT),
            pltpu.VMEM((rows // 2, 128), FLOAT),
            pltpu.VMEM((sent_lines(rows, own_x, lon_count, lat_count), 128), FLOAT),
            dma((17 + 2 * ROUNDS * bits,)),
        ],
        compiler_params=pltpu.CompilerParams(
            collective_id=0, has_side_effects=True, vmem_limit_bytes=32 * 1024 * 1024
        ),
    )(*[pltpu.with_memory_space_constraint(x, pltpu.HBM) for x in (state, depth, source_mask, gauge_lat, gauge_lon, misfit.T, *tables)])
    return pl.pallas_call(
        place,
        out_shape=shapes,
        in_specs=[vmem] * 2,
        out_specs=(hbm, hbm),
        scratch_shapes=[dma((2,))],
    )(*[pltpu.with_memory_space_constraint(x, pltpu.VMEM) for x in results])


def solution(mesh):
    lon_count, lat_count = mesh.shape["lon"], mesh.shape["lat"]
    placed = (P(None, None, "lat", "lon"), P("lat", "lon"), P("lat", "lon"), P(), P(), P())

    def whole(state, depth, source_mask, gauge_lat, gauge_lon, misfit):
        total_rows, total_cols = depth.shape
        scale = 2.0 / math.sqrt(total_rows * total_cols)
        tables = (lon_table(total_cols, lon_count), lat_table(total_rows, lat_count, scale))

        def local(*args):
            constants = tuple(jnp.asarray(table) for table in tables)
            return on_device(lon_count, lat_count, constants, *args)

        return jax.shard_map(
            local,
            mesh=mesh,
            in_specs=placed,
            out_specs=(P(None, None, "lat", "lon"), P(None, "lon", "lat")),
            check_vma=False,
        )(state, depth, source_mask, gauge_lat, gauge_lon, misfit)

    return whole
```

```python
import functools
import math

import jax
import jax.numpy as jnp
import ml_dtypes
import numpy as np
from jax import lax
from jax.experimental import pallas as pl
from jax.experimental.pallas import tpu as pltpu
from jax.sharding import PartitionSpec as P

STEPS = 6
KX = 512
KY = 512
ADJ = 4
ROUNDS = ADJ // 2
HALO = 16
REACH = 2 * STEPS
SLOTS = 128 // HALO

MESH = pl.DeviceIdType.MESH
FLOAT = jnp.float32
HALF = jnp.bfloat16


def basis(total, modes):
    cells = np.arange(total, dtype=np.int64)
    order = np.arange(modes, dtype=np.int64)
    half = modes // 2
    wave = np.where(order < half, order, order - half + 1)
    phase = (cells[:, None] * wave[None, :] % total).astype(np.float64) * (2.0 * math.pi / total)
    return np.where(order[None, :] < half, np.cos(phase), np.sin(phase))


def halves(table):
    high = table.astype(ml_dtypes.bfloat16)
    low = (table - high.astype(np.float64)).astype(ml_dtypes.bfloat16)
    return high, low


def bits_of(lon_count):
    return 2 if KX // lon_count % 32 == 0 else 1


def lon_table(total, count):
    chips, bits = count // 2, bits_of(count)
    part = KX // count // 2 // bits
    table = basis(total, KX).T.reshape(count, 2, bits, part, chips, total // chips).transpose(4, 2, 0, 3, 1, 5)
    return np.stack(halves(table.reshape(chips, KX // 2, 2 * total // chips)), axis=1)


def lat_table(total, count, scale):
    own, rows = KY // count, total // count
    table = (scale * basis(total, KY)).reshape(count, rows, count, own).transpose(2, 0, 1, 3)
    both = np.zeros((count, count, 2, rows, 2, own))
    both[:, :, 0, :, 0, :] = table
    both[:, :, 1, :, 1, :] = table
    return np.stack(halves(both.reshape(count, 2 * total, 2 * own)), axis=1)


def split(x):
    high = x.astype(HALF)
    return high, (x - high.astype(FLOAT)).astype(HALF)


def sent_lines(rows, own, lon_count, lat_count):
    return 14 * rows + ROUNDS * (own // 2 * (lon_count - 1) + own * (lat_count - 1))


def kernel(
    lon_count, lat_count,
    state_hbm, depth_hbm, source_hbm, gauge_lat_hbm, gauge_lon_hbm, misfit_hbm, lon_hbm, lat_hbm,
    fields, modes,
    source, gauge_lat, gauge_lon, misfit,
    ext, dep, stage, masks, pack, corner, got, met,
    height, flow, total, coef_e, coef_w, coef_n, inside, gauges,
    lon_tab, lat_tab, part, pieces, gathered,
    zero, zero_strip, blank, sems,
):
    rows, cols = depth_hbm.shape
    high = rows + 2 * HALO
    depth_of = (rows + 2 * REACH) // 8
    base = HALO - REACH
    mine = slice(HALO, HALO + rows)
    own = modes.shape[1]
    part_own = own // 2
    bits = pieces.shape[1]
    bit = part_own // bits
    fold = rows // 2
    own_y = modes.shape[2]
    lon = lax.axis_index("lon")
    lat = lax.axis_index("lat")
    chips = lon_count // 2
    chip, core = lon // 2, lax.rem(lon, 2)
    mate = lon + 1 - 2 * core
    has_e, has_w = chip < chips - 1, chip > 0
    has_n, has_s = lat < lat_count - 1, lat > 0
    side = 2 * core - 1
    has_side = jnp.logical_or(jnp.logical_and(core == 0, has_w), jnp.logical_and(core == 1, has_e))
    lower, upper = slice(0, REACH), slice(rows - REACH, rows)
    north, south = slice(HALO + rows, HALO + rows + REACH), slice(base, HALO)

    arrived_a, arrived_b, flanked, returned, sent, staged, lon_held, lat_held, first = range(9)
    reduced = first + 4
    spread = reduced + ROUNDS * bits

    def settle(index, lines):
        pltpu.make_async_copy(blank.at[0:lines], blank.at[0:lines], sems.at[index]).wait()

    barrier = pltpu.get_barrier_semaphore()

    def greet(there, device):
        if there is True:
            pl.semaphore_signal(barrier, 1, device_id=device, device_id_type=MESH)
        else:
            @pl.when(there)
            def _():
                pl.semaphore_signal(barrier, 1, device_id=device, device_id_type=MESH)

    both = jnp.logical_and
    greet(has_n, (lon, lat + 1))
    greet(has_s, (lon, lat - 1))
    greet(has_n, (mate, lat + 1))
    greet(has_s, (mate, lat - 1))
    for d in range(1, lon_count):
        greet(True, (lax.rem(lon + d, lon_count), lat))
    greet(both(has_e, has_n), (2 * chip + 2, lat + 1))
    greet(both(has_e, has_s), (2 * chip + 2, lat - 1))
    greet(both(has_w, has_n), (2 * chip - 1, lat + 1))
    greet(both(has_w, has_s), (2 * chip - 1, lat - 1))
    for d in range(1, lat_count):
        target = lax.rem(lat + d, lat_count)
        near = jnp.logical_or(target == lat + 1, target == lat - 1)
        greet(jnp.logical_not(near), (lon, target))

    pairs = [
        (source_hbm, source), (gauge_lat_hbm, gauge_lat), (gauge_lon_hbm, gauge_lon), (misfit_hbm, misfit),
        (depth_hbm, dep.at[core, mine]),
        (state_hbm.at[:, 2 * core], ext.at[0, :, core, mine]), (state_hbm.at[:, 2 * core + 1], ext.at[1, :, core, mine]),
        (lon_hbm.at[chip], lon_tab), (lat_hbm.at[lat], lat_tab),
        *[(state_hbm.at[:, i], stage.at[i]) for i in range(ADJ)],
    ]
    places = [first, first + 1, first + 2, first + 3, staged, arrived_a, arrived_b, lon_held, lat_held] + [staged] * ADJ
    loads = [pltpu.make_async_copy(a, b, sems.at[i]) for i, (a, b) in zip(places, pairs)]
    for i in (4, 9, 11, 10, 12, 0, 1, 2, 3, 5, 6):
        loads[i].start()

    def remote(source_ref, target, send, recv, device):
        return pltpu.make_async_remote_copy(
            src_ref=source_ref, dst_ref=target, send_sem=sems.at[send], recv_sem=sems.at[recv],
            device_id=device, device_id_type=MESH,
        )

    def ns_copy(way, k, item):
        taken, put, step = ((upper, south, 1), (lower, north, -1))[way]
        if item == 0:
            source_ref, target = dep.at[core, slice(taken.start + HALO, taken.stop + HALO)], dep.at[core, put]
        else:
            source_ref, target = stage.at[2 * k + item - 1, :, taken], ext.at[item - 1, :, core, put]
        return remote(source_ref, target, sent, (flanked, arrived_a, arrived_b)[item], (2 * chip + k, lat + step))

    def ns_blank(way, k, item):
        put = (south, north)[way]
        if item == 0:
            return pltpu.make_async_copy(zero.at[0, 0:REACH], dep.at[k, put], sems.at[flanked])
        return pltpu.make_async_copy(zero.at[:, 0:REACH], ext.at[item - 1, :, k, put], sems.at[(arrived_a, arrived_b)[item - 1]])

    ns_goes, ns_comes = (has_n, has_s), (has_s, has_n)

    def side_copy(k, piece):
        step = (0, 0, 1, -1)[piece]
        source_ref = pack.at[piece, k] if piece < 2 else corner.at[piece - 2, k]
        target = got.at[piece, core] if piece < 2 else met.at[piece - 2, core]
        return remote(
            source_ref, target, sent,
            arrived_b if piece == 1 else flanked, (2 * (chip + side) + k, lat + step),
        )

    def side_blank(way, piece):
        source_ref = zero_strip if piece < 2 else zero.at[0]
        target = got.at[piece, way] if piece < 2 else met.at[piece - 2, way]
        return pltpu.make_async_copy(source_ref, target, sems.at[arrived_b if piece == 1 else flanked])

    side_goes = (has_side, has_side, both(has_side, has_n), both(has_side, has_s))
    side_comes = [(x, x, both(x, has_s), both(x, has_n)) for x in (has_e, has_w)]

    def mate_copy(item):
        if item == 0:
            source_ref, target = dep.at[core, mine], dep.at[core, mine]
        elif item == 3:
            source_ref, target = masks.at[core], masks.at[core]
        elif item < 3:
            source_ref, target = stage.at[2 * (1 - core) + item - 1], ext.at[item - 1, :, core, mine]
        else:
            source_ref, target = ext.at[item - 4, :, 1 - core, mine], fields.at[:, 2 * core + item - 4]
        arrived = (flanked, arrived_a, arrived_b, flanked, returned, returned)[item]
        return remote(source_ref, target, sent, arrived, (mate, lat))

    def when(there, action):
        @pl.when(there)
        def _():
            action()

    zero[...] = jnp.zeros(zero.shape, FLOAT)
    zero_strip[...] = jnp.zeros(zero_strip.shape, FLOAT)
    for way in range(2):
        for k in range(2):
            for item in range(3):
                when(jnp.logical_not(ns_comes[way]), lambda: ns_blank(way, k, item).start())
        for piece in range(4):
            when(jnp.logical_not(side_comes[way][piece]), lambda: side_blank(way, piece).start())

    count = lon_count - 1 + lat_count - 1 + has_n.astype(jnp.int32) + has_s.astype(jnp.int32)
    count = count + 2 * side_goes[2].astype(jnp.int32) + 2 * side_goes[3].astype(jnp.int32)

    lane = lax.broadcasted_iota(jnp.int32, (fold, 128), 1)

    def slot_of(item, i, upper_half):
        return (i + SLOTS // 2 * (item + upper_half)) % SLOTS

    strips = {}
    settle(staged, (1 + 3 * ADJ) * rows)
    for item in range(2):
        for k in range(2):
            arrays = [stage[2 * k + item, f] for f in range(3)]
            if item == 0:
                arrays.append(dep[core, mine])
            strip = jnp.zeros((fold, 128), FLOAT)
            for i, array in enumerate(arrays):
                for upper_half in range(2):
                    at = slot_of(item, i, upper_half) * HALO
                    moved = pltpu.roll(array[upper_half * fold:(upper_half + 1) * fold], at + HALO * core, 1)
                    strip = jnp.where(jnp.logical_and(lane >= at, lane < at + HALO), moved, strip)
            pack[item, k] = strip
            strips[item, k] = strip
    for k in range(2):
        begin_lane = lane[:HALO] < 64
        first, second = strips[0, k], strips[1, k]
        corner[0, k] = jnp.where(begin_lane, second[fold - HALO:], first[fold - HALO:])
        corner[1, k] = jnp.where(begin_lane, first[:HALO], second[:HALO])
    pl.semaphore_wait(barrier, count)
    for k in range(2):
        for piece in (2, 3):
            when(side_goes[piece], lambda: side_copy(k, piece).start())
    for item in range(2):
        for k in range(2):
            when(has_side, lambda: side_copy(k, item).start())

    for item in (0, 1):
        for k in range(2):
            for way in range(2):
                when(ns_goes[way], lambda: ns_copy(way, k, item).start())
    mate_copy(0).start()
    mate_copy(1).start()

    for k in range(2):
        for way in range(2):
            when(ns_goes[way], lambda: ns_copy(way, k, 2).start())
    mate_copy(2).start()

    loads[7].start()
    loads[8].start()

    for copy in loads[:4]:
        copy.wait()
    line = lax.broadcasted_iota(jnp.int32, (rows, cols), 0)
    place = lax.broadcasted_iota(jnp.int32, (rows, cols), 1)
    mask = jnp.zeros((rows, cols), FLOAT)
    width = rows // source.shape[0]
    for i in range(source.shape[0]):
        for j in range(source.shape[1]):
            tile = (line >= i * width) & (line < (i + 1) * width) & (place >= j * width) & (place < (j + 1) * width)
            mask = jnp.where(tile, source[i, j].astype(FLOAT), mask)
    masks[core] = mask
    mate_copy(3).start()

    shape = (depth_of, 8, 128)
    near = lax.broadcasted_iota(jnp.int32, shape, 1) * depth_of + lax.broadcasted_iota(jnp.int32, shape, 0)
    row = lat * rows - REACH + near
    across = lax.broadcasted_iota(jnp.int32, shape, 2)
    for j in range(3):
        if j < 2:
            col, real = across + j * 128, row == row
        else:
            col = jnp.where(across < HALO, across + 256, across - 128)
            real = jnp.logical_or(across < HALO, across >= 128 - HALO)
        col = chip * 256 + col
        valid = (row >= 0) & (row < lat_count * rows) & (col >= 0) & (col < chips * 256) & real
        inside[j] = jnp.where(valid, 1.0, 0.0).astype(FLOAT)
        for a in range(2):
            hit = (row == gauge_lat[2 * core + a]) & (col == gauge_lon[2 * core + a]) & real
            gauges[a, j] = jnp.where(hit, 1.0, 0.0).astype(FLOAT)

    half_wide = lax.broadcasted_iota(jnp.int32, (fold + HALO, 128), 1)

    def unpacked(item, i):
        parts = []
        for upper_half in range(2):
            at = slot_of(item, i, upper_half) * HALO
            sides = [jnp.concatenate([got[item, way], met[1 - upper_half, way]], axis=0) for way in range(2)]
            right = pltpu.roll(sides[0], (128 - at) % 128, 1)
            left = pltpu.roll(sides[1], (128 - at - HALO) % 128, 1)
            parts.append(jnp.where(half_wide < HALO, right, jnp.where(half_wide >= 128 - HALO, left, 0.0)))
        lower_half, upper_half = parts
        return jnp.concatenate([upper_half[fold:], lower_half[:fold], upper_half[:fold], lower_half[fold:]], axis=0)

    def dealt(ref):
        return jnp.stack([ref[pl.ds(base + v, 8, stride=depth_of), :] for v in range(depth_of)])

    def north_of(x, n):
        return jnp.concatenate([x[n:], pltpu.roll(x[:n], 7, 1)], axis=0)

    def south_of(x, n):
        return jnp.concatenate([pltpu.roll(x[-n:], 1, 1), x[:-n]], axis=0)

    def east_of(xs, n):
        turned = [pltpu.roll(x, 128 - n, 2) for x in xs]
        return [jnp.where(across < 128 - n, turned[j], turned[(j + 1) % 3]) for j in range(3)]

    def west_of(xs, n):
        turned = [pltpu.roll(x, n, 2) for x in xs]
        return [jnp.where(across >= n, turned[j], turned[j - 1]) for j in range(3)]

    tiles = range(3)

    def arrive(a):
        settle((arrived_a, arrived_b)[a], 2 * 2 * 3 * REACH + 6 * rows + (2 * fold if a else 0))

    def arrive_first():
        settle(flanked, 2 * 2 * REACH + 2 * fold + 2 * 2 * HALO + 2 * rows)

    def deepen():
        dep[2] = unpacked(0, 3)
        deep = [dealt(dep.at[j]) * 0.0625 for j in tiles]
        ahead, behind = east_of(deep, 1), west_of(deep, 1)
        for j in tiles:
            coef_e[j] = ahead[j]
            coef_w[j] = behind[j]
            coef_n[j] = north_of(deep[j], 1)

    def flank(a):
        for f in range(3):
            ext[a, f, 2] = unpacked(a, f)

    def begin(a):
        east = [dealt(ext.at[a, 1, j]) for j in tiles]
        ahead, behind = east_of(east, 1), west_of(east, 1)
        for j in tiles:
            up = dealt(ext.at[a, 2, j])
            height[j] = dealt(ext.at[a, 0, j])
            change = (ahead[j] - behind[j]) + (north_of(up, 1) - south_of(up, 1))
            flow[j] = inside[j] * (0.25 * change)

    def rise(a, t, first):
        push = misfit[2 * core + a, t]
        now = []
        for j in tiles:
            h = height[j] + flow[j] + gauges[a, j] * push
            height[j] = h
            total[a, j] = h if first else total[a, j] + h
            now.append(h)
        return now

    def drive(now):
        ahead, behind = east_of(now, 2), west_of(now, 2)
        for j in tiles:
            lift = coef_n[j] * (north_of(now[j], 2) - now[j])
            along = coef_e[j] * (ahead[j] - now[j]) - coef_w[j] * (now[j] - behind[j])
            flow[j] = flow[j] + inside[j] * (along + (lift - south_of(lift, 2)))

    def advance(a):
        drive(rise(a, 0, True))

        def step(t, carry):
            drive(rise(a, t, False))
            return carry

        lax.fori_loop(1, STEPS - 1, step, 0, unroll=True)
        rise(a, STEPS - 1, False)

    def rs_copy(a, n, target):
        start = pl.multiple_of((n * lon_count + target) * bit, bit)
        return remote(
            part.at[a, pl.ds(start, bit)], pieces.at[a, n, lon],
            sent, reduced + a * bits + n, (target, lat),
        )

    dims = (((1,), (1,)), ((), ()))

    def project(a, beside):
        for j in range(2):
            for v in range(depth_of):
                ext[a, 0, j, pl.ds(base + v, 8, stride=depth_of), :] = height[j, v]
        masked = jnp.concatenate([ext[a, 0, j, mine] * masks[j] for j in range(2)], axis=1)
        high_m, low_m = split(masked)
        blank_m = jnp.zeros_like(high_m)

        def doubled(x):
            return jnp.concatenate(
                [jnp.concatenate([x, blank_m], axis=1), jnp.concatenate([blank_m, x], axis=1)], axis=0
            )

        data = jnp.concatenate([doubled(high_m), doubled(low_m)], axis=0)
        lines = lon_count * bit
        width = 2 * rows
        for n in range(bits):
            table = jnp.concatenate([lon_tab[0, n * lines:(n + 1) * lines], lon_tab[1, n * lines:(n + 1) * lines]], axis=0)
            result = lax.dot_general(table, data, dims, preferred_element_type=FLOAT)
            part[a, n * lines:(n + 1) * lines] = result[:lines, :width] + result[:lines, width:] + result[lines:, :width]
            for action in beside[n::bits]:
                action()
            for target in range(lon_count):
                when(target != lon, lambda: rs_copy(a, n, target).start())
            pieces[a, n, lon] = part[a, pl.ds(pl.multiple_of((n * lon_count + lon) * bit, bit), bit)]

    def finish(a):
        sums = [total[a, j] for j in tiles]
        ahead, behind = east_of(sums, 1), west_of(sums, 1)
        for j in range(2):
            deep = 0.25 * dealt(dep.at[j])
            east = dealt(ext.at[a, 1, j]) + deep * (ahead[j] - behind[j])
            up = dealt(ext.at[a, 2, j]) + deep * (north_of(sums[j], 1) - south_of(sums[j], 1))
            for v in range(depth_of):
                ext[a, 1, j, pl.ds(base + v, 8, stride=depth_of), :] = east[v]
                ext[a, 2, j, pl.ds(base + v, 8, stride=depth_of), :] = up[v]
        mate_copy(4 + a).start()
        for f in range(3):
            fields[f, 2 * core + a] = ext[a, f, core, mine]

    def ga_copy(a, n, z):
        return remote(gathered.at[a, n, lat], gathered.at[a, n, lat], sent, spread + a * bits + n, (lon, z))

    def collect(a, n):
        settle(reduced + a * bits + n, (lon_count - 1) * bit)
        sums = []
        for k in range(2):
            value = pieces[a, n, k]
            for c in range(1, chips):
                value = value + pieces[a, n, 2 * c + k]
            sums.append(value)
        gathered[a, n, lat] = jnp.concatenate(sums, axis=0)
        for z in range(lat_count):
            when(jnp.logical_or(z > lat, jnp.logical_and(z == 0, lat > 0)), lambda: ga_copy(a, n, z).start())

    def conclude(a, n):
        settle(spread + a * bits + n, (lat_count - 1) * 2 * bit)
        high_g, low_g = split(jnp.concatenate([gathered[a, n, z] for z in range(lat_count)], axis=1))
        result = jnp.dot(jnp.concatenate([high_g, low_g], axis=0), lat_tab[0], preferred_element_type=FLOAT)
        result = result[:2 * bit] + result[2 * bit:] + jnp.dot(high_g, lat_tab[1], preferred_element_type=FLOAT)
        for k in range(2):
            for h in range(2):
                modes[2 * k + a, h * part_own + n * bit:h * part_own + (n + 1) * bit] = result[
                    k * bit:(k + 1) * bit, h * own_y:(h + 1) * own_y
                ]

    arrive_first()
    deepen()
    flank(0)
    arrive(0)
    begin(0)
    advance(0)
    loads[7].wait()
    arrive(1)
    project(0, (lambda: flank(1), lambda: begin(1)))
    advance(1)
    project(1, ())
    finish(0)
    finish(1)
    loads[8].wait()
    for a in range(ROUNDS):
        for n in range(bits):
            collect(a, n)
    for a in range(ROUNDS):
        for n in range(bits):
            for z in range(1, lat_count - 1):
                when(z < lat, lambda: ga_copy(a, n, z).start())
    settle(returned, 2 * 3 * rows)
    for a in range(ROUNDS):
        for n in range(bits):
            conclude(a, n)

    for way in range(2):
        when(ns_goes[way], lambda: settle(sent, 2 * 7 * REACH))
        when(side_goes[2 + way], lambda: settle(sent, 2 * HALO))
    when(has_side, lambda: settle(sent, 4 * fold))
    settle(sent, sent_lines(rows, own, lon_count, lat_count))


def place(fields, modes, fields_out, modes_out, sem):
    copies = [
        pltpu.make_async_copy(fields, fields_out, sem.at[0]),
        pltpu.make_async_copy(modes, modes_out, sem.at[1]),
    ]
    for copy in copies:
        copy.start()
    for copy in copies:
        copy.wait()


def on_device(lon_count, lat_count, tables, state, depth, source_mask, gauge_lat, gauge_lon, misfit):
    rows, cols = depth.shape
    own_x, own_y = KX // lon_count, KY // lat_count
    high = rows + 2 * HALO
    bits = bits_of(lon_count)
    vmem = pl.BlockSpec(memory_space=pltpu.VMEM)
    hbm = pl.BlockSpec(memory_space=pltpu.HBM)
    dma = pltpu.SemaphoreType.DMA
    dealt = (3, (rows + 2 * REACH) // 8, 8, 128)
    shapes = (
        jax.ShapeDtypeStruct((3, ADJ, rows, cols), FLOAT),
        jax.ShapeDtypeStruct((ADJ, own_x, own_y), FLOAT),
    )
    results = pl.pallas_call(
        functools.partial(kernel, lon_count, lat_count),
        out_shape=shapes,
        in_specs=[hbm] * 8,
        out_specs=(vmem, vmem),
        scratch_shapes=[
            pltpu.SMEM(source_mask.shape, jnp.int32),
            pltpu.SMEM((ADJ,), jnp.int32),
            pltpu.SMEM((ADJ,), jnp.int32),
            pltpu.SMEM((ADJ, STEPS), FLOAT),
            pltpu.VMEM((2, 3, 3, high, 128), FLOAT),
            pltpu.VMEM((3, high, 128), FLOAT),
            pltpu.VMEM((ADJ, 3, rows, cols), FLOAT),
            pltpu.VMEM((2, rows, cols), FLOAT),
            pltpu.VMEM((2, 2, rows // 2, 128), FLOAT),
            pltpu.VMEM((2, 2, HALO, 128), FLOAT),
            pltpu.VMEM((2, 2, rows // 2, 128), FLOAT),
            pltpu.VMEM((2, 2, HALO, 128), FLOAT),
            pltpu.VMEM(dealt, FLOAT),
            pltpu.VMEM(dealt, FLOAT),
            pltpu.VMEM((2, *dealt), FLOAT),
            pltpu.VMEM(dealt, FLOAT),
            pltpu.VMEM(dealt, FLOAT),
            pltpu.VMEM(dealt, FLOAT),
            pltpu.VMEM(dealt, FLOAT),
            pltpu.VMEM((2, *dealt), FLOAT),
            pltpu.VMEM((2, KX // 2, 4 * cols), HALF),
            pltpu.VMEM((2, 2 * lat_count * rows, 2 * own_y), HALF),
            pltpu.VMEM((ROUNDS, KX // 2, 2 * rows), FLOAT),
            pltpu.VMEM((ROUNDS, bits, lon_count, own_x // 2 // bits, 2 * rows), FLOAT),
            pltpu.VMEM((ROUNDS, bits, lat_count, own_x // bits, 2 * rows), FLOAT),
            pltpu.VMEM((3, HALO, 128), FLOAT),
            pltpu.VMEM((rows // 2, 128), FLOAT),
            pltpu.VMEM((sent_lines(rows, own_x, lon_count, lat_count), 128), FLOAT),
            dma((13 + 2 * ROUNDS * bits,)),
        ],
        compiler_params=pltpu.CompilerParams(
            collective_id=0, has_side_effects=True, vmem_limit_bytes=32 * 1024 * 1024
        ),
    )(*[pltpu.with_memory_space_constraint(x, pltpu.HBM) for x in (state, depth, source_mask, gauge_lat, gauge_lon, misfit.T, *tables)])
    return pl.pallas_call(
        place,
        out_shape=shapes,
        in_specs=[vmem] * 2,
        out_specs=(hbm, hbm),
        scratch_shapes=[dma((2,))],
    )(*[pltpu.with_memory_space_constraint(x, pltpu.VMEM) for x in results])


def solution(mesh):
    lon_count, lat_count = mesh.shape["lon"], mesh.shape["lat"]
    placed = (P(None, None, "lat", "lon"), P("lat", "lon"), P("lat", "lon"), P(), P(), P())

    def whole(state, depth, source_mask, gauge_lat, gauge_lon, misfit):
        total_rows, total_cols = depth.shape
        scale = 2.0 / math.sqrt(total_rows * total_cols)
        tables = (lon_table(total_cols, lon_count), lat_table(total_rows, lat_count, scale))

        def local(*args):
            constants = tuple(jnp.asarray(table) for table in tables)
            return on_device(lon_count, lat_count, constants, *args)

        return jax.shard_map(
            local,
            mesh=mesh,
            in_specs=placed,
            out_specs=(P(None, None, "lat", "lon"), P(None, "lon", "lat")),
            check_vma=False,
        )(state, depth, source_mask, gauge_lat, gauge_lon, misfit)

    return whole
```

```python
import functools
import math

import jax
import jax.numpy as jnp
import ml_dtypes
import numpy as np
from jax import lax
from jax.experimental import pallas as pl
from jax.experimental.pallas import tpu as pltpu
from jax.sharding import PartitionSpec as P

STEPS = 6
KX = 512
KY = 512
ADJ = 4
ROUNDS = ADJ // 2
HALO = 16
REACH = 2 * STEPS
SLOTS = 128 // HALO

MESH = pl.DeviceIdType.MESH
FLOAT = jnp.float32
HALF = jnp.bfloat16


def basis(total, modes):
    cells = np.arange(total, dtype=np.int64)
    order = np.arange(modes, dtype=np.int64)
    half = modes // 2
    wave = np.where(order < half, order, order - half + 1)
    phase = (cells[:, None] * wave[None, :] % total).astype(np.float64) * (2.0 * math.pi / total)
    return np.where(order[None, :] < half, np.cos(phase), np.sin(phase))


def halves(table):
    high = table.astype(ml_dtypes.bfloat16)
    low = (table - high.astype(np.float64)).astype(ml_dtypes.bfloat16)
    return high, low


def bits_of(lon_count):
    return 2 if KX // lon_count % 32 == 0 else 1


def lon_table(total, count):
    chips, bits = count // 2, bits_of(count)
    part = KX // count // 2 // bits
    table = basis(total, KX).T.reshape(count, 2, bits, part, chips, total // chips).transpose(4, 2, 0, 3, 1, 5)
    return np.stack(halves(table.reshape(chips, KX // 2, 2 * total // chips)), axis=1)


def lat_table(total, count, scale):
    own, rows = KY // count, total // count
    table = (scale * basis(total, KY)).reshape(count, rows, count, own).transpose(2, 0, 1, 3)
    both = np.zeros((count, count, 2, rows, 2, own))
    both[:, :, 0, :, 0, :] = table
    both[:, :, 1, :, 1, :] = table
    return np.stack(halves(both.reshape(count, 2 * total, 2 * own)), axis=1)


def split(x):
    high = x.astype(HALF)
    return high, (x - high.astype(FLOAT)).astype(HALF)


def along_lat(gathered, lat_tab, a, n):
    lines = gathered.shape[3]
    high_g, low_g = split(jnp.concatenate([gathered[a, n, z] for z in range(gathered.shape[2])], axis=1))
    result = jnp.dot(jnp.concatenate([high_g, low_g], axis=0), lat_tab[0], preferred_element_type=FLOAT)
    return result[:lines] + result[lines:] + jnp.dot(high_g, lat_tab[1], preferred_element_type=FLOAT)


def sent_lines(rows, own, lon_count, lat_count):
    return 14 * rows + ROUNDS * (own // 2 * (lon_count - 1) + own * (lat_count - 1))


def kernel(
    lon_count, lat_count,
    state_hbm, depth_hbm, source_hbm, gauge_lat_hbm, gauge_lon_hbm, misfit_hbm, lon_hbm, lat_hbm,
    fields, modes, lat_tab, gathered,
    source, gauge_lat, gauge_lon, misfit,
    ext, dep, stage, masks, pack, corner, got, met,
    height, flow, total, coef_e, coef_w, coef_n, inside, gauges,
    lon_tab, part, pieces,
    zero, zero_strip, blank, sems,
):
    rows, cols = depth_hbm.shape
    high = rows + 2 * HALO
    depth_of = (rows + 2 * REACH) // 8
    base = HALO - REACH
    mine = slice(HALO, HALO + rows)
    own = modes.shape[1]
    part_own = own // 2
    bits = pieces.shape[1]
    bit = part_own // bits
    fold = rows // 2
    own_y = modes.shape[2]
    lon = lax.axis_index("lon")
    lat = lax.axis_index("lat")
    chips = lon_count // 2
    chip, core = lon // 2, lax.rem(lon, 2)
    mate = lon + 1 - 2 * core
    has_e, has_w = chip < chips - 1, chip > 0
    has_n, has_s = lat < lat_count - 1, lat > 0
    side = 2 * core - 1
    has_side = jnp.logical_or(jnp.logical_and(core == 0, has_w), jnp.logical_and(core == 1, has_e))
    lower, upper = slice(0, REACH), slice(rows - REACH, rows)
    north, south = slice(HALO + rows, HALO + rows + REACH), slice(base, HALO)

    arrived_a, arrived_b, flanked, returned, sent, staged, lon_held, lat_held, first = range(9)
    reduced = first + 4
    spread = reduced + ROUNDS * bits

    def settle(index, lines):
        pltpu.make_async_copy(blank.at[0:lines], blank.at[0:lines], sems.at[index]).wait()

    barrier = pltpu.get_barrier_semaphore()

    def greet(there, device):
        if there is True:
            pl.semaphore_signal(barrier, 1, device_id=device, device_id_type=MESH)
        else:
            @pl.when(there)
            def _():
                pl.semaphore_signal(barrier, 1, device_id=device, device_id_type=MESH)

    both = jnp.logical_and
    greet(has_n, (lon, lat + 1))
    greet(has_s, (lon, lat - 1))
    greet(has_n, (mate, lat + 1))
    greet(has_s, (mate, lat - 1))
    for d in range(1, lon_count):
        greet(True, (lax.rem(lon + d, lon_count), lat))
    greet(both(has_e, has_n), (2 * chip + 2, lat + 1))
    greet(both(has_e, has_s), (2 * chip + 2, lat - 1))
    greet(both(has_w, has_n), (2 * chip - 1, lat + 1))
    greet(both(has_w, has_s), (2 * chip - 1, lat - 1))
    for d in range(1, lat_count):
        target = lax.rem(lat + d, lat_count)
        near = jnp.logical_or(target == lat + 1, target == lat - 1)
        greet(jnp.logical_not(near), (lon, target))

    pairs = [
        (source_hbm, source), (gauge_lat_hbm, gauge_lat), (gauge_lon_hbm, gauge_lon), (misfit_hbm, misfit),
        (depth_hbm, dep.at[core, mine]),
        (state_hbm.at[:, 2 * core], ext.at[0, :, core, mine]), (state_hbm.at[:, 2 * core + 1], ext.at[1, :, core, mine]),
        (lon_hbm.at[chip], lon_tab), (lat_hbm.at[lat], lat_tab),
        *[(state_hbm.at[:, i], stage.at[i]) for i in range(ADJ)],
    ]
    places = [first, first + 1, first + 2, first + 3, staged, arrived_a, arrived_b, lon_held, lat_held] + [staged] * ADJ
    loads = [pltpu.make_async_copy(a, b, sems.at[i]) for i, (a, b) in zip(places, pairs)]
    for i in (4, 9, 11, 10, 12, 0, 1, 2, 3, 5, 6):
        loads[i].start()

    def remote(source_ref, target, send, recv, device):
        return pltpu.make_async_remote_copy(
            src_ref=source_ref, dst_ref=target, send_sem=sems.at[send], recv_sem=sems.at[recv],
            device_id=device, device_id_type=MESH,
        )

    def ns_copy(way, k, item):
        taken, put, step = ((upper, south, 1), (lower, north, -1))[way]
        if item == 0:
            source_ref, target = dep.at[core, slice(taken.start + HALO, taken.stop + HALO)], dep.at[core, put]
        else:
            source_ref, target = stage.at[2 * k + item - 1, :, taken], ext.at[item - 1, :, core, put]
        return remote(source_ref, target, sent, (flanked, arrived_a, arrived_b)[item], (2 * chip + k, lat + step))

    def ns_blank(way, k, item):
        put = (south, north)[way]
        if item == 0:
            return pltpu.make_async_copy(zero.at[0, 0:REACH], dep.at[k, put], sems.at[flanked])
        return pltpu.make_async_copy(zero.at[:, 0:REACH], ext.at[item - 1, :, k, put], sems.at[(arrived_a, arrived_b)[item - 1]])

    ns_goes, ns_comes = (has_n, has_s), (has_s, has_n)

    def side_copy(k, piece):
        step = (0, 0, 1, -1)[piece]
        source_ref = pack.at[piece, k] if piece < 2 else corner.at[piece - 2, k]
        target = got.at[piece, core] if piece < 2 else met.at[piece - 2, core]
        return remote(
            source_ref, target, sent,
            arrived_b if piece == 1 else flanked, (2 * (chip + side) + k, lat + step),
        )

    def side_blank(way, piece):
        source_ref = zero_strip if piece < 2 else zero.at[0]
        target = got.at[piece, way] if piece < 2 else met.at[piece - 2, way]
        return pltpu.make_async_copy(source_ref, target, sems.at[arrived_b if piece == 1 else flanked])

    side_goes = (has_side, has_side, both(has_side, has_n), both(has_side, has_s))
    side_comes = [(x, x, both(x, has_s), both(x, has_n)) for x in (has_e, has_w)]

    def mate_copy(item):
        if item == 0:
            source_ref, target = dep.at[core, mine], dep.at[core, mine]
        elif item == 3:
            source_ref, target = masks.at[core], masks.at[core]
        elif item < 3:
            source_ref, target = stage.at[2 * (1 - core) + item - 1], ext.at[item - 1, :, core, mine]
        else:
            source_ref, target = ext.at[item - 4, :, 1 - core, mine], fields.at[:, 2 * core + item - 4]
        arrived = (flanked, arrived_a, arrived_b, flanked, returned, returned)[item]
        return remote(source_ref, target, sent, arrived, (mate, lat))

    def when(there, action):
        @pl.when(there)
        def _():
            action()

    zero[...] = jnp.zeros(zero.shape, FLOAT)
    zero_strip[...] = jnp.zeros(zero_strip.shape, FLOAT)
    for way in range(2):
        for k in range(2):
            for item in range(3):
                when(jnp.logical_not(ns_comes[way]), lambda: ns_blank(way, k, item).start())
        for piece in range(4):
            when(jnp.logical_not(side_comes[way][piece]), lambda: side_blank(way, piece).start())

    count = lon_count - 1 + lat_count - 1 + has_n.astype(jnp.int32) + has_s.astype(jnp.int32)
    count = count + 2 * side_goes[2].astype(jnp.int32) + 2 * side_goes[3].astype(jnp.int32)

    lane = lax.broadcasted_iota(jnp.int32, (fold, 128), 1)

    def slot_of(item, i, upper_half):
        return (i + SLOTS // 2 * (item + upper_half)) % SLOTS

    strips = {}
    settle(staged, (1 + 3 * ADJ) * rows)
    for item in range(2):
        for k in range(2):
            arrays = [stage[2 * k + item, f] for f in range(3)]
            if item == 0:
                arrays.append(dep[core, mine])
            strip = jnp.zeros((fold, 128), FLOAT)
            for i, array in enumerate(arrays):
                for upper_half in range(2):
                    at = slot_of(item, i, upper_half) * HALO
                    moved = pltpu.roll(array[upper_half * fold:(upper_half + 1) * fold], at + HALO * core, 1)
                    strip = jnp.where(jnp.logical_and(lane >= at, lane < at + HALO), moved, strip)
            pack[item, k] = strip
            strips[item, k] = strip
    for k in range(2):
        begin_lane = lane[:HALO] < 64
        first, second = strips[0, k], strips[1, k]
        corner[0, k] = jnp.where(begin_lane, second[fold - HALO:], first[fold - HALO:])
        corner[1, k] = jnp.where(begin_lane, first[:HALO], second[:HALO])
    pl.semaphore_wait(barrier, count)
    for k in range(2):
        for piece in (2, 3):
            when(side_goes[piece], lambda: side_copy(k, piece).start())
    for item in range(2):
        for k in range(2):
            when(has_side, lambda: side_copy(k, item).start())

    for item in (0, 1):
        for k in range(2):
            for way in range(2):
                when(ns_goes[way], lambda: ns_copy(way, k, item).start())
    mate_copy(0).start()
    mate_copy(1).start()

    for k in range(2):
        for way in range(2):
            when(ns_goes[way], lambda: ns_copy(way, k, 2).start())
    mate_copy(2).start()

    loads[7].start()
    loads[8].start()

    for copy in loads[:4]:
        copy.wait()
    line = lax.broadcasted_iota(jnp.int32, (rows, cols), 0)
    place = lax.broadcasted_iota(jnp.int32, (rows, cols), 1)
    mask = jnp.zeros((rows, cols), FLOAT)
    width = rows // source.shape[0]
    for i in range(source.shape[0]):
        for j in range(source.shape[1]):
            tile = (line >= i * width) & (line < (i + 1) * width) & (place >= j * width) & (place < (j + 1) * width)
            mask = jnp.where(tile, source[i, j].astype(FLOAT), mask)
    masks[core] = mask
    mate_copy(3).start()

    shape = (depth_of, 8, 128)
    near = lax.broadcasted_iota(jnp.int32, shape, 1) * depth_of + lax.broadcasted_iota(jnp.int32, shape, 0)
    row = lat * rows - REACH + near
    across = lax.broadcasted_iota(jnp.int32, shape, 2)
    for j in range(3):
        if j < 2:
            col, real = across + j * 128, row == row
        else:
            col = jnp.where(across < HALO, across + 256, across - 128)
            real = jnp.logical_or(across < HALO, across >= 128 - HALO)
        col = chip * 256 + col
        valid = (row >= 0) & (row < lat_count * rows) & (col >= 0) & (col < chips * 256) & real
        inside[j] = jnp.where(valid, 1.0, 0.0).astype(FLOAT)
        for a in range(2):
            hit = (row == gauge_lat[2 * core + a]) & (col == gauge_lon[2 * core + a]) & real
            gauges[a, j] = jnp.where(hit, 1.0, 0.0).astype(FLOAT)

    half_wide = lax.broadcasted_iota(jnp.int32, (fold + HALO, 128), 1)

    def unpacked(item, i):
        parts = []
        for upper_half in range(2):
            at = slot_of(item, i, upper_half) * HALO
            sides = [jnp.concatenate([got[item, way], met[1 - upper_half, way]], axis=0) for way in range(2)]
            right = pltpu.roll(sides[0], (128 - at) % 128, 1)
            left = pltpu.roll(sides[1], (128 - at - HALO) % 128, 1)
            parts.append(jnp.where(half_wide < HALO, right, jnp.where(half_wide >= 128 - HALO, left, 0.0)))
        lower_half, upper_half = parts
        return jnp.concatenate([upper_half[fold:], lower_half[:fold], upper_half[:fold], lower_half[fold:]], axis=0)

    def dealt(ref):
        return jnp.stack([ref[pl.ds(base + v, 8, stride=depth_of), :] for v in range(depth_of)])

    def north_of(x, n):
        return jnp.concatenate([x[n:], pltpu.roll(x[:n], 7, 1)], axis=0)

    def south_of(x, n):
        return jnp.concatenate([pltpu.roll(x[-n:], 1, 1), x[:-n]], axis=0)

    def east_of(xs, n):
        turned = [pltpu.roll(x, 128 - n, 2) for x in xs]
        return [jnp.where(across < 128 - n, turned[j], turned[(j + 1) % 3]) for j in range(3)]

    def west_of(xs, n):
        turned = [pltpu.roll(x, n, 2) for x in xs]
        return [jnp.where(across >= n, turned[j], turned[j - 1]) for j in range(3)]

    tiles = range(3)

    def arrive(a):
        settle((arrived_a, arrived_b)[a], 2 * 2 * 3 * REACH + 6 * rows + (2 * fold if a else 0))

    def arrive_first():
        settle(flanked, 2 * 2 * REACH + 2 * fold + 2 * 2 * HALO + 2 * rows)

    def deepen():
        dep[2] = unpacked(0, 3)
        deep = [dealt(dep.at[j]) * 0.0625 for j in tiles]
        ahead, behind = east_of(deep, 1), west_of(deep, 1)
        for j in tiles:
            coef_e[j] = ahead[j]
            coef_w[j] = behind[j]
            coef_n[j] = north_of(deep[j], 1)

    def flank(a):
        for f in range(3):
            ext[a, f, 2] = unpacked(a, f)

    def begin(a):
        east = [dealt(ext.at[a, 1, j]) for j in tiles]
        ahead, behind = east_of(east, 1), west_of(east, 1)
        for j in tiles:
            up = dealt(ext.at[a, 2, j])
            height[j] = dealt(ext.at[a, 0, j])
            change = (ahead[j] - behind[j]) + (north_of(up, 1) - south_of(up, 1))
            flow[j] = inside[j] * (0.25 * change)

    def rise(a, t, first):
        push = misfit[2 * core + a, t]
        now = []
        for j in tiles:
            h = height[j] + flow[j] + gauges[a, j] * push
            height[j] = h
            total[a, j] = h if first else total[a, j] + h
            now.append(h)
        return now

    def drive(now):
        ahead, behind = east_of(now, 2), west_of(now, 2)
        for j in tiles:
            lift = coef_n[j] * (north_of(now[j], 2) - now[j])
            along = coef_e[j] * (ahead[j] - now[j]) - coef_w[j] * (now[j] - behind[j])
            flow[j] = flow[j] + inside[j] * (along + (lift - south_of(lift, 2)))

    def advance(a):
        drive(rise(a, 0, True))

        def step(t, carry):
            drive(rise(a, t, False))
            return carry

        lax.fori_loop(1, STEPS - 1, step, 0, unroll=True)
        rise(a, STEPS - 1, False)

    def rs_copy(a, n, target):
        start = pl.multiple_of((n * lon_count + target) * bit, bit)
        return remote(
            part.at[a, pl.ds(start, bit)], pieces.at[a, n, lon],
            sent, reduced + a * bits + n, (target, lat),
        )

    dims = (((1,), (1,)), ((), ()))

    def project(a, beside):
        for j in range(2):
            for v in range(depth_of):
                ext[a, 0, j, pl.ds(base + v, 8, stride=depth_of), :] = height[j, v]
        masked = jnp.concatenate([ext[a, 0, j, mine] * masks[j] for j in range(2)], axis=1)
        high_m, low_m = split(masked)
        blank_m = jnp.zeros_like(high_m)

        def doubled(x):
            return jnp.concatenate(
                [jnp.concatenate([x, blank_m], axis=1), jnp.concatenate([blank_m, x], axis=1)], axis=0
            )

        data = jnp.concatenate([doubled(high_m), doubled(low_m)], axis=0)
        lines = lon_count * bit
        width = 2 * rows
        for n in range(bits):
            table = jnp.concatenate([lon_tab[0, n * lines:(n + 1) * lines], lon_tab[1, n * lines:(n + 1) * lines]], axis=0)
            result = lax.dot_general(table, data, dims, preferred_element_type=FLOAT)
            part[a, n * lines:(n + 1) * lines] = result[:lines, :width] + result[:lines, width:] + result[lines:, :width]
            for action in beside[n::bits]:
                action()
            for target in range(lon_count):
                when(target != lon, lambda: rs_copy(a, n, target).start())
            pieces[a, n, lon] = part[a, pl.ds(pl.multiple_of((n * lon_count + lon) * bit, bit), bit)]

    def finish(a):
        sums = [total[a, j] for j in tiles]
        ahead, behind = east_of(sums, 1), west_of(sums, 1)
        for j in range(2):
            deep = 0.25 * dealt(dep.at[j])
            east = dealt(ext.at[a, 1, j]) + deep * (ahead[j] - behind[j])
            up = dealt(ext.at[a, 2, j]) + deep * (north_of(sums[j], 1) - south_of(sums[j], 1))
            for v in range(depth_of):
                ext[a, 1, j, pl.ds(base + v, 8, stride=depth_of), :] = east[v]
                ext[a, 2, j, pl.ds(base + v, 8, stride=depth_of), :] = up[v]
        mate_copy(4 + a).start()
        for f in range(3):
            fields[f, 2 * core + a] = ext[a, f, core, mine]

    def ga_copy(a, n, z):
        return remote(gathered.at[a, n, lat], gathered.at[a, n, lat], sent, spread + a * bits + n, (lon, z))

    def collect(a, n):
        settle(reduced + a * bits + n, (lon_count - 1) * bit)
        sums = []
        for k in range(2):
            value = pieces[a, n, k]
            for c in range(1, chips):
                value = value + pieces[a, n, 2 * c + k]
            sums.append(value)
        gathered[a, n, lat] = jnp.concatenate(sums, axis=0)
        for z in range(lat_count):
            when(jnp.logical_or(z > lat, jnp.logical_and(z == 0, lat > 0)), lambda: ga_copy(a, n, z).start())

    def conclude(a, n):
        settle(spread + a * bits + n, (lat_count - 1) * 2 * bit)
        result = along_lat(gathered, lat_tab, a, n)
        for k in range(2):
            for h in range(2):
                modes[2 * k + a, h * part_own + n * bit:h * part_own + (n + 1) * bit] = result[
                    k * bit:(k + 1) * bit, h * own_y:(h + 1) * own_y
                ]

    arrive_first()
    deepen()
    flank(0)
    arrive(0)
    begin(0)
    advance(0)
    loads[7].wait()
    arrive(1)
    project(0, (lambda: flank(1), lambda: begin(1)))
    advance(1)
    project(1, ())
    finish(0)
    finish(1)
    loads[8].wait()
    for a in range(ROUNDS):
        for n in range(bits):
            collect(a, n)
    for a in range(ROUNDS):
        for n in range(bits):
            for z in range(1, lat_count - 1):
                when(z < lat, lambda: ga_copy(a, n, z).start())
    settle(returned, 2 * 3 * rows)
    for a in range(ROUNDS):
        for n in range(bits):
            if (a, n) != (ROUNDS - 1, bits - 1):
                conclude(a, n)
    settle(spread + ROUNDS * bits - 1, (lat_count - 1) * 2 * bit)

    for way in range(2):
        when(ns_goes[way], lambda: settle(sent, 2 * 7 * REACH))
        when(side_goes[2 + way], lambda: settle(sent, 2 * HALO))
    when(has_side, lambda: settle(sent, 4 * fold))
    settle(sent, sent_lines(rows, own, lon_count, lat_count))


def place(fields, modes, lat_tab, gathered, fields_out, modes_out, last, sem):
    rounds, bits, _, lines, _ = gathered.shape
    bit, own_y = lines // 2, modes.shape[2]
    part_own = bits * bit
    copies = [pltpu.make_async_copy(fields, fields_out, sem.at[0])]
    for k in range(2):
        whole = pl.ds(rounds * k, rounds - 1)
        copies.append(pltpu.make_async_copy(modes.at[whole], modes_out.at[whole], sem.at[1 + k]))
    for copy in copies:
        copy.start()
    result = along_lat(gathered, lat_tab, rounds - 1, bits - 1)
    for k in range(2):
        row = rounds * k + rounds - 1
        last[k] = modes[row]
        for h in range(2):
            start = h * part_own + (bits - 1) * bit
            last[k, start:start + bit] = result[k * bit:(k + 1) * bit, h * own_y:(h + 1) * own_y]
        copies.append(pltpu.make_async_copy(last.at[k], modes_out.at[row], sem.at[3 + k]))
        copies[-1].start()
    for copy in copies:
        copy.wait()


def on_device(lon_count, lat_count, tables, state, depth, source_mask, gauge_lat, gauge_lon, misfit):
    rows, cols = depth.shape
    own_x, own_y = KX // lon_count, KY // lat_count
    high = rows + 2 * HALO
    bits = bits_of(lon_count)
    vmem = pl.BlockSpec(memory_space=pltpu.VMEM)
    hbm = pl.BlockSpec(memory_space=pltpu.HBM)
    dma = pltpu.SemaphoreType.DMA
    dealt = (3, (rows + 2 * REACH) // 8, 8, 128)
    shapes = (
        jax.ShapeDtypeStruct((3, ADJ, rows, cols), FLOAT),
        jax.ShapeDtypeStruct((ADJ, own_x, own_y), FLOAT),
    )
    held = (
        jax.ShapeDtypeStruct((2, 2 * lat_count * rows, 2 * own_y), HALF),
        jax.ShapeDtypeStruct((ROUNDS, bits, lat_count, own_x // bits, 2 * rows), FLOAT),
    )
    results = pl.pallas_call(
        functools.partial(kernel, lon_count, lat_count),
        out_shape=shapes + held,
        in_specs=[hbm] * 8,
        out_specs=(vmem,) * 4,
        scratch_shapes=[
            pltpu.SMEM(source_mask.shape, jnp.int32),
            pltpu.SMEM((ADJ,), jnp.int32),
            pltpu.SMEM((ADJ,), jnp.int32),
            pltpu.SMEM((ADJ, STEPS), FLOAT),
            pltpu.VMEM((2, 3, 3, high, 128), FLOAT),
            pltpu.VMEM((3, high, 128), FLOAT),
            pltpu.VMEM((ADJ, 3, rows, cols), FLOAT),
            pltpu.VMEM((2, rows, cols), FLOAT),
            pltpu.VMEM((2, 2, rows // 2, 128), FLOAT),
            pltpu.VMEM((2, 2, HALO, 128), FLOAT),
            pltpu.VMEM((2, 2, rows // 2, 128), FLOAT),
            pltpu.VMEM((2, 2, HALO, 128), FLOAT),
            pltpu.VMEM(dealt, FLOAT),
            pltpu.VMEM(dealt, FLOAT),
            pltpu.VMEM((2, *dealt), FLOAT),
            pltpu.VMEM(dealt, FLOAT),
            pltpu.VMEM(dealt, FLOAT),
            pltpu.VMEM(dealt, FLOAT),
            pltpu.VMEM(dealt, FLOAT),
            pltpu.VMEM((2, *dealt), FLOAT),
            pltpu.VMEM((2, KX // 2, 4 * cols), HALF),
            pltpu.VMEM((ROUNDS, KX // 2, 2 * rows), FLOAT),
            pltpu.VMEM((ROUNDS, bits, lon_count, own_x // 2 // bits, 2 * rows), FLOAT),
            pltpu.VMEM((3, HALO, 128), FLOAT),
            pltpu.VMEM((rows // 2, 128), FLOAT),
            pltpu.VMEM((sent_lines(rows, own_x, lon_count, lat_count), 128), FLOAT),
            dma((13 + 2 * ROUNDS * bits,)),
        ],
        compiler_params=pltpu.CompilerParams(
            collective_id=0, has_side_effects=True, vmem_limit_bytes=32 * 1024 * 1024
        ),
    )(*[pltpu.with_memory_space_constraint(x, pltpu.HBM) for x in (state, depth, source_mask, gauge_lat, gauge_lon, misfit.T, *tables)])
    return pl.pallas_call(
        place,
        out_shape=shapes,
        in_specs=[vmem] * 4,
        out_specs=(hbm, hbm),
        scratch_shapes=[pltpu.VMEM((2, own_x, own_y), FLOAT), dma((5,))],
    )(*[pltpu.with_memory_space_constraint(x, pltpu.VMEM) for x in results])


def solution(mesh):
    lon_count, lat_count = mesh.shape["lon"], mesh.shape["lat"]
    placed = (P(None, None, "lat", "lon"), P("lat", "lon"), P("lat", "lon"), P(), P(), P())

    def whole(state, depth, source_mask, gauge_lat, gauge_lon, misfit):
        total_rows, total_cols = depth.shape
        scale = 2.0 / math.sqrt(total_rows * total_cols)
        tables = (lon_table(total_cols, lon_count), lat_table(total_rows, lat_count, scale))

        def local(*args):
            constants = tuple(jnp.asarray(table) for table in tables)
            return on_device(lon_count, lat_count, constants, *args)

        return jax.shard_map(
            local,
            mesh=mesh,
            in_specs=placed,
            out_specs=(P(None, None, "lat", "lon"), P(None, "lon", "lat")),
            check_vma=False,
        )(state, depth, source_mask, gauge_lat, gauge_lon, misfit)

    return whole
```

```python
import functools
import math

import jax
import jax.numpy as jnp
import ml_dtypes
import numpy as np
from jax import lax
from jax.experimental import pallas as pl
from jax.experimental.pallas import tpu as pltpu
from jax.sharding import PartitionSpec as P

STEPS = 6
KX = 512
KY = 512
ADJ = 4
ROUNDS = ADJ // 2
HALO = 16
REACH = 2 * STEPS
SLOTS = 128 // HALO

MESH = pl.DeviceIdType.MESH
FLOAT = jnp.float32
HALF = jnp.bfloat16


def basis(total, modes):
    cells = np.arange(total, dtype=np.int64)
    order = np.arange(modes, dtype=np.int64)
    half = modes // 2
    wave = np.where(order < half, order, order - half + 1)
    phase = (cells[:, None] * wave[None, :] % total).astype(np.float64) * (2.0 * math.pi / total)
    return np.where(order[None, :] < half, np.cos(phase), np.sin(phase))


def halves(table):
    high = table.astype(ml_dtypes.bfloat16)
    low = (table - high.astype(np.float64)).astype(ml_dtypes.bfloat16)
    return high, low


def bits_of(lon_count):
    return 2 if KX // lon_count % 32 == 0 else 1


def lon_table(total, count):
    chips, bits = count // 2, bits_of(count)
    part = KX // count // 2 // bits
    table = basis(total, KX).T.reshape(count, 2, bits, part, chips, total // chips).transpose(4, 2, 0, 3, 1, 5)
    return np.stack(halves(table.reshape(chips, KX // 2, 2 * total // chips)), axis=1)


def lat_table(total, count, scale):
    own, rows = KY // count, total // count
    table = (scale * basis(total, KY)).reshape(count, rows, count, own).transpose(2, 0, 1, 3)
    both = np.zeros((count, count, 2, rows, 2, own))
    both[:, :, 0, :, 0, :] = table
    both[:, :, 1, :, 1, :] = table
    return np.stack(halves(both.reshape(count, 2 * total, 2 * own)), axis=1)


def split(x):
    high = x.astype(HALF)
    return high, (x - high.astype(FLOAT)).astype(HALF)


def along_lat(gathered, lat_tab, a, n):
    lines = gathered.shape[3]
    high_g, low_g = split(jnp.concatenate([gathered[a, n, z] for z in range(gathered.shape[2])], axis=1))
    result = jnp.dot(jnp.concatenate([high_g, low_g], axis=0), lat_tab[0], preferred_element_type=FLOAT)
    return result[:lines] + result[lines:] + jnp.dot(high_g, lat_tab[1], preferred_element_type=FLOAT)


def sent_lines(rows, own, lon_count, lat_count):
    return 14 * rows + ROUNDS * (own // 2 * (lon_count - 1) + own * (lat_count - 1))


def kernel(
    lon_count, lat_count,
    state_hbm, depth_hbm, source_hbm, gauge_lat_hbm, gauge_lon_hbm, misfit_hbm, lon_hbm, lat_hbm,
    fields, modes, lat_tab, gathered,
    source, gauge_lat, gauge_lon, misfit,
    ext, dep, stage, masks, pack, corner, got, met,
    height, flow, total, coef_e, coef_w, coef_n, inside, gauges,
    lon_tab, part, pieces,
    zero, zero_strip, blank, sems,
):
    rows, cols = depth_hbm.shape
    high = rows + 2 * HALO
    depth_of = (rows + 2 * REACH) // 8
    base = HALO - REACH
    mine = slice(HALO, HALO + rows)
    own = modes.shape[1]
    part_own = own // 2
    bits = pieces.shape[1]
    bit = part_own // bits
    fold = rows // 2
    own_y = modes.shape[2]
    lon = lax.axis_index("lon")
    lat = lax.axis_index("lat")
    chips = lon_count // 2
    chip, core = lon // 2, lax.rem(lon, 2)
    mate = lon + 1 - 2 * core
    has_e, has_w = chip < chips - 1, chip > 0
    has_n, has_s = lat < lat_count - 1, lat > 0
    side = 2 * core - 1
    has_side = jnp.logical_or(jnp.logical_and(core == 0, has_w), jnp.logical_and(core == 1, has_e))
    lower, upper = slice(0, REACH), slice(rows - REACH, rows)
    north, south = slice(HALO + rows, HALO + rows + REACH), slice(base, HALO)

    arrived_a, arrived_b, flanked, returned, sent, staged, lon_held, lat_held, first = range(9)
    reduced = first + 4
    spread = reduced + ROUNDS * bits

    def settle(index, lines):
        pltpu.make_async_copy(blank.at[0:lines], blank.at[0:lines], sems.at[index]).wait()

    barrier = pltpu.get_barrier_semaphore()

    def greet(there, device):
        if there is True:
            pl.semaphore_signal(barrier, 1, device_id=device, device_id_type=MESH)
        else:
            @pl.when(there)
            def _():
                pl.semaphore_signal(barrier, 1, device_id=device, device_id_type=MESH)

    both = jnp.logical_and
    greet(has_n, (lon, lat + 1))
    greet(has_s, (lon, lat - 1))
    greet(has_n, (mate, lat + 1))
    greet(has_s, (mate, lat - 1))
    for d in range(1, lon_count):
        greet(True, (lax.rem(lon + d, lon_count), lat))
    greet(both(has_e, has_n), (2 * chip + 2, lat + 1))
    greet(both(has_e, has_s), (2 * chip + 2, lat - 1))
    greet(both(has_w, has_n), (2 * chip - 1, lat + 1))
    greet(both(has_w, has_s), (2 * chip - 1, lat - 1))
    for d in range(1, lat_count):
        target = lax.rem(lat + d, lat_count)
        near = jnp.logical_or(target == lat + 1, target == lat - 1)
        greet(jnp.logical_not(near), (lon, target))

    pairs = [
        (source_hbm, source), (gauge_lat_hbm, gauge_lat), (gauge_lon_hbm, gauge_lon), (misfit_hbm, misfit),
        (depth_hbm, dep.at[core, mine]),
        (state_hbm.at[:, 2 * core], ext.at[0, :, core, mine]), (state_hbm.at[:, 2 * core + 1], ext.at[1, :, core, mine]),
        (lon_hbm.at[chip], lon_tab), (lat_hbm.at[lat], lat_tab),
        *[(state_hbm.at[:, i], stage.at[i]) for i in range(ADJ)],
    ]
    places = [first, first + 1, first + 2, first + 3, staged, arrived_a, arrived_b, lon_held, lat_held] + [staged] * ADJ
    loads = [pltpu.make_async_copy(a, b, sems.at[i]) for i, (a, b) in zip(places, pairs)]
    for i in (4, 9, 11, 10, 12, 0, 1, 2, 3, 5, 6):
        loads[i].start()

    def remote(source_ref, target, send, recv, device):
        return pltpu.make_async_remote_copy(
            src_ref=source_ref, dst_ref=target, send_sem=sems.at[send], recv_sem=sems.at[recv],
            device_id=device, device_id_type=MESH,
        )

    def ns_copy(way, k, item):
        taken, put, step = ((upper, south, 1), (lower, north, -1))[way]
        if item == 0:
            source_ref, target = dep.at[core, slice(taken.start + HALO, taken.stop + HALO)], dep.at[core, put]
        else:
            source_ref, target = stage.at[2 * k + item - 1, :, taken], ext.at[item - 1, :, core, put]
        return remote(source_ref, target, sent, (flanked, arrived_a, arrived_b)[item], (2 * chip + k, lat + step))

    def ns_blank(way, k, item):
        put = (south, north)[way]
        if item == 0:
            return pltpu.make_async_copy(zero.at[0, 0:REACH], dep.at[k, put], sems.at[flanked])
        return pltpu.make_async_copy(zero.at[:, 0:REACH], ext.at[item - 1, :, k, put], sems.at[(arrived_a, arrived_b)[item - 1]])

    ns_goes, ns_comes = (has_n, has_s), (has_s, has_n)

    def side_copy(k, piece):
        step = (0, 0, 1, -1)[piece]
        source_ref = pack.at[piece, k] if piece < 2 else corner.at[piece - 2, k]
        target = got.at[piece, core] if piece < 2 else met.at[piece - 2, core]
        return remote(
            source_ref, target, sent,
            arrived_b if piece == 1 else flanked, (2 * (chip + side) + k, lat + step),
        )

    def side_blank(way, piece):
        source_ref = zero_strip if piece < 2 else zero.at[0]
        target = got.at[piece, way] if piece < 2 else met.at[piece - 2, way]
        return pltpu.make_async_copy(source_ref, target, sems.at[arrived_b if piece == 1 else flanked])

    side_goes = (has_side, has_side, both(has_side, has_n), both(has_side, has_s))
    side_comes = [(x, x, both(x, has_s), both(x, has_n)) for x in (has_e, has_w)]

    def mate_copy(item):
        if item == 0:
            source_ref, target = dep.at[core, mine], dep.at[core, mine]
        elif item == 3:
            source_ref, target = masks.at[core], masks.at[core]
        elif item < 3:
            source_ref, target = stage.at[2 * (1 - core) + item - 1], ext.at[item - 1, :, core, mine]
        else:
            source_ref, target = ext.at[item - 4, :, 1 - core, mine], fields.at[:, 2 * core + item - 4]
        arrived = (flanked, arrived_a, arrived_b, flanked, returned, returned)[item]
        return remote(source_ref, target, sent, arrived, (mate, lat))

    def when(there, action):
        @pl.when(there)
        def _():
            action()

    zero[...] = jnp.zeros(zero.shape, FLOAT)
    zero_strip[...] = jnp.zeros(zero_strip.shape, FLOAT)
    for way in range(2):
        for k in range(2):
            for item in range(3):
                when(jnp.logical_not(ns_comes[way]), lambda: ns_blank(way, k, item).start())
        for piece in range(4):
            when(jnp.logical_not(side_comes[way][piece]), lambda: side_blank(way, piece).start())

    count = lon_count - 1 + lat_count - 1 + has_n.astype(jnp.int32) + has_s.astype(jnp.int32)
    count = count + 2 * side_goes[2].astype(jnp.int32) + 2 * side_goes[3].astype(jnp.int32)

    lane = lax.broadcasted_iota(jnp.int32, (fold, 128), 1)

    def slot_of(item, i, upper_half):
        return (i + SLOTS // 2 * (item + upper_half)) % SLOTS

    strips = {}
    settle(staged, (1 + 3 * ADJ) * rows)
    for item in range(2):
        for k in range(2):
            arrays = [stage[2 * k + item, f] for f in range(3)]
            if item == 0:
                arrays.append(dep[core, mine])
            strip = jnp.zeros((fold, 128), FLOAT)
            for i, array in enumerate(arrays):
                for upper_half in range(2):
                    at = slot_of(item, i, upper_half) * HALO
                    moved = pltpu.roll(array[upper_half * fold:(upper_half + 1) * fold], at + HALO * core, 1)
                    strip = jnp.where(jnp.logical_and(lane >= at, lane < at + HALO), moved, strip)
            pack[item, k] = strip
            strips[item, k] = strip
    for k in range(2):
        begin_lane = lane[:HALO] < 64
        first, second = strips[0, k], strips[1, k]
        corner[0, k] = jnp.where(begin_lane, second[fold - HALO:], first[fold - HALO:])
        corner[1, k] = jnp.where(begin_lane, first[:HALO], second[:HALO])
    pl.semaphore_wait(barrier, count)
    for k in range(2):
        for piece in (2, 3):
            when(side_goes[piece], lambda: side_copy(k, piece).start())
    for item in (0,):
        for k in range(2):
            for way in range(2):
                when(ns_goes[way], lambda: ns_copy(way, k, item).start())
    for item in (0,):
        for k in range(2):
            when(has_side, lambda: side_copy(k, item).start())

    for item in (1,):
        for k in range(2):
            for way in range(2):
                when(ns_goes[way], lambda: ns_copy(way, k, item).start())
    mate_copy(0).start()
    mate_copy(1).start()
    for item in (1,):
        for k in range(2):
            when(has_side, lambda: side_copy(k, item).start())

    for k in range(2):
        for way in range(2):
            when(ns_goes[way], lambda: ns_copy(way, k, 2).start())
    mate_copy(2).start()

    loads[7].start()
    loads[8].start()

    for copy in loads[:4]:
        copy.wait()
    line = lax.broadcasted_iota(jnp.int32, (rows, cols), 0)
    place = lax.broadcasted_iota(jnp.int32, (rows, cols), 1)
    mask = jnp.zeros((rows, cols), FLOAT)
    width = rows // source.shape[0]
    for i in range(source.shape[0]):
        for j in range(source.shape[1]):
            tile = (line >= i * width) & (line < (i + 1) * width) & (place >= j * width) & (place < (j + 1) * width)
            mask = jnp.where(tile, source[i, j].astype(FLOAT), mask)
    masks[core] = mask
    mate_copy(3).start()

    shape = (depth_of, 8, 128)
    near = lax.broadcasted_iota(jnp.int32, shape, 1) * depth_of + lax.broadcasted_iota(jnp.int32, shape, 0)
    row = lat * rows - REACH + near
    across = lax.broadcasted_iota(jnp.int32, shape, 2)
    for j in range(3):
        if j < 2:
            col, real = across + j * 128, row == row
        else:
            col = jnp.where(across < HALO, across + 256, across - 128)
            real = jnp.logical_or(across < HALO, across >= 128 - HALO)
        col = chip * 256 + col
        valid = (row >= 0) & (row < lat_count * rows) & (col >= 0) & (col < chips * 256) & real
        inside[j] = jnp.where(valid, 1.0, 0.0).astype(FLOAT)
        for a in range(2):
            hit = (row == gauge_lat[2 * core + a]) & (col == gauge_lon[2 * core + a]) & real
            gauges[a, j] = jnp.where(hit, 1.0, 0.0).astype(FLOAT)

    half_wide = lax.broadcasted_iota(jnp.int32, (fold + HALO, 128), 1)

    def unpacked(item, i):
        parts = []
        for upper_half in range(2):
            at = slot_of(item, i, upper_half) * HALO
            sides = [jnp.concatenate([got[item, way], met[1 - upper_half, way]], axis=0) for way in range(2)]
            right = pltpu.roll(sides[0], (128 - at) % 128, 1)
            left = pltpu.roll(sides[1], (128 - at - HALO) % 128, 1)
            parts.append(jnp.where(half_wide < HALO, right, jnp.where(half_wide >= 128 - HALO, left, 0.0)))
        lower_half, upper_half = parts
        return jnp.concatenate([upper_half[fold:], lower_half[:fold], upper_half[:fold], lower_half[fold:]], axis=0)

    def dealt(ref):
        return jnp.stack([ref[pl.ds(base + v, 8, stride=depth_of), :] for v in range(depth_of)])

    def north_of(x, n):
        return jnp.concatenate([x[n:], pltpu.roll(x[:n], 7, 1)], axis=0)

    def south_of(x, n):
        return jnp.concatenate([pltpu.roll(x[-n:], 1, 1), x[:-n]], axis=0)

    def east_of(xs, n):
        turned = [pltpu.roll(x, 128 - n, 2) for x in xs]
        return [jnp.where(across < 128 - n, turned[j], turned[(j + 1) % 3]) for j in range(3)]

    def west_of(xs, n):
        turned = [pltpu.roll(x, n, 2) for x in xs]
        return [jnp.where(across >= n, turned[j], turned[j - 1]) for j in range(3)]

    tiles = range(3)

    def arrive(a):
        settle((arrived_a, arrived_b)[a], 2 * 2 * 3 * REACH + 6 * rows + (2 * fold if a else 0))

    def arrive_first():
        settle(flanked, 2 * 2 * REACH + 2 * fold + 2 * 2 * HALO + 2 * rows)

    def deepen():
        dep[2] = unpacked(0, 3)
        deep = [dealt(dep.at[j]) * 0.0625 for j in tiles]
        ahead, behind = east_of(deep, 1), west_of(deep, 1)
        for j in tiles:
            coef_e[j] = ahead[j]
            coef_w[j] = behind[j]
            coef_n[j] = north_of(deep[j], 1)

    def flank(a):
        for f in range(3):
            ext[a, f, 2] = unpacked(a, f)

    def begin(a):
        east = [dealt(ext.at[a, 1, j]) for j in tiles]
        ahead, behind = east_of(east, 1), west_of(east, 1)
        for j in tiles:
            up = dealt(ext.at[a, 2, j])
            height[j] = dealt(ext.at[a, 0, j])
            change = (ahead[j] - behind[j]) + (north_of(up, 1) - south_of(up, 1))
            flow[j] = inside[j] * (0.25 * change)

    def rise(a, t, first):
        push = misfit[2 * core + a, t]
        now = []
        for j in tiles:
            h = height[j] + flow[j] + gauges[a, j] * push
            height[j] = h
            total[a, j] = h if first else total[a, j] + h
            now.append(h)
        return now

    def drive(now):
        ahead, behind = east_of(now, 2), west_of(now, 2)
        for j in tiles:
            lift = coef_n[j] * (north_of(now[j], 2) - now[j])
            along = coef_e[j] * (ahead[j] - now[j]) - coef_w[j] * (now[j] - behind[j])
            flow[j] = flow[j] + inside[j] * (along + (lift - south_of(lift, 2)))

    def advance(a):
        drive(rise(a, 0, True))

        def step(t, carry):
            drive(rise(a, t, False))
            return carry

        lax.fori_loop(1, STEPS - 1, step, 0, unroll=True)
        rise(a, STEPS - 1, False)

    def rs_copy(a, n, target):
        start = pl.multiple_of((n * lon_count + target) * bit, bit)
        return remote(
            part.at[a, pl.ds(start, bit)], pieces.at[a, n, lon],
            sent, reduced + a * bits + n, (target, lat),
        )

    dims = (((1,), (1,)), ((), ()))

    def project(a, beside):
        for j in range(2):
            for v in range(depth_of):
                ext[a, 0, j, pl.ds(base + v, 8, stride=depth_of), :] = height[j, v]
        masked = jnp.concatenate([ext[a, 0, j, mine] * masks[j] for j in range(2)], axis=1)
        high_m, low_m = split(masked)
        blank_m = jnp.zeros_like(high_m)

        def doubled(x):
            return jnp.concatenate(
                [jnp.concatenate([x, blank_m], axis=1), jnp.concatenate([blank_m, x], axis=1)], axis=0
            )

        data = jnp.concatenate([doubled(high_m), doubled(low_m)], axis=0)
        lines = lon_count * bit
        width = 2 * rows
        for n in range(bits):
            table = jnp.concatenate([lon_tab[0, n * lines:(n + 1) * lines], lon_tab[1, n * lines:(n + 1) * lines]], axis=0)
            result = lax.dot_general(table, data, dims, preferred_element_type=FLOAT)
            part[a, n * lines:(n + 1) * lines] = result[:lines, :width] + result[:lines, width:] + result[lines:, :width]
            for action in beside[n::bits]:
                action()
            for target in range(lon_count):
                when(target != lon, lambda: rs_copy(a, n, target).start())
            pieces[a, n, lon] = part[a, pl.ds(pl.multiple_of((n * lon_count + lon) * bit, bit), bit)]

    def finish(a):
        sums = [total[a, j] for j in tiles]
        ahead, behind = east_of(sums, 1), west_of(sums, 1)
        for j in range(2):
            deep = 0.25 * dealt(dep.at[j])
            east = dealt(ext.at[a, 1, j]) + deep * (ahead[j] - behind[j])
            up = dealt(ext.at[a, 2, j]) + deep * (north_of(sums[j], 1) - south_of(sums[j], 1))
            for v in range(depth_of):
                ext[a, 1, j, pl.ds(base + v, 8, stride=depth_of), :] = east[v]
                ext[a, 2, j, pl.ds(base + v, 8, stride=depth_of), :] = up[v]
        mate_copy(4 + a).start()
        for f in range(3):
            fields[f, 2 * core + a] = ext[a, f, core, mine]

    def ga_copy(a, n, z):
        return remote(gathered.at[a, n, lat], gathered.at[a, n, lat], sent, spread + a * bits + n, (lon, z))

    def collect(a, n):
        settle(reduced + a * bits + n, (lon_count - 1) * bit)
        sums = []
        for k in range(2):
            value = pieces[a, n, k]
            for c in range(1, chips):
                value = value + pieces[a, n, 2 * c + k]
            sums.append(value)
        gathered[a, n, lat] = jnp.concatenate(sums, axis=0)
        for z in range(lat_count):
            when(jnp.logical_or(z > lat, jnp.logical_and(z == 0, lat > 0)), lambda: ga_copy(a, n, z).start())

    def conclude(a, n):
        settle(spread + a * bits + n, (lat_count - 1) * 2 * bit)
        result = along_lat(gathered, lat_tab, a, n)
        for k in range(2):
            for h in range(2):
                modes[2 * k + a, h * part_own + n * bit:h * part_own + (n + 1) * bit] = result[
                    k * bit:(k + 1) * bit, h * own_y:(h + 1) * own_y
                ]

    arrive_first()
    deepen()
    flank(0)
    arrive(0)
    begin(0)
    advance(0)
    loads[7].wait()
    arrive(1)
    project(0, (lambda: flank(1), lambda: begin(1)))
    advance(1)
    project(1, ())
    finish(0)
    finish(1)
    loads[8].wait()
    for a in range(ROUNDS):
        for n in range(bits):
            collect(a, n)
    for a in range(ROUNDS):
        for n in range(bits):
            for z in range(1, lat_count - 1):
                when(z < lat, lambda: ga_copy(a, n, z).start())
    settle(returned, 2 * 3 * rows)
    for a in range(ROUNDS):
        for n in range(bits):
            if (a, n) != (ROUNDS - 1, bits - 1):
                conclude(a, n)
    settle(spread + ROUNDS * bits - 1, (lat_count - 1) * 2 * bit)

    for way in range(2):
        when(ns_goes[way], lambda: settle(sent, 2 * 7 * REACH))
        when(side_goes[2 + way], lambda: settle(sent, 2 * HALO))
    when(has_side, lambda: settle(sent, 4 * fold))
    settle(sent, sent_lines(rows, own, lon_count, lat_count))


def place(fields, modes, lat_tab, gathered, fields_out, modes_out, last, sem):
    rounds, bits, _, lines, _ = gathered.shape
    bit, own_y = lines // 2, modes.shape[2]
    part_own = bits * bit
    copies = [pltpu.make_async_copy(fields, fields_out, sem.at[0])]
    for k in range(2):
        whole = pl.ds(rounds * k, rounds - 1)
        copies.append(pltpu.make_async_copy(modes.at[whole], modes_out.at[whole], sem.at[1 + k]))
    for copy in copies:
        copy.start()
    result = along_lat(gathered, lat_tab, rounds - 1, bits - 1)
    for k in range(2):
        row = rounds * k + rounds - 1
        last[k] = modes[row]
        for h in range(2):
            start = h * part_own + (bits - 1) * bit
            last[k, start:start + bit] = result[k * bit:(k + 1) * bit, h * own_y:(h + 1) * own_y]
        copies.append(pltpu.make_async_copy(last.at[k], modes_out.at[row], sem.at[3 + k]))
        copies[-1].start()
    for copy in copies:
        copy.wait()


def on_device(lon_count, lat_count, tables, state, depth, source_mask, gauge_lat, gauge_lon, misfit):
    rows, cols = depth.shape
    own_x, own_y = KX // lon_count, KY // lat_count
    high = rows + 2 * HALO
    bits = bits_of(lon_count)
    vmem = pl.BlockSpec(memory_space=pltpu.VMEM)
    hbm = pl.BlockSpec(memory_space=pltpu.HBM)
    dma = pltpu.SemaphoreType.DMA
    dealt = (3, (rows + 2 * REACH) // 8, 8, 128)
    shapes = (
        jax.ShapeDtypeStruct((3, ADJ, rows, cols), FLOAT),
        jax.ShapeDtypeStruct((ADJ, own_x, own_y), FLOAT),
    )
    held = (
        jax.ShapeDtypeStruct((2, 2 * lat_count * rows, 2 * own_y), HALF),
        jax.ShapeDtypeStruct((ROUNDS, bits, lat_count, own_x // bits, 2 * rows), FLOAT),
    )
    results = pl.pallas_call(
        functools.partial(kernel, lon_count, lat_count),
        out_shape=shapes + held,
        in_specs=[hbm] * 8,
        out_specs=(vmem,) * 4,
        scratch_shapes=[
            pltpu.SMEM(source_mask.shape, jnp.int32),
            pltpu.SMEM((ADJ,), jnp.int32),
            pltpu.SMEM((ADJ,), jnp.int32),
            pltpu.SMEM((ADJ, STEPS), FLOAT),
            pltpu.VMEM((2, 3, 3, high, 128), FLOAT),
            pltpu.VMEM((3, high, 128), FLOAT),
            pltpu.VMEM((ADJ, 3, rows, cols), FLOAT),
            pltpu.VMEM((2, rows, cols), FLOAT),
            pltpu.VMEM((2, 2, rows // 2, 128), FLOAT),
            pltpu.VMEM((2, 2, HALO, 128), FLOAT),
            pltpu.VMEM((2, 2, rows // 2, 128), FLOAT),
            pltpu.VMEM((2, 2, HALO, 128), FLOAT),
            pltpu.VMEM(dealt, FLOAT),
            pltpu.VMEM(dealt, FLOAT),
            pltpu.VMEM((2, *dealt), FLOAT),
            pltpu.VMEM(dealt, FLOAT),
            pltpu.VMEM(dealt, FLOAT),
            pltpu.VMEM(dealt, FLOAT),
            pltpu.VMEM(dealt, FLOAT),
            pltpu.VMEM((2, *dealt), FLOAT),
            pltpu.VMEM((2, KX // 2, 4 * cols), HALF),
            pltpu.VMEM((ROUNDS, KX // 2, 2 * rows), FLOAT),
            pltpu.VMEM((ROUNDS, bits, lon_count, own_x // 2 // bits, 2 * rows), FLOAT),
            pltpu.VMEM((3, HALO, 128), FLOAT),
            pltpu.VMEM((rows // 2, 128), FLOAT),
            pltpu.VMEM((sent_lines(rows, own_x, lon_count, lat_count), 128), FLOAT),
            dma((13 + 2 * ROUNDS * bits,)),
        ],
        compiler_params=pltpu.CompilerParams(
            collective_id=0, has_side_effects=True, vmem_limit_bytes=32 * 1024 * 1024
        ),
    )(*[pltpu.with_memory_space_constraint(x, pltpu.HBM) for x in (state, depth, source_mask, gauge_lat, gauge_lon, misfit.T, *tables)])
    return pl.pallas_call(
        place,
        out_shape=shapes,
        in_specs=[vmem] * 4,
        out_specs=(hbm, hbm),
        scratch_shapes=[pltpu.VMEM((2, own_x, own_y), FLOAT), dma((5,))],
    )(*[pltpu.with_memory_space_constraint(x, pltpu.VMEM) for x in results])


def solution(mesh):
    lon_count, lat_count = mesh.shape["lon"], mesh.shape["lat"]
    placed = (P(None, None, "lat", "lon"), P("lat", "lon"), P("lat", "lon"), P(), P(), P())

    def whole(state, depth, source_mask, gauge_lat, gauge_lon, misfit):
        total_rows, total_cols = depth.shape
        scale = 2.0 / math.sqrt(total_rows * total_cols)
        tables = (lon_table(total_cols, lon_count), lat_table(total_rows, lat_count, scale))

        def local(*args):
            constants = tuple(jnp.asarray(table) for table in tables)
            return on_device(lon_count, lat_count, constants, *args)

        return jax.shard_map(
            local,
            mesh=mesh,
            in_specs=placed,
            out_specs=(P(None, None, "lat", "lon"), P(None, "lon", "lat")),
            check_vma=False,
        )(state, depth, source_mask, gauge_lat, gauge_lon, misfit)

    return whole
```

```python
import functools
import math

import jax
import jax.numpy as jnp
import ml_dtypes
import numpy as np
from jax import lax
from jax.experimental import pallas as pl
from jax.experimental.pallas import tpu as pltpu
from jax.sharding import PartitionSpec as P

STEPS = 6
KX = 512
KY = 512
ADJ = 4
ROUNDS = ADJ // 2
HALO = 16
REACH = 2 * STEPS
SLOTS = 128 // HALO

MESH = pl.DeviceIdType.MESH
FLOAT = jnp.float32
HALF = jnp.bfloat16


def basis(total, modes):
    cells = np.arange(total, dtype=np.int64)
    order = np.arange(modes, dtype=np.int64)
    half = modes // 2
    wave = np.where(order < half, order, order - half + 1)
    phase = (cells[:, None] * wave[None, :] % total).astype(np.float64) * (2.0 * math.pi / total)
    return np.where(order[None, :] < half, np.cos(phase), np.sin(phase))


def halves(table):
    high = table.astype(ml_dtypes.bfloat16)
    low = (table - high.astype(np.float64)).astype(ml_dtypes.bfloat16)
    return high, low


def bits_of(lon_count):
    return 2 if KX // lon_count % 32 == 0 else 1


def lon_table(total, count):
    chips, bits = count // 2, bits_of(count)
    part = KX // count // 2 // bits
    table = basis(total, KX).T.reshape(count, 2, bits, part, chips, total // chips).transpose(4, 2, 0, 3, 1, 5)
    return np.stack(halves(table.reshape(chips, KX // 2, 2 * total // chips)), axis=1)


def lat_table(total, count, scale):
    own, rows = KY // count, total // count
    table = (scale * basis(total, KY)).reshape(count, rows, count, own).transpose(2, 0, 1, 3)
    both = np.zeros((count, count, 2, rows, 2, own))
    both[:, :, 0, :, 0, :] = table
    both[:, :, 1, :, 1, :] = table
    return np.stack(halves(both.reshape(count, 2 * total, 2 * own)), axis=1)


def split(x):
    high = x.astype(HALF)
    return high, (x - high.astype(FLOAT)).astype(HALF)


def along_lat(gathered, lat_tab, a, n):
    lines = gathered.shape[3]
    high_g, low_g = split(jnp.concatenate([gathered[a, n, z] for z in range(gathered.shape[2])], axis=1))
    result = jnp.dot(jnp.concatenate([high_g, low_g], axis=0), lat_tab[0], preferred_element_type=FLOAT)
    return result[:lines] + result[lines:] + jnp.dot(high_g, lat_tab[1], preferred_element_type=FLOAT)


def sent_lines(rows, own, lon_count, lat_count):
    return 14 * rows + ROUNDS * (own // 2 * (lon_count - 1) + own * (lat_count - 1))


def kernel(
    lon_count, lat_count,
    state_hbm, depth_hbm, source_hbm, gauge_lat_hbm, gauge_lon_hbm, misfit_hbm, lon_hbm, lat_hbm,
    fields, modes, lat_tab, gathered,
    source, gauge_lat, gauge_lon, misfit,
    ext, dep, stage, masks, pack, corner, got, met,
    height, flow, total, coef_e, coef_w, coef_n, inside, gauges,
    lon_tab, part, pieces,
    zero, zero_strip, blank, sems,
):
    rows, cols = depth_hbm.shape
    high = rows + 2 * HALO
    depth_of = (rows + 2 * REACH) // 8
    base = HALO - REACH
    mine = slice(HALO, HALO + rows)
    own = modes.shape[1]
    part_own = own // 2
    bits = pieces.shape[1]
    bit = part_own // bits
    fold = rows // 2
    own_y = modes.shape[2]
    lon = lax.axis_index("lon")
    lat = lax.axis_index("lat")
    chips = lon_count // 2
    chip, core = lon // 2, lax.rem(lon, 2)
    mate = lon + 1 - 2 * core
    has_e, has_w = chip < chips - 1, chip > 0
    has_n, has_s = lat < lat_count - 1, lat > 0
    side = 2 * core - 1
    has_side = jnp.logical_or(jnp.logical_and(core == 0, has_w), jnp.logical_and(core == 1, has_e))
    lower, upper = slice(0, REACH), slice(rows - REACH, rows)
    north, south = slice(HALO + rows, HALO + rows + REACH), slice(base, HALO)

    arrived_a, arrived_b, flanked, returned, sent, staged, lon_held, lat_held, first = range(9)
    reduced = first + 4
    spread = reduced + ROUNDS * bits

    def settle(index, lines):
        pltpu.make_async_copy(blank.at[0:lines], blank.at[0:lines], sems.at[index]).wait()

    barrier = pltpu.get_barrier_semaphore()

    def greet(there, device):
        if there is True:
            pl.semaphore_signal(barrier, 1, device_id=device, device_id_type=MESH)
        else:
            @pl.when(there)
            def _():
                pl.semaphore_signal(barrier, 1, device_id=device, device_id_type=MESH)

    both = jnp.logical_and
    greet(has_n, (lon, lat + 1))
    greet(has_s, (lon, lat - 1))
    greet(has_n, (mate, lat + 1))
    greet(has_s, (mate, lat - 1))
    for d in range(1, lon_count):
        greet(True, (lax.rem(lon + d, lon_count), lat))
    greet(both(has_e, has_n), (2 * chip + 2, lat + 1))
    greet(both(has_e, has_s), (2 * chip + 2, lat - 1))
    greet(both(has_w, has_n), (2 * chip - 1, lat + 1))
    greet(both(has_w, has_s), (2 * chip - 1, lat - 1))
    for d in range(1, lat_count):
        target = lax.rem(lat + d, lat_count)
        near = jnp.logical_or(target == lat + 1, target == lat - 1)
        greet(jnp.logical_not(near), (lon, target))

    pairs = [
        (source_hbm, source), (gauge_lat_hbm, gauge_lat), (gauge_lon_hbm, gauge_lon), (misfit_hbm, misfit),
        (depth_hbm, dep.at[core, mine]),
        (state_hbm.at[:, 2 * core], ext.at[0, :, core, mine]), (state_hbm.at[:, 2 * core + 1], ext.at[1, :, core, mine]),
        (lon_hbm.at[chip], lon_tab), (lat_hbm.at[lat], lat_tab),
        *[(state_hbm.at[:, i], stage.at[i]) for i in range(ADJ)],
    ]
    places = [first, first + 1, first + 2, first + 3, staged, arrived_a, arrived_b, lon_held, lat_held] + [staged] * ADJ
    loads = [pltpu.make_async_copy(a, b, sems.at[i]) for i, (a, b) in zip(places, pairs)]
    for i in (4, 9, 11, 10, 12, 0, 1, 2, 3, 5, 6):
        loads[i].start()

    def remote(source_ref, target, send, recv, device):
        return pltpu.make_async_remote_copy(
            src_ref=source_ref, dst_ref=target, send_sem=sems.at[send], recv_sem=sems.at[recv],
            device_id=device, device_id_type=MESH,
        )

    def ns_copy(way, k, item):
        taken, put, step = ((upper, south, 1), (lower, north, -1))[way]
        if item == 0:
            source_ref, target = dep.at[core, slice(taken.start + HALO, taken.stop + HALO)], dep.at[core, put]
        else:
            source_ref, target = stage.at[2 * k + item - 1, :, taken], ext.at[item - 1, :, core, put]
        return remote(source_ref, target, sent, (flanked, arrived_a, arrived_b)[item], (2 * chip + k, lat + step))

    def ns_blank(way, k, item):
        put = (south, north)[way]
        if item == 0:
            return pltpu.make_async_copy(zero.at[0, 0:REACH], dep.at[k, put], sems.at[flanked])
        return pltpu.make_async_copy(zero.at[:, 0:REACH], ext.at[item - 1, :, k, put], sems.at[(arrived_a, arrived_b)[item - 1]])

    ns_goes, ns_comes = (has_n, has_s), (has_s, has_n)

    def side_copy(k, piece):
        step = (0, 0, 1, -1)[piece]
        source_ref = pack.at[piece, k] if piece < 2 else corner.at[piece - 2, k]
        target = got.at[piece, core] if piece < 2 else met.at[piece - 2, core]
        return remote(
            source_ref, target, sent,
            arrived_b if piece == 1 else flanked, (2 * (chip + side) + k, lat + step),
        )

    def side_blank(way, piece):
        source_ref = zero_strip if piece < 2 else zero.at[0]
        target = got.at[piece, way] if piece < 2 else met.at[piece - 2, way]
        return pltpu.make_async_copy(source_ref, target, sems.at[arrived_b if piece == 1 else flanked])

    side_goes = (has_side, has_side, both(has_side, has_n), both(has_side, has_s))
    side_comes = [(x, x, both(x, has_s), both(x, has_n)) for x in (has_e, has_w)]

    def mate_copy(item):
        if item == 0:
            source_ref, target = dep.at[core, mine], dep.at[core, mine]
        elif item == 3:
            source_ref, target = masks.at[core], masks.at[core]
        elif item < 3:
            source_ref, target = stage.at[2 * (1 - core) + item - 1], ext.at[item - 1, :, core, mine]
        else:
            source_ref, target = ext.at[item - 4, :, 1 - core, mine], fields.at[:, 2 * core + item - 4]
        arrived = (flanked, arrived_a, arrived_b, flanked, returned, returned)[item]
        return remote(source_ref, target, sent, arrived, (mate, lat))

    def when(there, action):
        @pl.when(there)
        def _():
            action()

    zero[...] = jnp.zeros(zero.shape, FLOAT)
    zero_strip[...] = jnp.zeros(zero_strip.shape, FLOAT)
    for way in range(2):
        for k in range(2):
            for item in range(3):
                when(jnp.logical_not(ns_comes[way]), lambda: ns_blank(way, k, item).start())
        for piece in range(4):
            when(jnp.logical_not(side_comes[way][piece]), lambda: side_blank(way, piece).start())

    count = lon_count - 1 + lat_count - 1 + has_n.astype(jnp.int32) + has_s.astype(jnp.int32)
    count = count + 2 * side_goes[2].astype(jnp.int32) + 2 * side_goes[3].astype(jnp.int32)

    lane = lax.broadcasted_iota(jnp.int32, (fold, 128), 1)

    def slot_of(item, i, upper_half):
        return (i + SLOTS // 2 * (item + upper_half)) % SLOTS

    strips = {}
    settle(staged, (1 + 3 * ADJ) * rows)
    for item in range(2):
        for k in range(2):
            arrays = [stage[2 * k + item, f] for f in range(3)]
            if item == 0:
                arrays.append(dep[core, mine])
            strip = jnp.zeros((fold, 128), FLOAT)
            for i, array in enumerate(arrays):
                for upper_half in range(2):
                    at = slot_of(item, i, upper_half) * HALO
                    moved = pltpu.roll(array[upper_half * fold:(upper_half + 1) * fold], at + HALO * core, 1)
                    strip = jnp.where(jnp.logical_and(lane >= at, lane < at + HALO), moved, strip)
            pack[item, k] = strip
            strips[item, k] = strip
    for k in range(2):
        begin_lane = lane[:HALO] < 64
        first, second = strips[0, k], strips[1, k]
        corner[0, k] = jnp.where(begin_lane, second[fold - HALO:], first[fold - HALO:])
        corner[1, k] = jnp.where(begin_lane, first[:HALO], second[:HALO])
    pl.semaphore_wait(barrier, count)
    for k in range(2):
        for piece in (2, 3):
            when(side_goes[piece], lambda: side_copy(k, piece).start())
    for item in range(2):
        for k in range(2):
            when(has_side, lambda: side_copy(k, item).start())

    for item in (0, 1):
        for k in range(2):
            for way in range(2):
                when(ns_goes[way], lambda: ns_copy(way, k, item).start())
    mate_copy(0).start()
    mate_copy(1).start()

    for k in range(2):
        for way in range(2):
            when(ns_goes[way], lambda: ns_copy(way, k, 2).start())
    mate_copy(2).start()

    loads[7].start()
    loads[8].start()

    for copy in loads[:4]:
        copy.wait()
    line = lax.broadcasted_iota(jnp.int32, (rows, cols), 0)
    place = lax.broadcasted_iota(jnp.int32, (rows, cols), 1)
    mask = jnp.zeros((rows, cols), FLOAT)
    width = rows // source.shape[0]
    for i in range(source.shape[0]):
        for j in range(source.shape[1]):
            tile = (line >= i * width) & (line < (i + 1) * width) & (place >= j * width) & (place < (j + 1) * width)
            mask = jnp.where(tile, source[i, j].astype(FLOAT), mask)
    masks[core] = mask
    mate_copy(3).start()

    shape = (depth_of, 8, 128)
    near = lax.broadcasted_iota(jnp.int32, shape, 1) * depth_of + lax.broadcasted_iota(jnp.int32, shape, 0)
    row = lat * rows - REACH + near
    across = lax.broadcasted_iota(jnp.int32, shape, 2)
    for j in range(3):
        if j < 2:
            col, real = across + j * 128, row == row
        else:
            col = jnp.where(across < HALO, across + 256, across - 128)
            real = jnp.logical_or(across < HALO, across >= 128 - HALO)
        col = chip * 256 + col
        valid = (row >= 0) & (row < lat_count * rows) & (col >= 0) & (col < chips * 256) & real
        inside[j] = jnp.where(valid, 1.0, 0.0).astype(FLOAT)
        for a in range(2):
            hit = (row == gauge_lat[2 * core + a]) & (col == gauge_lon[2 * core + a]) & real
            gauges[a, j] = jnp.where(hit, 1.0, 0.0).astype(FLOAT)

    half_wide = lax.broadcasted_iota(jnp.int32, (fold + HALO, 128), 1)

    def unpacked(item, i):
        parts = []
        for upper_half in range(2):
            at = slot_of(item, i, upper_half) * HALO
            sides = [jnp.concatenate([got[item, way], met[1 - upper_half, way]], axis=0) for way in range(2)]
            right = pltpu.roll(sides[0], (128 - at) % 128, 1)
            left = pltpu.roll(sides[1], (128 - at - HALO) % 128, 1)
            parts.append(jnp.where(half_wide < HALO, right, jnp.where(half_wide >= 128 - HALO, left, 0.0)))
        lower_half, upper_half = parts
        return jnp.concatenate([upper_half[fold:], lower_half[:fold], upper_half[:fold], lower_half[fold:]], axis=0)

    def dealt(ref):
        return jnp.stack([ref[pl.ds(base + v, 8, stride=depth_of), :] for v in range(depth_of)])

    def north_of(x, n):
        return jnp.concatenate([x[n:], pltpu.roll(x[:n], 7, 1)], axis=0)

    def south_of(x, n):
        return jnp.concatenate([pltpu.roll(x[-n:], 1, 1), x[:-n]], axis=0)

    def east_of(xs, n):
        turned = [pltpu.roll(x, 128 - n, 2) for x in xs]
        return [jnp.where(across < 128 - n, turned[j], turned[(j + 1) % 3]) for j in range(3)]

    def west_of(xs, n):
        turned = [pltpu.roll(x, n, 2) for x in xs]
        return [jnp.where(across >= n, turned[j], turned[j - 1]) for j in range(3)]

    tiles = range(3)

    def arrive(a):
        settle((arrived_a, arrived_b)[a], 2 * 2 * 3 * REACH + 6 * rows + (2 * fold if a else 0))

    def arrive_first():
        settle(flanked, 2 * 2 * REACH + 2 * fold + 2 * 2 * HALO + 2 * rows)

    def deepen():
        dep[2] = unpacked(0, 3)
        deep = [dealt(dep.at[j]) * 0.0625 for j in tiles]
        ahead, behind = east_of(deep, 1), west_of(deep, 1)
        for j in tiles:
            coef_e[j] = ahead[j]
            coef_w[j] = behind[j]
            coef_n[j] = north_of(deep[j], 1)

    def flank(a):
        for f in range(3):
            ext[a, f, 2] = unpacked(a, f)

    def begin(a):
        east = [dealt(ext.at[a, 1, j]) for j in tiles]
        ahead, behind = east_of(east, 1), west_of(east, 1)
        for j in tiles:
            up = dealt(ext.at[a, 2, j])
            height[j] = dealt(ext.at[a, 0, j])
            change = (ahead[j] - behind[j]) + (north_of(up, 1) - south_of(up, 1))
            flow[j] = inside[j] * (0.25 * change)

    def rise(a, t, first):
        push = misfit[2 * core + a, t]
        now = []
        for j in tiles:
            h = height[j] + flow[j] + gauges[a, j] * push
            height[j] = h
            total[a, j] = h if first else total[a, j] + h
            now.append(h)
        return now

    def drive(now):
        ahead, behind = east_of(now, 2), west_of(now, 2)
        for j in tiles:
            lift = coef_n[j] * (north_of(now[j], 2) - now[j])
            along = coef_e[j] * (ahead[j] - now[j]) - coef_w[j] * (now[j] - behind[j])
            flow[j] = flow[j] + inside[j] * (along + (lift - south_of(lift, 2)))

    def advance(a):
        drive(rise(a, 0, True))

        def step(t, carry):
            drive(rise(a, t, False))
            return carry

        lax.fori_loop(1, STEPS - 1, step, 0, unroll=True)
        rise(a, STEPS - 1, False)

    def rs_copy(a, n, target):
        start = pl.multiple_of((n * lon_count + target) * bit, bit)
        return remote(
            part.at[a, pl.ds(start, bit)], pieces.at[a, n, lon],
            sent, reduced + a * bits + n, (target, lat),
        )

    dims = (((1,), (1,)), ((), ()))

    def project(a, beside):
        for j in range(2):
            for v in range(depth_of):
                ext[a, 0, j, pl.ds(base + v, 8, stride=depth_of), :] = height[j, v]
        masked = jnp.concatenate([ext[a, 0, j, mine] * masks[j] for j in range(2)], axis=1)
        high_m, low_m = split(masked)
        blank_m = jnp.zeros_like(high_m)

        def doubled(x):
            return jnp.concatenate(
                [jnp.concatenate([x, blank_m], axis=1), jnp.concatenate([blank_m, x], axis=1)], axis=0
            )

        data = jnp.concatenate([doubled(high_m), doubled(low_m)], axis=0)
        lines = lon_count * bit
        width = 2 * rows
        for n in range(bits):
            table = jnp.concatenate([lon_tab[0, n * lines:(n + 1) * lines], lon_tab[1, n * lines:(n + 1) * lines]], axis=0)
            result = lax.dot_general(table, data, dims, preferred_element_type=FLOAT)
            part[a, n * lines:(n + 1) * lines] = result[:lines, :width] + result[:lines, width:] + result[lines:, :width]
            for action in beside[n::bits]:
                action()
            for target in range(lon_count):
                when(target // 2 != chip, lambda: rs_copy(a, n, target).start())
            rs_copy(a, n, mate).start()
            pieces[a, n, lon] = part[a, pl.ds(pl.multiple_of((n * lon_count + lon) * bit, bit), bit)]

    def finish(a):
        sums = [total[a, j] for j in tiles]
        ahead, behind = east_of(sums, 1), west_of(sums, 1)
        for j in range(2):
            deep = 0.25 * dealt(dep.at[j])
            east = dealt(ext.at[a, 1, j]) + deep * (ahead[j] - behind[j])
            up = dealt(ext.at[a, 2, j]) + deep * (north_of(sums[j], 1) - south_of(sums[j], 1))
            for v in range(depth_of):
                ext[a, 1, j, pl.ds(base + v, 8, stride=depth_of), :] = east[v]
                ext[a, 2, j, pl.ds(base + v, 8, stride=depth_of), :] = up[v]
        mate_copy(4 + a).start()
        for f in range(3):
            fields[f, 2 * core + a] = ext[a, f, core, mine]

    def ga_copy(a, n, z):
        return remote(gathered.at[a, n, lat], gathered.at[a, n, lat], sent, spread + a * bits + n, (lon, z))

    def collect(a, n):
        settle(reduced + a * bits + n, (lon_count - 1) * bit)
        sums = []
        for k in range(2):
            value = pieces[a, n, k]
            for c in range(1, chips):
                value = value + pieces[a, n, 2 * c + k]
            sums.append(value)
        gathered[a, n, lat] = jnp.concatenate(sums, axis=0)
        for z in range(lat_count):
            when(jnp.logical_or(z > lat, jnp.logical_and(z == 0, lat > 0)), lambda: ga_copy(a, n, z).start())

    def conclude(a, n):
        settle(spread + a * bits + n, (lat_count - 1) * 2 * bit)
        result = along_lat(gathered, lat_tab, a, n)
        for k in range(2):
            for h in range(2):
                modes[2 * k + a, h * part_own + n * bit:h * part_own + (n + 1) * bit] = result[
                    k * bit:(k + 1) * bit, h * own_y:(h + 1) * own_y
                ]

    arrive_first()
    deepen()
    flank(0)
    arrive(0)
    begin(0)
    advance(0)
    loads[7].wait()
    arrive(1)
    project(0, (lambda: flank(1), lambda: begin(1)))
    advance(1)
    project(1, ())
    finish(0)
    finish(1)
    loads[8].wait()
    for a in range(ROUNDS):
        for n in range(bits):
            collect(a, n)
    for a in range(ROUNDS):
        for n in range(bits):
            for z in range(1, lat_count - 1):
                when(z < lat, lambda: ga_copy(a, n, z).start())
    settle(returned, 2 * 3 * rows)
    for a in range(ROUNDS):
        for n in range(bits):
            if (a, n) != (ROUNDS - 1, bits - 1):
                conclude(a, n)
    settle(spread + ROUNDS * bits - 1, (lat_count - 1) * 2 * bit)

    for way in range(2):
        when(ns_goes[way], lambda: settle(sent, 2 * 7 * REACH))
        when(side_goes[2 + way], lambda: settle(sent, 2 * HALO))
    when(has_side, lambda: settle(sent, 4 * fold))
    settle(sent, sent_lines(rows, own, lon_count, lat_count))


def place(fields, modes, lat_tab, gathered, fields_out, modes_out, last, sem):
    rounds, bits, _, lines, _ = gathered.shape
    bit, own_y = lines // 2, modes.shape[2]
    part_own = bits * bit
    copies = [pltpu.make_async_copy(fields, fields_out, sem.at[0])]
    for k in range(2):
        whole = pl.ds(rounds * k, rounds - 1)
        copies.append(pltpu.make_async_copy(modes.at[whole], modes_out.at[whole], sem.at[1 + k]))
    for copy in copies:
        copy.start()
    result = along_lat(gathered, lat_tab, rounds - 1, bits - 1)
    for k in range(2):
        row = rounds * k + rounds - 1
        last[k] = modes[row]
        for h in range(2):
            start = h * part_own + (bits - 1) * bit
            last[k, start:start + bit] = result[k * bit:(k + 1) * bit, h * own_y:(h + 1) * own_y]
        copies.append(pltpu.make_async_copy(last.at[k], modes_out.at[row], sem.at[3 + k]))
        copies[-1].start()
    for copy in copies:
        copy.wait()


def on_device(lon_count, lat_count, tables, state, depth, source_mask, gauge_lat, gauge_lon, misfit):
    rows, cols = depth.shape
    own_x, own_y = KX // lon_count, KY // lat_count
    high = rows + 2 * HALO
    bits = bits_of(lon_count)
    vmem = pl.BlockSpec(memory_space=pltpu.VMEM)
    hbm = pl.BlockSpec(memory_space=pltpu.HBM)
    dma = pltpu.SemaphoreType.DMA
    dealt = (3, (rows + 2 * REACH) // 8, 8, 128)
    shapes = (
        jax.ShapeDtypeStruct((3, ADJ, rows, cols), FLOAT),
        jax.ShapeDtypeStruct((ADJ, own_x, own_y), FLOAT),
    )
    held = (
        jax.ShapeDtypeStruct((2, 2 * lat_count * rows, 2 * own_y), HALF),
        jax.ShapeDtypeStruct((ROUNDS, bits, lat_count, own_x // bits, 2 * rows), FLOAT),
    )
    results = pl.pallas_call(
        functools.partial(kernel, lon_count, lat_count),
        out_shape=shapes + held,
        in_specs=[hbm] * 8,
        out_specs=(vmem,) * 4,
        scratch_shapes=[
            pltpu.SMEM(source_mask.shape, jnp.int32),
            pltpu.SMEM((ADJ,), jnp.int32),
            pltpu.SMEM((ADJ,), jnp.int32),
            pltpu.SMEM((ADJ, STEPS), FLOAT),
            pltpu.VMEM((2, 3, 3, high, 128), FLOAT),
            pltpu.VMEM((3, high, 128), FLOAT),
            pltpu.VMEM((ADJ, 3, rows, cols), FLOAT),
            pltpu.VMEM((2, rows, cols), FLOAT),
            pltpu.VMEM((2, 2, rows // 2, 128), FLOAT),
            pltpu.VMEM((2, 2, HALO, 128), FLOAT),
            pltpu.VMEM((2, 2, rows // 2, 128), FLOAT),
            pltpu.VMEM((2, 2, HALO, 128), FLOAT),
            pltpu.VMEM(dealt, FLOAT),
            pltpu.VMEM(dealt, FLOAT),
            pltpu.VMEM((2, *dealt), FLOAT),
            pltpu.VMEM(dealt, FLOAT),
            pltpu.VMEM(dealt, FLOAT),
            pltpu.VMEM(dealt, FLOAT),
            pltpu.VMEM(dealt, FLOAT),
            pltpu.VMEM((2, *dealt), FLOAT),
            pltpu.VMEM((2, KX // 2, 4 * cols), HALF),
            pltpu.VMEM((ROUNDS, KX // 2, 2 * rows), FLOAT),
            pltpu.VMEM((ROUNDS, bits, lon_count, own_x // 2 // bits, 2 * rows), FLOAT),
            pltpu.VMEM((3, HALO, 128), FLOAT),
            pltpu.VMEM((rows // 2, 128), FLOAT),
            pltpu.VMEM((sent_lines(rows, own_x, lon_count, lat_count), 128), FLOAT),
            dma((13 + 2 * ROUNDS * bits,)),
        ],
        compiler_params=pltpu.CompilerParams(
            collective_id=0, has_side_effects=True, vmem_limit_bytes=32 * 1024 * 1024
        ),
    )(*[pltpu.with_memory_space_constraint(x, pltpu.HBM) for x in (state, depth, source_mask, gauge_lat, gauge_lon, misfit.T, *tables)])
    return pl.pallas_call(
        place,
        out_shape=shapes,
        in_specs=[vmem] * 4,
        out_specs=(hbm, hbm),
        scratch_shapes=[pltpu.VMEM((2, own_x, own_y), FLOAT), dma((5,))],
    )(*[pltpu.with_memory_space_constraint(x, pltpu.VMEM) for x in results])


def solution(mesh):
    lon_count, lat_count = mesh.shape["lon"], mesh.shape["lat"]
    placed = (P(None, None, "lat", "lon"), P("lat", "lon"), P("lat", "lon"), P(), P(), P())

    def whole(state, depth, source_mask, gauge_lat, gauge_lon, misfit):
        total_rows, total_cols = depth.shape
        scale = 2.0 / math.sqrt(total_rows * total_cols)
        tables = (lon_table(total_cols, lon_count), lat_table(total_rows, lat_count, scale))

        def local(*args):
            constants = tuple(jnp.asarray(table) for table in tables)
            return on_device(lon_count, lat_count, constants, *args)

        return jax.shard_map(
            local,
            mesh=mesh,
            in_specs=placed,
            out_specs=(P(None, None, "lat", "lon"), P(None, "lon", "lat")),
            check_vma=False,
        )(state, depth, source_mask, gauge_lat, gauge_lon, misfit)

    return whole
```
